32 devices in a mesh: dp: 8 (over z, x), mp: 4 (over y, core).
Axes of the slice: x: 2, y: 2, z: 4, core: 2. Of those that a mesh axis runs over, the one named last changes fastest.
Arguments:
- passage_embeds: bfloat16 [18432, 1024], P('dp'), may hold values from -24 to 24
- passage_lengths: int32 [8, 24], P('dp'), may hold values from 1 to 192, 2304 in all within a row
- slot_question: int32 [8, 24], P('dp'), may hold values from 0 to 7, as said below
- answer_states: bfloat16 [1024, 1024], P('dp'), may hold values from -24 to 24
- w_enc_attn: bfloat16 [4, 1024, 1024], P(None, 'dp', 'mp'), may hold values from -0.1875 to 0.1875
- w_enc_ff: bfloat16 [3, 1024, 2816], P(None, 'dp', 'mp'), may hold values from -0.1875 to 0.1875
- w_cross_kv: bfloat16 [2, 1024, 1024], P(None, 'dp', 'mp'), may hold values from -0.1875 to 0.1875
- w_dec_attn: bfloat16 [6, 1024, 1024], P(None, 'dp', 'mp'), may hold values from -0.1875 to 0.1875
- w_dec_ff: bfloat16 [3, 1024, 2816], P(None, 'dp', 'mp'), may hold values from -0.1875 to 0.1875
Outputs:
- decoded: bfloat16 [1024, 1024], P('dp', 'mp')
The draws below stay inside these ranges and needn't reach their ends.
Inputs may be any that keep to these rules, and one draw needn't show every extreme that they name: `passage_lengths`: each row sums to 2304. `slot_question`: each question is named by exactly 24 slots; a row names one question at most 3 times, and every row names some question that many times.
All inputs are finite; a program needn't handle non-finite values.
Results may differ from the reference program's by a relative error of at most 0.025.
Values may be sent and summed in bfloat16 or wider, within the bound.
No kernel may reach another device: no remote copies, remote signals or barrier semaphores. Data moves between devices by JAX's collectives and lax.ppermute only.
A program may use at most 128 MiB of HBM per device.

```python
import math
import jax
import jax.numpy as jnp
import numpy as np
from jax import lax

D = 1024
HEADS = 16
HEAD_DIM = 64
FF = 2816
PASSAGES = 24
AVG_LEN = 96
DEC_LEN = 128
MOST_LEN = 192
TOK_DEV = 2304
QUESTIONS = 8
TOKENS = 18432
SLOT = 576
N_DP = 8
N_MP = 4


def scaled_normal(key, row_count, column_count):
    base = jax.random.normal(jax.random.fold_in(key, 11), (row_count, column_count), jnp.float32)
    return jnp.clip(base, -24.0, 24.0)


def draw_passage_embeds(key, part):
    return scaled_normal(jax.random.fold_in(key, 31), TOKENS, D).astype(jnp.bfloat16)


def draw_answer_states(key, part):
    return scaled_normal(jax.random.fold_in(key, 37), QUESTIONS * DEC_LEN, D).astype(jnp.bfloat16)


def draw_slot_question(key, part):
    shifts = jax.random.permutation(jax.random.fold_in(key, 21), N_DP)
    row_keys = jax.random.split(jax.random.fold_in(key, 22), N_DP)
    orders = jax.vmap(lambda row_key: jax.random.permutation(row_key, PASSAGES))(row_keys)
    return ((shifts[:, None] + orders) % N_DP).astype(jnp.int32)


def block_levels(own_key, dims, pieces, low, high):
    def one(axis_at, parts):
        steps = jax.random.uniform(jax.random.fold_in(jax.random.fold_in(own_key, 6), axis_at), (parts,), jnp.float32, low / len(pieces), high / len(pieces))
        return jnp.repeat(jnp.exp(steps), dims[axis_at] // parts).reshape((-1,) + (1,) * (len(dims) - axis_at - 1))

    factor_of = one(*pieces[0])
    for cut in pieces[1:]:
        factor_of = factor_of * one(*cut)
    return factor_of


def split_up(number_of, total, limit, slope):
    portions = [(1 << 20) // math.isqrt(standing ** slope) + 1 for standing in range(2, number_of + 1)]
    spare, given = total - limit - (number_of - 1), [1] * (number_of - 1)
    while spare > 0:
        movable = [i for i in range(number_of - 1) if given[i] < limit]
        whole, budget = sum([portions[i] for i in movable]), spare
        for i in movable:
            more = min(limit - given[i], max(1, budget * portions[i] // whole), spare)
            given[i] = given[i] + more
            spare = spare - more
    return np.array([limit] + given)


def uneven_parts(own_key, number_of, total, limit, lean):
    if number_of == 2:
        one = jax.random.randint(own_key, (), max(1, total - limit), min(limit, total - 1) + 1)
        return jnp.stack([one, total - one])
    sizes = jnp.asarray(split_up(number_of, total, limit, lean), jnp.int32)
    couples = (number_of - 1) // 2
    source_of, receiver = sizes[1:1 + 2 * couples:2], sizes[2:2 + 2 * couples:2]
    slack = jnp.minimum(source_of - 1, limit - receiver)
    moved = jax.random.randint(jax.random.fold_in(own_key, 1), (couples,), 0, 1 << 20) % (slack + 1)
    sizes = sizes.at[1:1 + 2 * couples:2].set(source_of - moved).at[2:2 + 2 * couples:2].set(receiver + moved)
    return sizes[jax.random.permutation(jax.random.fold_in(own_key, 2), number_of)]


def normal_values(own_key, shape, spread, bound, pieces=(), kind=jnp.bfloat16):
    result = jax.random.normal(own_key, shape, jnp.float32) * spread
    if len(pieces) > 0:
        result = block_levels(own_key, shape, pieces, -0.22, 0.18) * result
    return jnp.clip(result, min=-bound, max=bound).astype(kind)


def setup_inputs(seed: int = 0) -> dict:
    key_of = jax.random.split(jax.random.key(seed), 10)
    passage_embeds = draw_passage_embeds(jax.random.fold_in(key_of[9], 71), 0)
    passage_lengths = jax.vmap(lambda own: uneven_parts(own, PASSAGES, TOK_DEV, MOST_LEN, 2))(jax.random.split(key_of[1], QUESTIONS)).reshape((QUESTIONS, PASSAGES)).astype(jnp.int32)
    slot_question = draw_slot_question(jax.random.fold_in(key_of[9], 71), 0)
    answer_states = draw_answer_states(jax.random.fold_in(key_of[9], 71), 0)
    w_enc_attn = normal_values(key_of[4], (4, D, D), D ** -0.5, 0.1875, ((1, 8), (2, 4)))
    w_enc_ff = normal_values(key_of[5], (3, D, FF), D ** -0.5, 0.1875, ((1, 8), (2, 4)))
    w_cross_kv = normal_values(key_of[6], (2, D, D), D ** -0.5, 0.1875, ((1, 8), (2, 4)))
    w_dec_attn = normal_values(key_of[7], (6, D, D), D ** -0.5, 0.1875, ((1, 8), (2, 4)))
    w_dec_ff = normal_values(key_of[8], (3, D, FF), D ** -0.5, 0.1875, ((1, 8), (2, 4)))
    return dict(passage_embeds=passage_embeds, passage_lengths=passage_lengths, slot_question=slot_question, answer_states=answer_states, w_enc_attn=w_enc_attn, w_enc_ff=w_enc_ff, w_cross_kv=w_cross_kv, w_dec_attn=w_dec_attn, w_dec_ff=w_dec_ff)


EPSILON = 1e-06

def to_bf16(values):
    return lax.optimization_barrier(values.astype(jnp.bfloat16))

def rms_normed(values):
    values = values.astype(jnp.float32)
    factor = lax.rsqrt(lax.optimization_barrier(jnp.mean(values * values, axis=-1, keepdims=True)) + EPSILON)
    return to_bf16(values * factor)

def score_factor():
    return 3.0 / math.sqrt(HEAD_DIM)

def project(normed, weight):
    return to_bf16(jnp.dot(normed, weight, preferred_element_type=jnp.float32))

def grouped_sum(left, right):
    row_count, inner = left.shape
    width = inner // N_MP
    summed = jnp.zeros((row_count, right.shape[0]), jnp.float32)
    for group_index in range(N_MP):
        begin_col = group_index * width
        piece = jnp.dot(left[:, begin_col:begin_col + width], right[:, begin_col:begin_col + width].T, preferred_element_type=jnp.float32)
        summed = summed + to_bf16(piece).astype(jnp.float32)
    return summed

def attend(queries, key_rows, value_rows, allowed):
    scores = jnp.einsum('qhc,khc->hqk', queries.astype(jnp.float32), key_rows.astype(jnp.float32)) * score_factor()
    weights = jnp.where(allowed[None], jnp.exp(scores), 0.0)
    totals = lax.optimization_barrier(jnp.sum(weights, axis=2))
    mixture = jnp.einsum('hqk,khc->qhc', to_bf16(weights).astype(jnp.float32), value_rows.astype(jnp.float32))
    return to_bf16(mixture / jnp.transpose(totals)[:, :, None])

def passage_attention(queries, key_rows, value_rows, segment):
    row_count = queries.shape[0]
    margin = 4 * AVG_LEN
    block_rows = math.gcd(row_count, 768)
    window = block_rows + 2 * margin
    queries = queries.reshape(row_count, HEADS, HEAD_DIM)
    key_rows = jnp.pad(key_rows, ((margin, margin), (0, 0))).reshape(row_count + 2 * margin, HEADS, HEAD_DIM)
    value_rows = jnp.pad(value_rows, ((margin, margin), (0, 0))).reshape(row_count + 2 * margin, HEADS, HEAD_DIM)
    padded_segment = jnp.pad(segment, (margin, margin), constant_values=-1)

    def one_block(block_index):
        begin_row = block_index * block_rows
        query_block = lax.dynamic_slice_in_dim(queries, begin_row, block_rows, 0)
        key_block = lax.dynamic_slice_in_dim(key_rows, begin_row, window, 0)
        value_block = lax.dynamic_slice_in_dim(value_rows, begin_row, window, 0)
        own_segment = lax.dynamic_slice_in_dim(segment, begin_row, block_rows, 0)
        other_segment = lax.dynamic_slice_in_dim(padded_segment, begin_row, window, 0)
        allowed = own_segment[:, None] == other_segment[None, :]
        return attend(query_block, key_block, value_block, allowed)
    blocks = lax.map(one_block, jnp.arange(row_count // block_rows, dtype=jnp.int32))
    return blocks.reshape(row_count, HEADS * HEAD_DIM)

def slot_targets(lengths, questions, row_count, capacity):
    passage_ends = jnp.cumsum(lengths).astype(jnp.int32)
    passage_starts = (passage_ends - lengths).astype(jnp.int32)
    positions = jnp.arange(row_count, dtype=jnp.int32)
    passage_of = lax.optimization_barrier(jnp.sum((positions[:, None] >= passage_ends[None, :]).astype(jnp.int32), axis=1)).astype(jnp.int32)
    slots_index = jnp.arange(lengths.shape[0], dtype=jnp.int32)
    membership = (passage_of[:, None] == slots_index[None, :]).astype(jnp.int32)
    earlier = (questions[:, None] == questions[None, :]) & (slots_index[None, :] < slots_index[:, None])
    offset = lax.optimization_barrier(jnp.sum(jnp.where(earlier, lengths[None, :], 0), axis=1)).astype(jnp.int32)
    shifted = (questions * capacity + offset - passage_starts).astype(jnp.int32)
    target = (lax.optimization_barrier(jnp.sum(membership * shifted[None, :], axis=1)) + positions).astype(jnp.int32)
    return (passage_of, target)

def question_counts(lengths, questions, owners):
    chosen = questions[:, None] == jnp.arange(owners, dtype=jnp.int32)[None, :]
    return lax.optimization_barrier(jnp.sum(jnp.where(chosen, lengths[:, None], 0), axis=0)).astype(jnp.int32)

def pick_rows(source_rows, picks):
    return source_rows[picks]

def reference(passage_embeds, passage_lengths, slot_question, answer_states, w_enc_attn, w_enc_ff, w_cross_kv, w_dec_attn, w_dec_ff):

    def encode_row(packed):
        embeds, lengths, questions = packed
        passage_of, target = slot_targets(lengths, questions, TOK_DEV, SLOT)
        normed = rms_normed(embeds)
        mixture = passage_attention(project(normed, w_enc_attn[0]), project(normed, w_enc_attn[1]), project(normed, w_enc_attn[2]), passage_of)
        first_rows = to_bf16(embeds.astype(jnp.float32) + grouped_sum(mixture, w_enc_attn[3]))
        normed = rms_normed(first_rows)
        gate_rows = jnp.dot(normed, w_enc_ff[0], preferred_element_type=jnp.float32)
        up_rows = jnp.dot(normed, w_enc_ff[1], preferred_element_type=jnp.float32)
        hidden = to_bf16(jax.nn.gelu(gate_rows, approximate=True) * up_rows)
        second_rows = to_bf16(first_rows.astype(jnp.float32) + grouped_sum(hidden, w_enc_ff[2]))
        final_rows = rms_normed(second_rows)
        inverse = jnp.zeros((N_DP * SLOT,), jnp.int32).at[target].set(jnp.arange(TOK_DEV, dtype=jnp.int32))
        counts = question_counts(lengths, questions, QUESTIONS)
        return (project(final_rows, w_cross_kv[0]), project(final_rows, w_cross_kv[1]), inverse, counts)
    packed = (passage_embeds.reshape(N_DP, TOK_DEV, D), passage_lengths, slot_question)
    enc_keys, enc_values, inverse, counts = lax.map(encode_row, packed)

    def heads_view(values):
        return values.reshape(QUESTIONS, DEC_LEN, HEADS, HEAD_DIM)
    answer_normed = rms_normed(answer_states)
    causal = jnp.arange(DEC_LEN)[None, :] <= jnp.arange(DEC_LEN)[:, None]
    self_mix = jax.vmap(attend, in_axes=(0, 0, 0, None))(heads_view(project(answer_normed, w_dec_attn[0])), heads_view(project(answer_normed, w_dec_attn[1])), heads_view(project(answer_normed, w_dec_attn[2])), causal).reshape(QUESTIONS * DEC_LEN, D)
    first_rows = to_bf16(answer_states.astype(jnp.float32) + grouped_sum(self_mix, w_dec_attn[3]))
    query_rows = heads_view(project(rms_normed(first_rows), w_dec_attn[4]))

    def cross_one(question):
        columns = lax.dynamic_slice_in_dim(inverse, question * SLOT, SLOT, 1)
        key_rows = jax.vmap(pick_rows)(enc_keys, columns).reshape(N_DP * SLOT, HEADS, HEAD_DIM)
        value_rows = jax.vmap(pick_rows)(enc_values, columns).reshape(N_DP * SLOT, HEADS, HEAD_DIM)
        arrived = lax.dynamic_index_in_dim(counts, question, 1, keepdims=False)
        usable = (jnp.arange(SLOT, dtype=jnp.int32)[None, :] < arrived[:, None]).reshape(N_DP * SLOT)
        queries = lax.dynamic_index_in_dim(query_rows, question, 0, keepdims=False)
        allowed = jnp.broadcast_to(usable[None, :], (DEC_LEN, N_DP * SLOT))
        return attend(queries, key_rows, value_rows, allowed)
    cross_mix = lax.map(cross_one, jnp.arange(QUESTIONS, dtype=jnp.int32)).reshape(QUESTIONS * DEC_LEN, D)
    second_rows = to_bf16(first_rows.astype(jnp.float32) + grouped_sum(cross_mix, w_dec_attn[5]))
    normed = rms_normed(second_rows)
    gate_rows = jnp.dot(normed, w_dec_ff[0], preferred_element_type=jnp.float32)
    up_rows = jnp.dot(normed, w_dec_ff[1], preferred_element_type=jnp.float32)
    hidden = to_bf16(jax.nn.gelu(gate_rows, approximate=True) * up_rows)
    return (second_rows.astype(jnp.float32) + grouped_sum(hidden, w_dec_ff[2])).astype(jnp.bfloat16)
```

```python
import functools
import math

import jax
import jax.numpy as jnp
from jax import lax
from jax.experimental import pallas as pl
from jax.experimental.pallas import tpu as pltpu
from jax.sharding import PartitionSpec as P

HEAD_DIM = 64
MOST_LEN = 192
EPSILON = 1e-06
LANES = 128
HALO = 256
F32 = jnp.float32
BF16 = jnp.bfloat16
EXP2_FACTOR = 3.0 / math.sqrt(HEAD_DIM) * math.log2(math.e)


def rms_normed(values):
    values = values.astype(F32)
    factor = lax.rsqrt(jnp.mean(values * values, axis=-1, keepdims=True) + EPSILON)
    return (values * factor).astype(BF16)


def dot(left, right):
    return jnp.dot(left, right, preferred_element_type=F32)


def dot_t(left, right):
    return lax.dot_general(left, right, (((1,), (1,)), ((), ())), preferred_element_type=F32)


def swap_x(value):
    count = lax.axis_size("dp")
    return lax.ppermute(value, "dp", [(i, i ^ 1) for i in range(count)])


def swap_core(value):
    count = lax.axis_size("mp")
    return lax.ppermute(value, "mp", [(i, i ^ 1) for i in range(count)])


def z_groups():
    count = lax.axis_size("dp")
    return [[i + x for i in range(0, count, 2)] for x in range(2)]


def y_groups():
    count = lax.axis_size("mp")
    return [[i + c for i in range(0, count, 2)] for c in range(2)]


def gather_z(value, axis):
    return lax.all_gather(value, "dp", axis_index_groups=z_groups(), axis=axis, tiled=True)


def gather_y(value):
    size_y = lax.axis_size("mp") // 2
    if size_y == 1:
        return [value]
    if size_y == 2:
        return [value, lax.ppermute(value, "mp", [(i, i ^ 2) for i in range(4)])]
    pieces = lax.all_gather(value, "mp", axis_index_groups=y_groups(), axis=0)
    return [pieces[i] for i in range(size_y)]


def gather_y_rows(value):
    size_y = lax.axis_size("mp") // 2
    if size_y == 2:
        other = lax.ppermute(value, "mp", [(i, i ^ 2) for i in range(4)])
        first = lax.axis_index("mp") < 2
        return jnp.concatenate(
            [jnp.where(first, value, other), jnp.where(first, other, value)], axis=0
        )
    return lax.all_gather(value, "mp", axis_index_groups=y_groups(), axis=0, tiled=True)


def scatter_y_sum(value):
    size_y = lax.axis_size("mp") // 2
    y = lax.axis_index("mp") // 2
    if size_y == 2:
        other = lax.ppermute(
            lax.dynamic_index_in_dim(value, 1 - y, 0, keepdims=False),
            "mp",
            [(i, i ^ 2) for i in range(4)],
        )
        own = lax.dynamic_index_in_dim(value, y, 0, keepdims=False)
        return own.astype(F32) + other.astype(F32)
    summed = lax.psum_scatter(
        value, "mp", scatter_dimension=0, axis_index_groups=y_groups(), tiled=True
    )
    return summed[0].astype(F32)


def pick(value, index, count, axis):
    width = value.shape[axis] // count
    return lax.dynamic_slice_in_dim(value, index * width, width, axis)


def in_order(first, own, other, axis):
    return jnp.concatenate(
        [jnp.where(first, own, other), jnp.where(first, other, own)], axis=axis
    )


def fetch_enc(shard, x_first):
    own = gather_z(shard, 1)
    if x_first:
        return gather_y(jnp.concatenate([own, swap_x(own)], axis=1))
    return [jnp.concatenate([w, swap_x(w)], axis=1) for w in gather_y(own)]


def fetch_dec(shard, x):
    both = jnp.stack([pick(shard, x, 2, 2), swap_x(pick(shard, 1 - x, 2, 2))], axis=1)
    full = gather_z(both, 2)
    return full.reshape(full.shape[0], -1, full.shape[3])


def own_first(values, x, width):
    size_z = values.shape[1] // (2 * width)
    blocks = [
        lax.dynamic_slice_in_dim(values, (2 * z + index) * width, width, 1)
        for index in (x, 1 - x)
        for z in range(size_z)
    ]
    return jnp.concatenate(blocks, axis=1)


def plain_order(values, x, width):
    rows, features = values.shape
    half = features // 2
    own = values[:, :half].reshape(rows, half // width, 1, width)
    other = values[:, half:].reshape(rows, half // width, 1, width)
    return in_order(x == 0, own, other, 2).reshape(rows, features)


def enc_attention_kernel(low_ref, high_ref, seg_q_ref, seg_k_ref, q_ref, k_ref, v_ref, o_ref, acc):
    block = pl.program_id(0)
    rows, width = q_ref.shape
    key_rows = seg_k_ref.shape[2]
    acc[...] = jnp.zeros_like(acc)
    lane = lax.broadcasted_iota(jnp.int32, (1, LANES), 1)
    low_half = lane < HEAD_DIM
    queries = []
    for p in range(width // LANES):
        pair = q_ref[:, p * LANES : (p + 1) * LANES]
        zero = jnp.zeros_like(pair)
        queries.append(
            jnp.concatenate(
                [jnp.where(low_half, pair, zero), jnp.where(low_half, zero, pair)], axis=0
            )
        )
    seg_q = seg_q_ref[:, :key_rows]
    seg_q = jnp.concatenate([seg_q, seg_q], axis=0)

    def step(j, carry):
        begin = pl.multiple_of(j * key_rows, key_rows)
        allowed = seg_q == seg_k_ref[j]
        for p in range(width // LANES):
            keys = k_ref[pl.ds(begin, key_rows), p * LANES : (p + 1) * LANES]
            vals = v_ref[pl.ds(begin, key_rows), p * LANES : (p + 1) * LANES]
            scores = dot_t(queries[p], keys) * EXP2_FACTOR
            weights = jnp.where(allowed, jnp.exp2(scores), 0.0).astype(BF16)
            one = jnp.ones_like(vals)
            acc[2 * p] += dot(weights[:rows], jnp.where(low_half, vals, one))
            acc[2 * p + 1] += dot(weights[rows:], jnp.where(low_half, one, vals))
        return carry

    lax.fori_loop(low_ref[block], high_ref[block], step, 0)
    for p in range(width // LANES):
        first, second = acc[2 * p], acc[2 * p + 1]
        o_ref[:, p * LANES : (p + 1) * LANES] = jnp.where(
            low_half,
            first / pltpu.roll(first, HEAD_DIM, 1),
            second / pltpu.roll(second, HEAD_DIM, 1),
        ).astype(BF16)


def enc_attention(low, high, seg_q, seg_k, q, k, v):
    rows, width = q.shape
    blocks = low.shape[0]
    query_rows = rows // blocks
    full = lambda i, *_: (0, 0)
    return pl.pallas_call(
        enc_attention_kernel,
        out_shape=jax.ShapeDtypeStruct((rows, width), BF16),
        grid_spec=pltpu.PrefetchScalarGridSpec(
            num_scalar_prefetch=2,
            grid=(blocks,),
            in_specs=[
                pl.BlockSpec((query_rows, LANES), lambda i, *_: (i, 0)),
                pl.BlockSpec(seg_k.shape, lambda i, *_: (0, 0, 0)),
                pl.BlockSpec((query_rows, width), lambda i, *_: (i, 0)),
                pl.BlockSpec(k.shape, full),
                pl.BlockSpec(v.shape, full),
            ],
            out_specs=pl.BlockSpec((query_rows, width), lambda i, *_: (i, 0)),
            scratch_shapes=[pltpu.VMEM((width // HEAD_DIM, query_rows, LANES), F32)],
        ),
        cost_estimate=pl.CostEstimate(
            flops=rows * 384 * width * 8, bytes_accessed=rows * width * 8, transcendentals=0
        ),
        name="enc_attention",
    )(low, high, seg_q, seg_k, q, k, v)


def cross_kernel(begin_ref, end_ref, question_ref, q_ref, k_ref, v_ref, num_ref, tot_ref, acc, *, key_rows):
    questions, length, width = q_ref.shape
    acc[...] = jnp.zeros_like(acc)
    lane = lax.broadcasted_iota(jnp.int32, (1, LANES), 1)
    low_half = lane < HEAD_DIM

    def passage(s, carry):
        begin, end, question = begin_ref[s], end_ref[s], question_ref[s]

        def step(j, inner):
            offset = pl.multiple_of(j * key_rows, key_rows)
            position = offset + lax.broadcasted_iota(jnp.int32, (1, key_rows), 1)
            allowed = (position >= begin) & (position < end)
            for p in range(width // LANES):
                columns = slice(p * LANES, (p + 1) * LANES)
                pair = q_ref[question, :, columns]
                zero = jnp.zeros_like(pair)
                queries = jnp.concatenate(
                    [jnp.where(low_half, pair, zero), jnp.where(low_half, zero, pair)], axis=0
                )
                keys = k_ref[pl.ds(offset, key_rows), columns]
                vals = v_ref[pl.ds(offset, key_rows), columns]
                scores = dot_t(queries, keys) * EXP2_FACTOR
                weights = jnp.where(allowed, jnp.exp2(scores), 0.0).astype(BF16)
                one = jnp.ones_like(vals)
                acc[question, 2 * p] += dot(weights[:length], jnp.where(low_half, vals, one))
                acc[question, 2 * p + 1] += dot(weights[length:], jnp.where(low_half, one, vals))
            return inner

        blocks = jnp.where(end > begin, (end + key_rows - 1) // key_rows, 0)
        lax.fori_loop(begin // key_rows, blocks, step, 0)
        return carry

    lax.fori_loop(0, begin_ref.shape[0], passage, 0)
    eye = lax.broadcasted_iota(jnp.int32, (length, LANES), 0) == lax.broadcasted_iota(
        jnp.int32, (length, LANES), 1
    )

    def finish(question, carry):
        for p in range(width // LANES):
            first, second = acc[question, 2 * p], acc[question, 2 * p + 1]
            num_ref[question, :, p * LANES : (p + 1) * LANES] = jnp.where(
                low_half, first, second
            ).astype(BF16)
            first = jnp.where(low_half, pltpu.roll(first, HEAD_DIM, 1), first)
            second = jnp.where(low_half, second, pltpu.roll(second, HEAD_DIM, 1))
            for h, total in ((2 * p, first), (2 * p + 1, second)):
                tot_ref[question, h : h + 1, :] = jnp.sum(
                    jnp.where(eye, total, 0.0), axis=0, keepdims=True
                )
        return carry

    lax.fori_loop(0, questions, finish, 0)


def cross_attention(begin, end, question, q, k, v):
    questions, length, width = q.shape
    key_rows = math.gcd(k.shape[0], LANES)
    vmem = pl.BlockSpec(memory_space=pltpu.VMEM)
    smem = pl.BlockSpec(memory_space=pltpu.SMEM)
    return pl.pallas_call(
        functools.partial(cross_kernel, key_rows=key_rows),
        out_shape=(
            jax.ShapeDtypeStruct((questions, length, width), BF16),
            jax.ShapeDtypeStruct((questions, width // HEAD_DIM, length), F32),
        ),
        in_specs=[smem, smem, smem, vmem, vmem, vmem],
        out_specs=(vmem, vmem),
        scratch_shapes=[pltpu.VMEM((questions, width // HEAD_DIM, length, LANES), F32)],
        cost_estimate=pl.CostEstimate(
            flops=k.shape[0] * 256 * width * 8, bytes_accessed=4 * q.size, transcendentals=0
        ),
        name="cross_attention",
    )(begin, end, question, q, k, v)


def self_attention(q, k, v, questions):
    rows, width = q.shape
    heads = width // HEAD_DIM
    length = rows // questions
    shape = (questions, length, heads, HEAD_DIM)
    q, k, v = q.reshape(shape), k.reshape(shape), v.reshape(shape)
    scores = jnp.einsum("oqhc,okhc->ohqk", q, k, preferred_element_type=F32)
    causal = jnp.arange(length)[None, :] <= jnp.arange(length)[:, None]
    weights = jnp.where(causal, jnp.exp(scores * (3.0 / math.sqrt(HEAD_DIM))), 0.0)
    totals = jnp.sum(weights, axis=3)
    mixture = jnp.einsum("ohqk,okhc->oqhc", weights.astype(BF16), v, preferred_element_type=F32)
    return (mixture / jnp.transpose(totals, (0, 2, 1))[..., None]).astype(BF16).reshape(rows, width)


def core_rows_sum(partial, core):
    other = swap_core(pick(partial, 1 - core, 2, 0).astype(BF16))
    return pick(partial, core, 2, 0) + other.astype(F32)


def answer_sum(partial, residual, core, y, size_y):
    half = partial.shape[1] // 2
    mine = core_rows_sum(partial, core)
    mine = mine[:, :half] + swap_x(mine[:, half:].astype(BF16)).astype(F32)
    rows = mine.shape[0] // size_y
    summed = scatter_y_sum(mine.astype(BF16).reshape(size_y, rows, half))
    own_rows = pick(pick(residual, core, 2, 0)[:, :half], y, size_y, 0)
    updated = (own_rows.astype(F32) + summed).astype(BF16)
    updated = gather_y_rows(updated)
    updated = jnp.concatenate([updated, swap_x(updated)], axis=1)
    return in_order(core == 0, updated, swap_core(updated), 0)


def local(
    passage_embeds,
    passage_lengths,
    slot_question,
    answer_states,
    w_enc_attn,
    w_enc_ff,
    w_cross_kv,
    w_dec_attn,
    w_dec_ff,
):
    dp_count, mp_count = lax.axis_size("dp"), lax.axis_size("mp")
    size_z, size_y = dp_count // 2, mp_count // 2
    x = lax.axis_index("dp") % 2
    core = lax.axis_index("mp") % 2
    y = lax.axis_index("mp") // 2
    features = passage_embeds.shape[1]
    shard_width = features // dp_count

    kv_weights = fetch_enc(w_enc_attn[1:3], True)
    qo_weights = fetch_enc(jnp.concatenate([w_enc_attn[0:1], w_enc_attn[3:4]]), False)
    gate_weights = fetch_enc(w_enc_ff[0:1], True)
    up_weights = fetch_enc(w_enc_ff[1:2], False)
    down_weights = fetch_enc(w_enc_ff[2:3], True)
    cross_weights = fetch_enc(w_cross_kv, False)
    dec_attn = fetch_dec(w_dec_attn, x)
    dec_ff = fetch_dec(w_dec_ff, x)

    row_count = passage_embeds.shape[0]
    rows = row_count // size_y
    sides = min(size_y - 1, 2)
    window = min(row_count, rows + sides * HALO)
    row_begin = y * rows
    window_begin = jnp.clip(row_begin - HALO, 0, row_count - window)
    lengths = passage_lengths[0]
    ends = jnp.cumsum(lengths)
    starts = ends - lengths
    positions = window_begin + jnp.arange(window, dtype=jnp.int32)
    segment = jnp.sum((positions[:, None] >= ends[None, :]).astype(jnp.int32), axis=1)
    query_block = math.gcd(rows, LANES)
    key_block = math.gcd(window, LANES)
    block_first = row_begin + jnp.arange(rows // query_block, dtype=jnp.int32) * query_block
    block_last = block_first + query_block - 1
    inside_first = jnp.max(
        jnp.where(starts[None, :] <= block_first[:, None], starts[None, :], 0), axis=1
    )
    inside_last = jnp.min(
        jnp.where(ends[None, :] > block_last[:, None], ends[None, :], row_count), axis=1
    )
    low = (inside_first - window_begin) // key_block
    high = (inside_last - window_begin + key_block - 1) // key_block
    seg_k = segment.reshape(window // key_block, 1, key_block)
    seg_q = jnp.broadcast_to(
        lax.dynamic_slice_in_dim(segment, row_begin - window_begin, rows, 0)[:, None],
        (rows, LANES),
    )

    embeds = own_first(
        lax.dynamic_slice_in_dim(passage_embeds, window_begin, window, 0), x, shard_width
    )
    normed = rms_normed(embeds)
    own_begin = row_begin - window_begin
    normed_q = lax.dynamic_slice_in_dim(normed, own_begin, rows, 0)
    partial = 0.0
    for kv, qo in zip(kv_weights, qo_weights):
        mixture = enc_attention(
            low,
            high,
            seg_q,
            seg_k,
            dot(normed_q, qo[0]).astype(BF16),
            dot(normed, kv[0]).astype(BF16),
            dot(normed, kv[1]).astype(BF16),
        )
        partial = partial + dot_t(mixture, qo[1])
    own_embeds = lax.dynamic_slice_in_dim(embeds, own_begin + core * (rows // 2), rows // 2, 0)
    first_rows = (own_embeds.astype(F32) + core_rows_sum(partial, core)).astype(BF16)
    normed = rms_normed(first_rows)
    normed = in_order(core == 0, normed, swap_core(normed), 0)
    partial = 0.0
    for gate, up, down in zip(gate_weights, up_weights, down_weights):
        hidden = (
            jax.nn.gelu(dot(normed, gate[0]), approximate=True) * dot(normed, up[0])
        ).astype(BF16)
        partial = partial + dot_t(hidden, down[0])
    second_rows = (first_rows.astype(F32) + core_rows_sum(partial, core)).astype(BF16)
    normed = rms_normed(second_rows)
    normed = in_order(core == 0, normed, swap_core(normed), 0)

    length = answer_states.shape[0]
    answers = in_order(x == 0, answer_states, swap_x(answer_states), 0)
    answers = own_first(answers, x, shard_width)
    answer_normed = rms_normed(answers)
    self_mix = self_attention(
        dot(answer_normed, dec_attn[0]).astype(BF16),
        dot(answer_normed, dec_attn[1]).astype(BF16),
        dot(answer_normed, dec_attn[2]).astype(BF16),
        2,
    )
    first_answer = answer_sum(dot_t(self_mix, dec_attn[3]), answers, core, y, size_y)
    cross_q = dot(rms_normed(first_answer), dec_attn[4]).astype(BF16)
    cross_q = gather_z(cross_q, 0)
    cross_q = in_order(x == 0, cross_q, swap_x(cross_q), 1)
    cross_q = gather_y(cross_q.reshape(dp_count, length, cross_q.shape[1]))

    begin = jnp.clip(starts - row_begin, 0, rows)
    end = jnp.clip(ends - row_begin, 0, rows)
    questions = slot_question[0]
    packed = []
    for queries, kv in zip(cross_q, cross_weights):
        num, tot = cross_attention(
            begin,
            end,
            questions,
            queries,
            dot(normed, kv[0]).astype(BF16),
            dot(normed, kv[1]).astype(BF16),
        )
        width = num.shape[2] // 2
        heads = tot.shape[1] // 2
        num = num.reshape(size_z, 2 * length, 2, width).transpose(0, 2, 1, 3)
        tot = tot.reshape(size_z, 2, 2, heads * length).transpose(0, 2, 1, 3).astype(BF16)
        tot = tot.reshape(size_z, 2, 2 * heads * length // width, width)
        packed.append(jnp.concatenate([num, tot], axis=2))
    if size_y == 2:
        other = lax.ppermute(packed[1], "mp", [(i, i ^ 2) for i in range(4)])
        summed = packed[0].astype(F32) + other.astype(F32)
    elif size_y == 1:
        summed = packed[0].astype(F32)
    else:
        summed = scatter_y_sum(jnp.stack(packed))
    other = swap_x(lax.dynamic_index_in_dim(summed, 1 - x, 1, keepdims=False).astype(BF16))
    summed = lax.dynamic_index_in_dim(summed, x, 1, keepdims=False) + other.astype(F32)
    exchanged = lax.all_to_all(
        summed.astype(BF16), "dp", 0, 0, axis_index_groups=z_groups(), tiled=True
    )
    summed = jnp.sum(exchanged.astype(F32), axis=0)
    width = summed.shape[1]
    heads = width // HEAD_DIM
    num = summed[: 2 * length].reshape(2, length, heads, HEAD_DIM)
    tot = summed[2 * length :].reshape(2, heads, length).transpose(0, 2, 1)
    cross_mix = (num / tot[..., None]).astype(BF16).reshape(2 * length, width)
    second_answer = answer_sum(dot_t(cross_mix, dec_attn[5]), first_answer, core, y, size_y)
    answer_normed = rms_normed(second_answer)
    hidden = (
        jax.nn.gelu(dot(answer_normed, dec_ff[0]), approximate=True)
        * dot(answer_normed, dec_ff[1])
    ).astype(BF16)
    partial = plain_order(dot_t(hidden, dec_ff[2]), x, shard_width)
    residual = plain_order(pick(second_answer, x, 2, 0), x, shard_width)
    mine = pick(partial, x, 2, 0) + swap_x(pick(partial, 1 - x, 2, 0).astype(BF16)).astype(F32)
    mine = mine.reshape(length, size_y, 2, features // mp_count)
    other = swap_core(lax.dynamic_index_in_dim(mine, 1 - core, 2, keepdims=False).astype(BF16))
    mine = lax.dynamic_index_in_dim(mine, core, 2, keepdims=False) + other.astype(F32)
    summed = scatter_y_sum(mine.astype(BF16).transpose(1, 0, 2))
    own = pick(residual, lax.axis_index("mp"), mp_count, 1)
    return (own.astype(F32) + summed).astype(BF16)


def solution(mesh):
    in_specs = (
        P("dp", None),
        P("dp", None),
        P("dp", None),
        P("dp", None),
        P(None, "dp", "mp"),
        P(None, "dp", "mp"),
        P(None, "dp", "mp"),
        P(None, "dp", "mp"),
        P(None, "dp", "mp"),
    )
    out_specs = P("dp", "mp")
    return jax.shard_map(local, mesh=mesh, in_specs=in_specs, out_specs=out_specs, check_vma=False)
```

```python
import functools
import math

import jax
import jax.numpy as jnp
from jax import lax
from jax.experimental import pallas as pl
from jax.experimental.pallas import tpu as pltpu
from jax.sharding import PartitionSpec as P

HEAD_DIM = 64
MOST_LEN = 192
EPSILON = 1e-06
LANES = 128
HALO = 256
F32 = jnp.float32
BF16 = jnp.bfloat16
EXP2_FACTOR = 3.0 / math.sqrt(HEAD_DIM) * math.log2(math.e)


def rms_normed(values):
    values = values.astype(F32)
    factor = lax.rsqrt(jnp.mean(values * values, axis=-1, keepdims=True) + EPSILON)
    return (values * factor).astype(BF16)


def dot(left, right):
    return jnp.dot(left, right, preferred_element_type=F32)


def dot_t(left, right):
    return lax.dot_general(left, right, (((1,), (1,)), ((), ())), preferred_element_type=F32)


def swap_x(value):
    count = lax.axis_size("dp")
    return lax.ppermute(value, "dp", [(i, i ^ 1) for i in range(count)])


def swap_core(value):
    count = lax.axis_size("mp")
    return lax.ppermute(value, "mp", [(i, i ^ 1) for i in range(count)])


def z_groups():
    count = lax.axis_size("dp")
    return [[i + x for i in range(0, count, 2)] for x in range(2)]


def y_groups():
    count = lax.axis_size("mp")
    return [[i + c for i in range(0, count, 2)] for c in range(2)]


def gather_z(value, axis):
    return lax.all_gather(value, "dp", axis_index_groups=z_groups(), axis=axis, tiled=True)


def few_z():
    return lax.axis_size("dp") // 2 <= 4


def swap_z(value, step):
    count = lax.axis_size("dp")
    return lax.ppermute(value, "dp", [(i, i ^ (2 * step)) for i in range(count)])


def z_place(index):
    return index ^ (lax.axis_index("dp") // 2) if few_z() else index


def collect_z(value, axis):
    if not few_z():
        return gather_z(value, axis)
    pieces = [value] + [swap_z(value, step) for step in range(1, lax.axis_size("dp") // 2)]
    return jnp.concatenate(pieces, axis=axis)


def tie(value, *others):
    return lax.optimization_barrier((value, *others))[0]


def swap_y(value):
    return lax.ppermute(value, "mp", [(i, i ^ 2) for i in range(4)])


def gather_y(value):
    size_y = lax.axis_size("mp") // 2
    if size_y == 1:
        return [value]
    if size_y == 2:
        return [value, swap_y(value)]
    pieces = lax.all_gather(value, "mp", axis_index_groups=y_groups(), axis=0)
    return [pieces[i] for i in range(size_y)]


def scatter_y_sum(value):
    size_y = lax.axis_size("mp") // 2
    y = lax.axis_index("mp") // 2
    if size_y == 2:
        other = swap_y(lax.dynamic_index_in_dim(value, 1 - y, 0, keepdims=False))
        own = lax.dynamic_index_in_dim(value, y, 0, keepdims=False)
        return own.astype(F32) + other.astype(F32)
    summed = lax.psum_scatter(
        value, "mp", scatter_dimension=0, axis_index_groups=y_groups(), tiled=True
    )
    return summed[0].astype(F32)


def pick(value, index, count, axis):
    width = value.shape[axis] // count
    return lax.dynamic_slice_in_dim(value, index * width, width, axis)


def in_order(first, own, other, axis):
    return jnp.concatenate(
        [jnp.where(first, own, other), jnp.where(first, other, own)], axis=axis
    )


def spread(block, through_x):
    if lax.axis_size("mp") != 4:
        return gather_y(jnp.concatenate([block, swap_x(block)], axis=1))
    side, over = swap_x(block), swap_y(block)
    far = []
    if through_x > 0:
        far.append(swap_x(over[:through_x]))
    if through_x < block.shape[0]:
        far.append(swap_y(side[through_x:]))
    far = far[0] if len(far) == 1 else jnp.concatenate(far, axis=0)
    return [jnp.concatenate([block, side], axis=1), jnp.concatenate([over, far], axis=1)]


def fetch_dec(shard, x, after):
    both = jnp.stack([pick(shard, x, 2, 2), swap_x(pick(shard, 1 - x, 2, 2))], axis=1)
    full = gather_z(tie(both, after), 2)
    return full.reshape(full.shape[0], -1, full.shape[3])


def own_first(values, x, width, place):
    size_z = values.shape[1] // (2 * width)
    blocks = [
        lax.dynamic_slice_in_dim(values, (2 * place(z) + index) * width, width, 1)
        for index in (x, 1 - x)
        for z in range(size_z)
    ]
    return jnp.concatenate(blocks, axis=1)


def enc_attention_kernel(low_ref, high_ref, seg_q_ref, seg_k_ref, q_ref, k_ref, v_ref, o_ref, acc):
    block = pl.program_id(0)
    rows, width = q_ref.shape
    key_rows = seg_k_ref.shape[2]
    acc[...] = jnp.zeros_like(acc)
    lane = lax.broadcasted_iota(jnp.int32, (1, LANES), 1)
    low_half = lane < HEAD_DIM
    queries = []
    for p in range(width // LANES):
        pair = q_ref[:, p * LANES : (p + 1) * LANES]
        zero = jnp.zeros_like(pair)
        queries.append(
            jnp.concatenate(
                [jnp.where(low_half, pair, zero), jnp.where(low_half, zero, pair)], axis=0
            )
        )
    seg_q = seg_q_ref[:, :key_rows]
    seg_q = jnp.concatenate([seg_q, seg_q], axis=0)

    def step(j, carry):
        begin = pl.multiple_of(j * key_rows, key_rows)
        allowed = seg_q == seg_k_ref[j]
        for p in range(width // LANES):
            keys = k_ref[pl.ds(begin, key_rows), p * LANES : (p + 1) * LANES]
            vals = v_ref[pl.ds(begin, key_rows), p * LANES : (p + 1) * LANES]
            scores = dot_t(queries[p], keys) * EXP2_FACTOR
            weights = jnp.where(allowed, jnp.exp2(scores), 0.0).astype(BF16)
            one = jnp.ones_like(vals)
            acc[2 * p] += dot(weights[:rows], jnp.where(low_half, vals, one))
            acc[2 * p + 1] += dot(weights[rows:], jnp.where(low_half, one, vals))
        return carry

    lax.fori_loop(low_ref[block], high_ref[block], step, 0)
    for p in range(width // LANES):
        first, second = acc[2 * p], acc[2 * p + 1]
        o_ref[:, p * LANES : (p + 1) * LANES] = jnp.where(
            low_half,
            first / pltpu.roll(first, HEAD_DIM, 1),
            second / pltpu.roll(second, HEAD_DIM, 1),
        ).astype(BF16)


def enc_attention(low, high, seg_q, seg_k, q, k, v):
    rows, width = q.shape
    blocks = low.shape[0]
    query_rows = rows // blocks
    full = lambda i, *_: (0, 0)
    return pl.pallas_call(
        enc_attention_kernel,
        out_shape=jax.ShapeDtypeStruct((rows, width), BF16),
        grid_spec=pltpu.PrefetchScalarGridSpec(
            num_scalar_prefetch=2,
            grid=(blocks,),
            in_specs=[
                pl.BlockSpec((query_rows, LANES), lambda i, *_: (i, 0)),
                pl.BlockSpec(seg_k.shape, lambda i, *_: (0, 0, 0)),
                pl.BlockSpec((query_rows, width), lambda i, *_: (i, 0)),
                pl.BlockSpec(k.shape, full),
                pl.BlockSpec(v.shape, full),
            ],
            out_specs=pl.BlockSpec((query_rows, width), lambda i, *_: (i, 0)),
            scratch_shapes=[pltpu.VMEM((width // HEAD_DIM, query_rows, LANES), F32)],
        ),
        cost_estimate=pl.CostEstimate(
            flops=rows * 384 * width * 8, bytes_accessed=rows * width * 8, transcendentals=0
        ),
        name="enc_attention",
    )(low, high, seg_q, seg_k, q, k, v)


def cross_kernel(begin_ref, end_ref, question_ref, q_ref, k_ref, v_ref, num_ref, tot_ref, acc, *, key_rows):
    questions, length, width = q_ref.shape
    acc[...] = jnp.zeros_like(acc)
    lane = lax.broadcasted_iota(jnp.int32, (1, LANES), 1)
    low_half = lane < HEAD_DIM

    def passage(s, carry):
        begin, end, question = begin_ref[s], end_ref[s], question_ref[s]

        def step(j, inner):
            offset = pl.multiple_of(j * key_rows, key_rows)
            position = offset + lax.broadcasted_iota(jnp.int32, (1, key_rows), 1)
            allowed = (position >= begin) & (position < end)
            for p in range(width // LANES):
                columns = slice(p * LANES, (p + 1) * LANES)
                pair = q_ref[question, :, columns]
                zero = jnp.zeros_like(pair)
                queries = jnp.concatenate(
                    [jnp.where(low_half, pair, zero), jnp.where(low_half, zero, pair)], axis=0
                )
                keys = k_ref[pl.ds(offset, key_rows), columns]
                vals = v_ref[pl.ds(offset, key_rows), columns]
                scores = dot_t(queries, keys) * EXP2_FACTOR
                weights = jnp.where(allowed, jnp.exp2(scores), 0.0).astype(BF16)
                one = jnp.ones_like(vals)
                acc[question, 2 * p] += dot(weights[:length], jnp.where(low_half, vals, one))
                acc[question, 2 * p + 1] += dot(weights[length:], jnp.where(low_half, one, vals))
            return inner

        blocks = jnp.where(end > begin, (end + key_rows - 1) // key_rows, 0)
        lax.fori_loop(begin // key_rows, blocks, step, 0)
        return carry

    lax.fori_loop(0, begin_ref.shape[0], passage, 0)
    eye = lax.broadcasted_iota(jnp.int32, (length, LANES), 0) == lax.broadcasted_iota(
        jnp.int32, (length, LANES), 1
    )

    def finish(question, carry):
        for p in range(width // LANES):
            first, second = acc[question, 2 * p], acc[question, 2 * p + 1]
            num_ref[question, :, p * LANES : (p + 1) * LANES] = jnp.where(
                low_half, first, second
            ).astype(BF16)
            first = jnp.where(low_half, pltpu.roll(first, HEAD_DIM, 1), first)
            second = jnp.where(low_half, second, pltpu.roll(second, HEAD_DIM, 1))
            for h, total in ((2 * p, first), (2 * p + 1, second)):
                tot_ref[question, h : h + 1, :] = jnp.sum(
                    jnp.where(eye, total, 0.0), axis=0, keepdims=True
                )
        return carry

    lax.fori_loop(0, questions, finish, 0)


def cross_attention(begin, end, question, q, k, v):
    questions, length, width = q.shape
    key_rows = math.gcd(k.shape[0], LANES)
    vmem = pl.BlockSpec(memory_space=pltpu.VMEM)
    smem = pl.BlockSpec(memory_space=pltpu.SMEM)
    return pl.pallas_call(
        functools.partial(cross_kernel, key_rows=key_rows),
        out_shape=(
            jax.ShapeDtypeStruct((questions, length, width), BF16),
            jax.ShapeDtypeStruct((questions, width // HEAD_DIM, length), F32),
        ),
        in_specs=[smem, smem, smem, vmem, vmem, vmem],
        out_specs=(vmem, vmem),
        scratch_shapes=[pltpu.VMEM((questions, width // HEAD_DIM, length, LANES), F32)],
        cost_estimate=pl.CostEstimate(
            flops=k.shape[0] * 256 * width * 8, bytes_accessed=4 * q.size, transcendentals=0
        ),
        name="cross_attention",
    )(begin, end, question, q, k, v)


def self_attention(q, k, v, questions):
    rows, width = q.shape
    heads = width // HEAD_DIM
    length = rows // questions
    shape = (questions, length, heads, HEAD_DIM)
    q, k, v = q.reshape(shape), k.reshape(shape), v.reshape(shape)
    scores = jnp.einsum("oqhc,okhc->ohqk", q, k, preferred_element_type=F32)
    causal = jnp.arange(length)[None, :] <= jnp.arange(length)[:, None]
    weights = jnp.where(causal, jnp.exp(scores * (3.0 / math.sqrt(HEAD_DIM))), 0.0)
    totals = jnp.sum(weights, axis=3)
    mixture = jnp.einsum("ohqk,okhc->oqhc", weights.astype(BF16), v, preferred_element_type=F32)
    return (mixture / jnp.transpose(totals, (0, 2, 1))[..., None]).astype(BF16).reshape(rows, width)


def core_rows_sum(partial, core):
    other = swap_core(pick(partial, 1 - core, 2, 0).astype(BF16))
    return pick(partial, core, 2, 0) + other.astype(F32)


def flip(values):
    half = values.shape[1] // 2
    return jnp.concatenate([values[:, half:], values[:, :half]], axis=1)


def answer_sum(partial, core, size_y):
    mine = core_rows_sum(partial, core).astype(BF16)
    if size_y != 2:
        mine = (mine.astype(F32) + flip(swap_x(mine)).astype(F32)).astype(BF16)
        return lax.psum(mine.astype(F32), "mp", axis_index_groups=y_groups())
    rows = mine.shape[0] // 2
    top, bottom = mine[:rows], mine[rows:]
    other_top, other_bottom = swap_x(top), swap_y(bottom)
    top = (top.astype(F32) + flip(other_top).astype(F32)).astype(BF16)
    bottom = (bottom.astype(F32) + other_bottom.astype(F32)).astype(BF16)
    other_top, other_bottom = swap_y(top), swap_x(bottom)
    top = top.astype(F32) + other_top.astype(F32)
    bottom = bottom.astype(F32) + flip(other_bottom).astype(F32)
    return jnp.concatenate([top, bottom], axis=0)


def both_cores(values, core):
    return in_order(core == 0, values, swap_core(values), 0)


def local(
    passage_embeds,
    passage_lengths,
    slot_question,
    answer_states,
    w_enc_attn,
    w_enc_ff,
    w_cross_kv,
    w_dec_attn,
    w_dec_ff,
):
    dp_count, mp_count = lax.axis_size("dp"), lax.axis_size("mp")
    size_z, size_y = dp_count // 2, mp_count // 2
    x = lax.axis_index("dp") % 2
    core = lax.axis_index("mp") % 2
    y = lax.axis_index("mp") // 2
    features = passage_embeds.shape[1]
    shard_width = features // dp_count

    z = lax.axis_index("dp") // 2
    block = collect_z(w_enc_attn, 1)
    gate_block = collect_z(tie(w_enc_ff[0:1], block), 1)
    up_block = collect_z(tie(w_enc_ff[1:2], gate_block), 1)
    down_block = collect_z(tie(w_enc_ff[2:3], up_block), 1)
    cross_block = collect_z(tie(w_cross_kv, down_block), 1)
    attn_weights = spread(block, 2)
    gate_weights = spread(tie(gate_block, *attn_weights), 1)
    up_weights = spread(tie(up_block, *gate_weights), 0)
    down_weights = spread(tie(down_block, *up_weights), 1)
    cross_weights = spread(tie(cross_block, *down_weights), 0)
    dec_attn = fetch_dec(w_dec_attn, x, block)
    dec_ff = fetch_dec(w_dec_ff, x, down_block)

    row_count = passage_embeds.shape[0]
    rows = row_count // size_y
    sides = min(size_y - 1, 2)
    window = min(row_count, rows + sides * HALO)
    row_begin = y * rows
    window_begin = jnp.clip(row_begin - HALO, 0, row_count - window)
    lengths = passage_lengths[0]
    ends = jnp.cumsum(lengths)
    starts = ends - lengths
    positions = window_begin + jnp.arange(window, dtype=jnp.int32)
    segment = jnp.sum((positions[:, None] >= ends[None, :]).astype(jnp.int32), axis=1)
    query_block = math.gcd(rows, LANES)
    key_block = math.gcd(window, LANES)
    block_first = row_begin + jnp.arange(rows // query_block, dtype=jnp.int32) * query_block
    block_last = block_first + query_block - 1
    inside_first = jnp.max(
        jnp.where(starts[None, :] <= block_first[:, None], starts[None, :], 0), axis=1
    )
    inside_last = jnp.min(
        jnp.where(ends[None, :] > block_last[:, None], ends[None, :], row_count), axis=1
    )
    low = (inside_first - window_begin) // key_block
    high = (inside_last - window_begin + key_block - 1) // key_block
    seg_k = segment.reshape(window // key_block, 1, key_block)
    seg_q = jnp.broadcast_to(
        lax.dynamic_slice_in_dim(segment, row_begin - window_begin, rows, 0)[:, None],
        (rows, LANES),
    )

    embeds = own_first(
        lax.dynamic_slice_in_dim(passage_embeds, window_begin, window, 0), x, shard_width, z_place
    )
    normed = rms_normed(embeds)
    own_begin = row_begin - window_begin
    normed_q = lax.dynamic_slice_in_dim(normed, own_begin, rows, 0)
    partial = 0.0
    for weights in attn_weights:
        mixture = enc_attention(
            low,
            high,
            seg_q,
            seg_k,
            dot(normed_q, weights[0]).astype(BF16),
            dot(normed, weights[1]).astype(BF16),
            dot(normed, weights[2]).astype(BF16),
        )
        partial = partial + dot_t(mixture, weights[3])
    own_embeds = lax.dynamic_slice_in_dim(embeds, own_begin + core * (rows // 2), rows // 2, 0)
    first_rows = (own_embeds.astype(F32) + core_rows_sum(partial, core)).astype(BF16)
    normed = rms_normed(first_rows)
    normed = both_cores(normed, core)
    partial = 0.0
    for gate, up, down in zip(gate_weights, up_weights, down_weights):
        hidden = (
            jax.nn.gelu(dot(normed, gate[0]), approximate=True) * dot(normed, up[0])
        ).astype(BF16)
        partial = partial + dot_t(hidden, down[0])
    second_rows = (first_rows.astype(F32) + core_rows_sum(partial, core)).astype(BF16)
    normed = rms_normed(second_rows)
    normed = both_cores(normed, core)

    length = answer_states.shape[0]
    answers = in_order(x == 0, answer_states, swap_x(answer_states), 0)
    answers = own_first(answers, x, shard_width, lambda index: index)
    answer_normed = rms_normed(answers)
    self_mix = self_attention(
        dot(answer_normed, dec_attn[0]).astype(BF16),
        dot(answer_normed, dec_attn[1]).astype(BF16),
        dot(answer_normed, dec_attn[2]).astype(BF16),
        2,
    )
    first_sum = answer_sum(dot_t(self_mix, dec_attn[3]), core, size_y)
    first_answer = (pick(answers, core, 2, 0).astype(F32) + first_sum).astype(BF16)
    cross_q = dot(both_cores(rms_normed(first_answer), core), dec_attn[4]).astype(BF16)
    cross_q = collect_z(cross_q, 0)
    cross_q = in_order(x == 0, cross_q, swap_x(cross_q), 1)
    cross_q = gather_y(cross_q.reshape(dp_count, length, cross_q.shape[1]))

    begin = jnp.clip(starts - row_begin, 0, rows)
    end = jnp.clip(ends - row_begin, 0, rows)
    questions = slot_question[0]
    questions = z_place(questions // 2) * 2 + questions % 2
    packed = []
    for queries, kv in zip(cross_q[::-1], cross_weights[::-1]):
        if packed:
            queries = tie(queries, packed[-1])
        num, tot = cross_attention(
            begin,
            end,
            questions,
            queries,
            dot(normed, kv[0]).astype(BF16),
            dot(normed, kv[1]).astype(BF16),
        )
        width = num.shape[2] // 2
        heads = tot.shape[1] // 2
        num = num.reshape(size_z, 2 * length, 2, width).transpose(0, 2, 1, 3)
        tot = tot.reshape(size_z, 2, 2, heads * length).transpose(0, 2, 1, 3).astype(BF16)
        tot = tot.reshape(size_z, 2, 2 * heads * length // width, width)
        packed.append(jnp.concatenate([num, tot], axis=2))
    packed = packed[::-1]
    if size_y == 2:
        summed = packed[0].astype(F32) + swap_y(packed[1]).astype(F32)
    elif size_y == 1:
        summed = packed[0].astype(F32)
    else:
        summed = scatter_y_sum(jnp.stack(packed))
    other = swap_x(lax.dynamic_index_in_dim(summed, 1 - x, 1, keepdims=False).astype(BF16))
    summed = lax.dynamic_index_in_dim(summed, x, 1, keepdims=False) + other.astype(F32)
    if few_z():
        own = summed[0]
        for step in range(1, size_z):
            own = own + swap_z(summed[step].astype(BF16), step).astype(F32)
        summed = own
    else:
        exchanged = lax.all_to_all(
            summed.astype(BF16), "dp", 0, 0, axis_index_groups=z_groups(), tiled=True
        )
        summed = jnp.sum(exchanged.astype(F32), axis=0)
    width = summed.shape[1]
    heads = width // HEAD_DIM
    num = summed[: 2 * length].reshape(2, length, heads, HEAD_DIM)
    tot = summed[2 * length :].reshape(2, heads, length).transpose(0, 2, 1)
    cross_mix = (num / tot[..., None]).astype(BF16).reshape(2 * length, width)
    second_sum = answer_sum(dot_t(cross_mix, dec_attn[5]), core, size_y)
    second_answer = (first_answer.astype(F32) + second_sum).astype(BF16)
    answer_normed = both_cores(rms_normed(second_answer), core)
    hidden = (
        jax.nn.gelu(dot(answer_normed, dec_ff[0]), approximate=True)
        * dot(answer_normed, dec_ff[1])
    ).astype(BF16)
    columns = features // (2 * mp_count)
    partial = dot_t(hidden, dec_ff[2]).reshape(2 * length, 2, size_y, 2, columns)
    other = swap_core(lax.dynamic_index_in_dim(partial, 1 - core, 3, keepdims=False).astype(BF16))
    mine = lax.dynamic_index_in_dim(partial, core, 3, keepdims=False) + other.astype(F32)
    other = swap_x(pick(mine, 1 - x, 2, 0).astype(BF16)).astype(F32)
    mine = pick(mine, x, 2, 0) + jnp.stack([other[:, 1], other[:, 0]], axis=1)
    summed = scatter_y_sum(mine.astype(BF16).transpose(2, 0, 1, 3))
    residual = pick(both_cores(second_answer, core), x, 2, 0)
    residual = residual.reshape(length, 2, mp_count, columns)
    residual = lax.dynamic_index_in_dim(residual, lax.axis_index("mp"), 2, keepdims=False)
    result = (residual.astype(F32) + summed).astype(BF16)
    result = result.reshape(length, 2, columns // shard_width, 1, shard_width)
    return in_order(x == 0, result[:, 0], result[:, 1], 2).reshape(length, 2 * columns)


def solution(mesh):
    in_specs = (
        P("dp", None),
        P("dp", None),
        P("dp", None),
        P("dp", None),
        P(None, "dp", "mp"),
        P(None, "dp", "mp"),
        P(None, "dp", "mp"),
        P(None, "dp", "mp"),
        P(None, "dp", "mp"),
    )
    out_specs = P("dp", "mp")
    return jax.shard_map(local, mesh=mesh, in_specs=in_specs, out_specs=out_specs, check_vma=False)
```

```python
import functools
import math

import jax
import jax.numpy as jnp
from jax import lax
from jax.experimental import pallas as pl
from jax.experimental.pallas import tpu as pltpu
from jax.sharding import PartitionSpec as P


HEAD_DIM = 64
EPSILON = 1e-06
LANES = 128
HALO = 256
F32 = jnp.float32
BF16 = jnp.bfloat16
EXP2_FACTOR = 3.0 / math.sqrt(HEAD_DIM) * math.log2(math.e)


def rms_normed(values):
    values = values.astype(F32)
    factor = lax.rsqrt(jnp.mean(values * values, axis=-1, keepdims=True) + EPSILON)
    return (values * factor).astype(BF16)


def dot(left, right):
    return jnp.dot(left, right, preferred_element_type=F32)


def dot_t(left, right):
    return lax.dot_general(left, right, (((1,), (1,)), ((), ())), preferred_element_type=F32)


def swap_x(value):
    count = lax.axis_size("dp")
    return lax.ppermute(value, "dp", [(i, i ^ 1) for i in range(count)])


def swap_core(value):
    count = lax.axis_size("mp")
    return lax.ppermute(value, "mp", [(i, i ^ 1) for i in range(count)])


def z_groups():
    count = lax.axis_size("dp")
    return [[i + x for i in range(0, count, 2)] for x in range(2)]


def y_groups():
    count = lax.axis_size("mp")
    return [[i + c for i in range(0, count, 2)] for c in range(2)]


def gather_z(value, axis):
    return lax.all_gather(value, "dp", axis_index_groups=z_groups(), axis=axis, tiled=True)


def few_z():
    return lax.axis_size("dp") // 2 <= 4


def swap_z(value, step):
    count = lax.axis_size("dp")
    return lax.ppermute(value, "dp", [(i, i ^ (2 * step)) for i in range(count)])


def z_place(index):
    return index ^ (lax.axis_index("dp") // 2) if few_z() else index


def pieces_z(value, axis):
    if not few_z():
        return [gather_z(value, axis)]
    return [value] + [swap_z(value, step) for step in range(1, lax.axis_size("dp") // 2)]


def meet(*values):
    return lax.optimization_barrier(values)


def swap_y(value):
    return lax.ppermute(value, "mp", [(i, i ^ 2) for i in range(4)])


def gather_y(value):
    size_y = lax.axis_size("mp") // 2
    if size_y == 1:
        return [value]
    if size_y == 2:
        return [value, swap_y(value)]
    pieces = lax.all_gather(value, "mp", axis_index_groups=y_groups(), axis=0)
    return [pieces[i] for i in range(size_y)]


def scatter_y_sum(value):
    size_y = lax.axis_size("mp") // 2
    y = lax.axis_index("mp") // 2
    if size_y == 2:
        other = swap_y(lax.dynamic_index_in_dim(value, 1 - y, 0, keepdims=False))
        own = lax.dynamic_index_in_dim(value, y, 0, keepdims=False)
        return own.astype(F32) + other.astype(F32)
    summed = lax.psum_scatter(
        value, "mp", scatter_dimension=0, axis_index_groups=y_groups(), tiled=True
    )
    return summed[0].astype(F32)


def join_kernel(*refs, axis):
    *pieces, out, sems = refs
    begin, copies = 0, []
    for index, piece in enumerate(pieces):
        size = piece.shape[axis]
        where = (slice(None),) * axis + (pl.ds(begin, size),)
        copies.append(pltpu.make_async_copy(piece, out.at[where], sems.at[index]))
        copies[-1].start()
        begin += size
    for copy in copies:
        copy.wait()


def join(pieces, axis):
    if len(pieces) == 1:
        return pieces[0]
    shape = list(pieces[0].shape)
    shape[axis] = sum(piece.shape[axis] for piece in pieces)
    if axis == len(shape) - 1 and pieces[0].shape[axis] % LANES:
        return jnp.concatenate(pieces, axis=axis)
    return pl.pallas_call(
        functools.partial(join_kernel, axis=axis),
        out_shape=jax.ShapeDtypeStruct(tuple(shape), pieces[0].dtype),
        in_specs=[pl.BlockSpec(memory_space=pl.ANY)] * len(pieces),
        out_specs=pl.BlockSpec(memory_space=pltpu.VMEM),
        scratch_shapes=[pltpu.SemaphoreType.DMA((len(pieces),))],
        cost_estimate=pl.CostEstimate(
            flops=0, bytes_accessed=4 * math.prod(shape), transcendentals=0
        ),
        name="join",
    )(*pieces)


def pick(value, index, count, axis):
    width = value.shape[axis] // count
    return lax.dynamic_slice_in_dim(value, index * width, width, axis)


def in_order(first, own, other, axis):
    return jnp.concatenate(
        [jnp.where(first, own, other), jnp.where(first, other, own)], axis=axis
    )


def spread_near(block):
    return (swap_x(block), swap_y(block)) if lax.axis_size("mp") == 4 else (swap_x(block),)


def spread_far(near, axis):
    if len(near) == 1:
        return ()
    side, over = near
    cut = far_cut(side.shape[axis])
    first = lax.slice_in_dim(over, 0, cut, axis=axis)
    second = lax.slice_in_dim(side, cut, side.shape[axis], axis=axis)
    return (swap_x(first), swap_y(second))


def far_cut(size):
    return -(-(size // 2) // LANES) * LANES


def attn_pieces(block, near, far):
    own = join([block, near[0]], 1)
    if len(near) == 1:
        return gather_y(own)
    return [own, join([near[1], *far], 1)]


def ff_piece(block, near, far):
    own = [(block, 0, block.shape[1]), (near[0], 0, block.shape[1])]
    if len(near) == 1:
        rest = [gather_y(half)[1:] for half in (block, near[0])]
        return [own] + [
            [(mine, 0, mine.shape[1]), (theirs, 0, theirs.shape[1])]
            for mine, theirs in zip(*rest)
        ]
    over = near[1]
    cut = far[0].shape[1]
    return [
        own,
        [(over, 0, cut), (far[0], 0, cut)],
        [(over, cut, over.shape[1] - cut), (far[1], 0, over.shape[1] - cut)],
    ]


def ff_kernel(*refs, chunks, done, last):
    h_ref, refs, out_ref = refs[0], refs[1:-1], refs[-1]
    half = h_ref.shape[1] // 2
    mine, theirs = h_ref[:, :half], h_ref[:, half:]

    def weight(place):
        index, lead, begin, count = place
        return refs[index][lead, begin : begin + count, :]

    sums = [None, None]

    def add(hidden, places):
        for k in range(2):
            term = dot(hidden, weight(places[k]))
            sums[k] = term if sums[k] is None else sums[k] + term

    for index, places in done:
        add(refs[index][...], places)
    for gate, up, *down in chunks:
        gated = dot_t(mine, weight(gate[0])) + dot_t(theirs, weight(gate[1]))
        linear = dot_t(mine, weight(up[0])) + dot_t(theirs, weight(up[1]))
        hidden = (jax.nn.gelu(gated, approximate=True) * linear).astype(BF16)
        if last:
            add(hidden, down[0])
        else:
            out_ref[...] = hidden
    if last:
        out_ref[:, :half] = sums[0].astype(BF16)
        out_ref[:, half:] = sums[1].astype(BF16)


def ff(h, chunks, done, last):
    rows = h.shape[0]
    block = math.gcd(rows, 384)
    operands, specs, seen = [h], [pl.BlockSpec((block, h.shape[1]), lambda i: (i, 0))], {}

    def place(lead, entry):
        array, begin, count, *more = entry
        lead += sum(more)
        if id(array) not in seen:
            seen[id(array)] = len(operands) - 1
            operands.append(array)
            specs.append(pl.BlockSpec(array.shape, lambda i: (0, 0, 0)))
        return seen[id(array)], lead, begin, count

    def places(lead, entries):
        return tuple(place(lead, entry) for entry in entries)

    before = []
    for hidden, (lead, entries) in done:
        operands.append(hidden)
        specs.append(pl.BlockSpec((block, hidden.shape[1]), lambda i: (i, 0)))
        before.append((len(operands) - 2, places(lead, entries)))
    plan = [tuple(places(lead, entries) for lead, entries in chunk) for chunk in chunks]
    width = h.shape[1] if last else chunks[0][0][1][0][2]
    flops = 2 * rows * h.shape[1] * (4 if last else 2) * sum(c[0][1][0][2] for c in chunks)
    return pl.pallas_call(
        functools.partial(ff_kernel, chunks=plan, done=before, last=last),
        out_shape=jax.ShapeDtypeStruct((rows, width), BF16),
        grid=(rows // block,),
        in_specs=specs,
        out_specs=pl.BlockSpec((block, width), lambda i: (i, 0)),
        compiler_params=pltpu.CompilerParams(vmem_limit_bytes=48 * 2**20),
        cost_estimate=pl.CostEstimate(
            flops=flops, bytes_accessed=2 * rows * (h.shape[1] + width), transcendentals=0
        ),
        name="ff",
    )(*operands)


def out_kernel(*refs):
    *pairs, out_ref = refs
    total = None
    for mix_ref, weight_ref in zip(pairs[::2], pairs[1::2]):
        term = dot_t(mix_ref[...], weight_ref[0])
        total = term if total is None else total + term
    out_ref[...] = total.astype(BF16)


def out_project(mixes, weights, index):
    rows, features = mixes[0].shape[0], weights[0].shape[1]
    block = math.gcd(rows, 384)
    operands, specs = [], []
    for mix, weight in zip(mixes, weights):
        operands += [mix, weight]
        specs.append(pl.BlockSpec((block, mix.shape[1]), lambda i: (i, 0)))
        specs.append(pl.BlockSpec((1, *weight.shape[1:]), lambda i: (index, 0, 0)))
    return pl.pallas_call(
        out_kernel,
        out_shape=jax.ShapeDtypeStruct((rows, features), BF16),
        grid=(rows // block,),
        in_specs=specs,
        out_specs=pl.BlockSpec((block, features), lambda i: (i, 0)),
        compiler_params=pltpu.CompilerParams(vmem_limit_bytes=24 * 2**20),
        cost_estimate=pl.CostEstimate(
            flops=2 * rows * features * sum(m.shape[1] for m in mixes),
            bytes_accessed=4 * rows * features,
            transcendentals=0,
        ),
        name="out_project",
    )(*operands)


def own_first(values, x, width, place):
    size_z = values.shape[1] // (2 * width)
    blocks = [
        lax.dynamic_slice_in_dim(values, (2 * place(z) + index) * width, width, 1)
        for index in (x, 1 - x)
        for z in range(size_z)
    ]
    return jnp.concatenate(blocks, axis=1)


def two_heads(q, k, v, allowed, low_half):
    zero, one = jnp.zeros_like(v), jnp.ones_like(v)
    keys = jnp.concatenate([jnp.where(low_half, k, zero), jnp.where(low_half, zero, k)], axis=0)
    vals = jnp.concatenate(
        [
            jnp.concatenate([jnp.where(low_half, v, zero), jnp.where(low_half, one, zero)], axis=1),
            jnp.concatenate([jnp.where(low_half, zero, v), jnp.where(low_half, zero, one)], axis=1),
        ],
        axis=0,
    )
    weights = jnp.exp2(dot_t(q, keys) * EXP2_FACTOR)
    count = k.shape[0]
    if count % LANES == 0:
        weights = jnp.where(jnp.concatenate([allowed, allowed], axis=1), weights, 0.0)
        return dot(weights.astype(BF16), vals)
    first = jnp.where(allowed, weights[:, :count], 0.0).astype(BF16)
    second = jnp.where(allowed, weights[:, count:], 0.0).astype(BF16)
    return dot(first, vals[:count]) + dot(second, vals[count:])


def enc_attention_kernel(
    low_ref, high_ref, seg_q_ref, seg_k_ref, q_ref, k_ref, v_ref, o_ref, acc, *, rows
):
    width = q_ref.shape[1]
    key_rows = seg_k_ref.shape[2]
    last = seg_k_ref.shape[0] - 1
    low_half = lax.broadcasted_iota(jnp.int32, (1, LANES), 1) < HEAD_DIM

    def block(i, carry):
        begin = pl.multiple_of(i * rows, rows)
        low, high = low_ref[i], high_ref[i]
        acc[...] = jnp.zeros_like(acc)

        def step(j, inner):
            for p in range(width // LANES):
                columns = slice(p * LANES, (p + 1) * LANES)
                total = None
                for u in range(2):
                    index = low + 2 * j + u
                    clipped = jnp.minimum(index, last)
                    offset = pl.multiple_of(clipped * key_rows, key_rows)
                    seg_k = jnp.where(index < high, seg_k_ref[clipped], -1)
                    allowed = seg_q_ref[pl.ds(begin, rows), :key_rows] == seg_k
                    part = two_heads(
                        q_ref[pl.ds(begin, rows), columns],
                        k_ref[pl.ds(offset, key_rows), columns],
                        v_ref[pl.ds(offset, key_rows), columns],
                        allowed,
                        low_half,
                    )
                    total = part if total is None else total + part
                acc[p] += total
            return inner

        lax.fori_loop(0, (high - low + 1) // 2, step, 0)
        for p in range(width // LANES):
            sums = acc[p]
            o_ref[pl.ds(begin, rows), p * LANES : (p + 1) * LANES] = (
                sums[:, :LANES] / sums[:, LANES:]
            ).astype(BF16)
        return carry

    lax.fori_loop(0, low_ref.shape[0], block, 0)


def enc_attention(low, high, seg_q, seg_k, q, k, v):
    rows, width = q.shape
    query_rows = rows // low.shape[0]
    vmem = pl.BlockSpec(memory_space=pltpu.VMEM)
    smem = pl.BlockSpec(memory_space=pltpu.SMEM)
    return pl.pallas_call(
        functools.partial(enc_attention_kernel, rows=query_rows),
        out_shape=jax.ShapeDtypeStruct((rows, width), BF16),
        in_specs=[smem, smem] + [vmem] * 5,
        out_specs=vmem,
        scratch_shapes=[pltpu.VMEM((width // LANES, query_rows, 2 * LANES), F32)],
        cost_estimate=pl.CostEstimate(
            flops=rows * 384 * width * 8, bytes_accessed=rows * width * 8, transcendentals=0
        ),
        name="enc_attention",
    )(low, high, seg_q, seg_k, q, k, v)


def cross_kernel(
    begin_ref, end_ref, question_ref, q_ref, k_ref, v_ref, o_ref, acc, *, key_rows
):
    questions, length, width = q_ref.shape
    pairs = width // LANES
    last = k_ref.shape[0] // key_rows - 1
    acc[...] = jnp.zeros_like(acc)
    low_half = lax.broadcasted_iota(jnp.int32, (1, LANES), 1) < HEAD_DIM

    def passage(s, carry):
        begin, end, question = begin_ref[s], end_ref[s], question_ref[s]
        first = begin // key_rows

        def step(j, inner):
            for p in range(pairs):
                columns = slice(p * LANES, (p + 1) * LANES)
                total = None
                for u in range(2):
                    index = first + 2 * j + u
                    offset = pl.multiple_of(jnp.minimum(index, last) * key_rows, key_rows)
                    position = index * key_rows + lax.broadcasted_iota(
                        jnp.int32, (1, key_rows), 1
                    )
                    allowed = (position >= begin) & (position < end)
                    part = two_heads(
                        q_ref[question, :, columns],
                        k_ref[pl.ds(offset, key_rows), columns],
                        v_ref[pl.ds(offset, key_rows), columns],
                        allowed,
                        low_half,
                    )
                    total = part if total is None else total + part
                acc[question, p] += total
            return inner

        blocks = (end + key_rows - 1) // key_rows - first
        lax.fori_loop(0, jnp.where(end > begin, (blocks + 1) // 2, 0), step, 0)
        return carry

    lax.fori_loop(0, begin_ref.shape[0], passage, 0)
    eye = lax.broadcasted_iota(jnp.int32, (length, LANES), 0) == lax.broadcasted_iota(
        jnp.int32, (length, LANES), 1
    )
    extra = o_ref.shape[2] - 2 * length
    place = lax.broadcasted_iota(jnp.int32, (extra, LANES), 0)

    def finish(z, carry):
        for p in range(pairs):
            totals = jnp.zeros((extra, LANES), F32)
            for x in range(2):
                sums = acc[2 * z + x, p]
                o_ref[z, p, x * length : (x + 1) * length, :] = sums[:, :LANES].astype(BF16)
                total = sums[:, LANES:]
                turned = pltpu.roll(total, HEAD_DIM, 1)
                for h in range(2):
                    own = jnp.where(low_half, total, turned) if h == 0 else jnp.where(low_half, turned, total)
                    row = jnp.sum(jnp.where(eye, own, 0.0), axis=0, keepdims=True)
                    totals = jnp.where(place == 2 * x + h, row, totals)
            o_ref[z, p, 2 * length :, :] = totals.astype(BF16)
        return carry

    lax.fori_loop(0, questions // 2, finish, 0)


def cross_attention(begin, end, question, q, k, v):
    questions, length, width = q.shape
    key_rows = math.gcd(k.shape[0], LANES)
    pairs = width // LANES
    vmem = pl.BlockSpec(memory_space=pltpu.VMEM)
    smem = pl.BlockSpec(memory_space=pltpu.SMEM)
    return pl.pallas_call(
        functools.partial(cross_kernel, key_rows=key_rows),
        out_shape=jax.ShapeDtypeStruct((questions // 2, pairs, 2 * length + 16, LANES), BF16),
        in_specs=[smem, smem, smem, vmem, vmem, vmem],
        out_specs=vmem,
        scratch_shapes=[pltpu.VMEM((questions, pairs, length, 2 * LANES), F32)],
        cost_estimate=pl.CostEstimate(
            flops=k.shape[0] * 256 * width * 8, bytes_accessed=4 * q.size, transcendentals=0
        ),
        name="cross_attention",
    )(begin, end, question, q, k, v)


def by_column_x(sums, length):
    size_z, pairs = sums.shape[:2]
    if pairs == 2:
        return sums
    num = sums[:, 0, : 2 * length].reshape(size_z, 2 * length, 2, HEAD_DIM).transpose(0, 2, 1, 3)
    tot = sums[:, 0, 2 * length : 2 * length + 4].reshape(size_z, 2, 2, length)
    tot = tot.transpose(0, 2, 1, 3).reshape(size_z, 2, -1, HEAD_DIM)
    return jnp.concatenate([num, tot], axis=2)


def self_attention(q, k, v, questions):
    rows, width = q.shape
    heads = width // HEAD_DIM
    length = rows // questions
    shape = (questions, length, heads, HEAD_DIM)
    q, k, v = q.reshape(shape), k.reshape(shape), v.reshape(shape)
    scores = jnp.einsum("oqhc,okhc->ohqk", q, k, preferred_element_type=F32)
    causal = jnp.arange(length)[None, :] <= jnp.arange(length)[:, None]
    weights = jnp.where(causal, jnp.exp(scores * (3.0 / math.sqrt(HEAD_DIM))), 0.0)
    totals = jnp.sum(weights, axis=3)
    mixture = jnp.einsum("ohqk,okhc->oqhc", weights.astype(BF16), v, preferred_element_type=F32)
    return (mixture / jnp.transpose(totals, (0, 2, 1))[..., None]).astype(BF16).reshape(rows, width)


def core_rows_sum(partial, core):
    other = swap_core(pick(partial, 1 - core, 2, 0).astype(BF16))
    return pick(partial, core, 2, 0).astype(F32) + other.astype(F32)


def flip(values):
    half = values.shape[1] // 2
    return jnp.concatenate([values[:, half:], values[:, :half]], axis=1)


def answer_start(partial, core, size_y):
    mine = core_rows_sum(partial, core).astype(BF16)
    if size_y != 2:
        return (mine, swap_x(mine))
    rows = mine.shape[0] // 2
    top, bottom = mine[:rows], mine[rows:]
    return top, bottom, swap_x(top), swap_y(bottom)


def answer_turn(values):
    if len(values) == 2:
        mine, other = values
        mine = mine.astype(F32) + flip(other).astype(F32)
        return (lax.psum(mine, "mp", axis_index_groups=y_groups()),)
    top, bottom, other_top, other_bottom = values
    top = (top.astype(F32) + flip(other_top).astype(F32)).astype(BF16)
    bottom = (bottom.astype(F32) + other_bottom.astype(F32)).astype(BF16)
    return top, bottom, swap_y(top), swap_x(bottom)


def answer_end(values):
    if len(values) == 1:
        return values[0]
    top, bottom, other_top, other_bottom = values
    top = top.astype(F32) + other_top.astype(F32)
    bottom = bottom.astype(F32) + flip(other_bottom).astype(F32)
    return jnp.concatenate([top, bottom], axis=0)


def both_cores(values, core):
    return in_order(core == 0, values, swap_core(values), 0)


def local(
    passage_embeds,
    passage_lengths,
    slot_question,
    answer_states,
    w_enc_attn,
    w_enc_ff,
    w_cross_kv,
    w_dec_attn,
    w_dec_ff,
):
    dp_count, mp_count = lax.axis_size("dp"), lax.axis_size("mp")
    size_z, size_y = dp_count // 2, mp_count // 2
    x = lax.axis_index("dp") % 2
    core = lax.axis_index("mp") % 2
    y = lax.axis_index("mp") // 2
    features = passage_embeds.shape[1]
    shard_width = features // dp_count

    length = answer_states.shape[0]
    enc_ff_t = w_enc_ff.transpose(0, 2, 1)
    dec_ff_t = w_dec_ff.transpose(0, 2, 1)
    attn_z = pieces_z(w_enc_attn, 1)
    dec_attn_pair = (pick(w_dec_attn, x, 2, 2), swap_x(pick(w_dec_attn, 1 - x, 2, 2)))
    dec_ff_pair = (pick(dec_ff_t, x, 2, 1), swap_x(pick(dec_ff_t, 1 - x, 2, 1)))
    other_answers = swap_x(answer_states)

    row_count = passage_embeds.shape[0]
    rows = row_count // size_y
    sides = min(size_y - 1, 2)
    window = min(row_count, rows + sides * HALO)
    row_begin = y * rows
    window_begin = jnp.clip(row_begin - HALO, 0, row_count - window)
    lengths = passage_lengths[0]
    ends = jnp.cumsum(lengths)
    starts = ends - lengths
    positions = window_begin + jnp.arange(window, dtype=jnp.int32)
    segment = jnp.sum((positions[:, None] >= ends[None, :]).astype(jnp.int32), axis=1)
    query_block = math.gcd(rows, LANES)
    key_block = math.gcd(window, LANES)
    block_first = row_begin + jnp.arange(rows // query_block, dtype=jnp.int32) * query_block
    block_last = block_first + query_block - 1
    inside_first = jnp.max(
        jnp.where(starts[None, :] <= block_first[:, None], starts[None, :], 0), axis=1
    )
    inside_last = jnp.min(
        jnp.where(ends[None, :] > block_last[:, None], ends[None, :], row_count), axis=1
    )
    low = (inside_first - window_begin) // key_block
    high = (inside_last - window_begin + key_block - 1) // key_block
    seg_k = segment.reshape(window // key_block, 1, key_block)
    seg_q = jnp.broadcast_to(
        lax.dynamic_slice_in_dim(segment, row_begin - window_begin, rows, 0)[:, None],
        (rows, LANES),
    )

    embeds = own_first(
        lax.dynamic_slice_in_dim(passage_embeds, window_begin, window, 0), x, shard_width, z_place
    )
    normed = rms_normed(embeds)
    own_begin = row_begin - window_begin
    normed_q = lax.dynamic_slice_in_dim(normed, own_begin, rows, 0)

    attn_z, dec_attn_pair, dec_ff_pair, other_answers, enc_ff_t = meet(
        attn_z, dec_attn_pair, dec_ff_pair, other_answers, enc_ff_t
    )
    answers = in_order(x == 0, answer_states, other_answers, 0)
    answers = own_first(answers, x, shard_width, z_place)
    answer_normed = rms_normed(answers)
    attn_block = join(attn_z, 1)
    attn_near = spread_near(attn_block)
    gate_z = pieces_z(enc_ff_t[0:1], 2)
    rest_z = pieces_z(enc_ff_t[1:3], 2)

    attn_near, gate_z, dec_attn_pair = meet(attn_near, gate_z, dec_attn_pair)
    attn_far = spread_far(attn_near, 1)
    gate_block = join(gate_z, 2)
    gate_near = spread_near(gate_block)
    dec_attn_z = pieces_z(jnp.stack(dec_attn_pair, axis=1), 2)

    def attend(weights):
        return enc_attention(
            low,
            high,
            seg_q,
            seg_k,
            dot(normed_q, weights[0]).astype(BF16),
            dot(normed, weights[1]).astype(BF16),
            dot(normed, weights[2]).astype(BF16),
        )

    if size_y == 2:
        attn_weights = [join([attn_block, attn_near[0]], 1)]
        mixes = [attend(attn_weights[0])]
        attn_far, gate_near, rest_z, mixes, w_cross_kv = meet(
            attn_far, gate_near, rest_z, mixes, w_cross_kv
        )
    gate_far = spread_far(gate_near, 1)
    rest_block = join(rest_z, 2)
    rest_near = spread_near(rest_block)
    cross_z = pieces_z(w_cross_kv, 1)
    if size_y == 2:
        attn_weights.append(join([attn_near[1], *attn_far], 1))
        mixes.append(attend(attn_weights[1]))
    else:
        attn_weights = attn_pieces(attn_block, attn_near, attn_far)
        mixes = [attend(weights) for weights in attn_weights]
    partial = out_project(mixes, attn_weights, 3)
    own_embeds = lax.dynamic_slice_in_dim(embeds, own_begin + core * (rows // 2), rows // 2, 0)
    first_rows = (own_embeds.astype(F32) + core_rows_sum(partial, core)).astype(BF16)
    normed = both_cores(rms_normed(first_rows), core)

    gate_far, rest_near, dec_attn_z, cross_z, normed, dec_ff_pair = meet(
        gate_far, rest_near, dec_attn_z, cross_z, normed, dec_ff_pair
    )
    rest_far = spread_far(rest_near, 1)
    cross_block = join(cross_z, 1)
    cross_near = spread_near(cross_block)
    dec_ff_z = pieces_z(jnp.stack(dec_ff_pair, axis=1).reshape(-1, *dec_ff_pair[0].shape[1:]), 2)
    gate_ff = ff_piece(gate_block, gate_near, gate_far)
    own_rest = [(rest_block, 0, rest_block.shape[1]), (rest_near[0], 0, rest_block.shape[1])]
    hidden = ff(normed, [((0, gate_ff[0]), (0, own_rest))], [], False)
    dec_attn = join(dec_attn_z, 2).reshape(w_dec_attn.shape[0], features, -1)
    self_mix = self_attention(
        dot(answer_normed, dec_attn[0]).astype(BF16),
        dot(answer_normed, dec_attn[1]).astype(BF16),
        dot(answer_normed, dec_attn[2]).astype(BF16),
        2,
    )
    self_partial = dot_t(self_mix, dec_attn[3]).astype(BF16)

    rest_far, cross_near, hidden, self_partial = meet(rest_far, cross_near, hidden, self_partial)
    exchange = answer_start(self_partial, core, size_y)
    cross_far = spread_far(cross_near, 1)
    rest_ff = ff_piece(rest_block, rest_near, rest_far)
    chunks = [((0, g), (0, r), (1, r)) for g, r in zip(gate_ff[1:], rest_ff[1:])]
    if chunks:
        partial = ff(normed, chunks, [(hidden, (1, rest_ff[0]))], True)
    else:
        partial = ff(normed, [((0, gate_ff[0]), (0, own_rest), (1, own_rest))], [], True)

    cross_far, exchange, dec_ff_z, partial = meet(cross_far, exchange, dec_ff_z, partial)
    exchange = answer_turn(exchange)
    first_answer = (pick(answers, core, 2, 0).astype(F32) + answer_end(exchange)).astype(BF16)
    cross_q = dot(both_cores(rms_normed(first_answer), core), dec_attn[4]).astype(BF16)
    cross_q = join(pieces_z(cross_q, 0), 0)
    cross_q = in_order(x == 0, cross_q, swap_x(cross_q), 1)
    cross_q = gather_y(cross_q.reshape(dp_count, length, cross_q.shape[1]))
    second_rows = (first_rows.astype(F32) + core_rows_sum(partial, core)).astype(BF16)
    normed = both_cores(rms_normed(second_rows), core)
    cross_weights = attn_pieces(cross_block, cross_near, cross_far)
    dec_ff = join(dec_ff_z, 2)

    begin = jnp.clip(starts - row_begin, 0, rows)
    end = jnp.clip(ends - row_begin, 0, rows)
    questions = slot_question[0]
    questions = z_place(questions // 2) * 2 + questions % 2
    keys = [
        (dot(normed, kv[0]).astype(BF16), dot(normed, kv[1]).astype(BF16)) for kv in cross_weights
    ]
    cross_q, keys, dec_ff = meet(cross_q, keys, dec_ff)

    def answer_part(index):
        sums = cross_attention(begin, end, questions, cross_q[index], *keys[index])
        return by_column_x(sums, length)

    if size_y == 2:
        other = swap_y(answer_part(1))
        own = answer_part(0)
        summed = own.astype(F32) + other.astype(F32)
    else:
        packed = [answer_part(index) for index in range(size_y)]
        summed = packed[0].astype(F32) if size_y == 1 else scatter_y_sum(jnp.stack(packed))
    other = swap_x(lax.dynamic_index_in_dim(summed, 1 - x, 1, keepdims=False).astype(BF16))
    summed = lax.dynamic_index_in_dim(summed, x, 1, keepdims=False) + other.astype(F32)
    if few_z():
        own = summed[0]
        for step in range(1, size_z):
            own = own + swap_z(summed[step].astype(BF16), step).astype(F32)
        summed = own
    else:
        exchanged = lax.all_to_all(
            summed.astype(BF16), "dp", 0, 0, axis_index_groups=z_groups(), tiled=True
        )
        summed = jnp.sum(exchanged.astype(F32), axis=0)
    width = summed.shape[1]
    heads = width // HEAD_DIM
    num = summed[: 2 * length].reshape(2, length, heads, HEAD_DIM)
    tot = summed[2 * length : 2 * length + 2 * heads * length // width]
    tot = tot.reshape(2, heads, length).transpose(0, 2, 1)
    cross_mix = (num / tot[..., None]).astype(BF16).reshape(2 * length, width)
    exchange = answer_start(dot_t(cross_mix, dec_attn[5]).astype(BF16), core, size_y)
    second_sum = answer_end(answer_turn(exchange))
    second_answer = (first_answer.astype(F32) + second_sum).astype(BF16)
    answer_normed = both_cores(rms_normed(second_answer), core)
    halves = [(dec_ff, 0, dec_ff.shape[1], half) for half in range(2)]
    partial = ff(answer_normed, [((0, halves), (2, halves), (4, halves))], [], True)
    per_column = size_z // mp_count
    columns = per_column * shard_width

    def columns_of(values, indices):
        values = values.reshape(values.shape[0], 2, size_z, shard_width)
        blocks = [
            lax.dynamic_index_in_dim(values, z_place(index * per_column + i), 2, keepdims=False)
            for index in indices
            for i in range(per_column)
        ]
        return jnp.stack(blocks, axis=2).reshape(values.shape[0], 2, len(indices), columns)

    other = swap_core(columns_of(partial, [2 * i + 1 - core for i in range(size_y)]))
    mine = columns_of(partial, [2 * i + core for i in range(size_y)])
    mine = mine.astype(F32) + other.astype(F32)
    other = swap_x(pick(mine, 1 - x, 2, 0).astype(BF16)).astype(F32)
    mine = pick(mine, x, 2, 0) + jnp.stack([other[:, 1], other[:, 0]], axis=1)
    summed = scatter_y_sum(mine.astype(BF16).transpose(2, 0, 1, 3))
    residual = pick(both_cores(second_answer, core), x, 2, 0)
    residual = columns_of(residual, [lax.axis_index("mp")])[:, :, 0]
    result = (residual.astype(F32) + summed).astype(BF16)
    result = result.reshape(length, 2, per_column, 1, shard_width)
    return in_order(x == 0, result[:, 0], result[:, 1], 2).reshape(length, 2 * columns)


def solution(mesh):
    in_specs = (
        P("dp", None),
        P("dp", None),
        P("dp", None),
        P("dp", None),
        P(None, "dp", "mp"),
        P(None, "dp", "mp"),
        P(None, "dp", "mp"),
        P(None, "dp", "mp"),
        P(None, "dp", "mp"),
    )
    out_specs = P("dp", "mp")

    return jax.shard_map(local, mesh=mesh, in_specs=in_specs, out_specs=out_specs, check_vma=False)
```

```python
import functools
import math

import jax
import jax.numpy as jnp
from jax import lax
from jax.experimental import pallas as pl
from jax.experimental.pallas import tpu as pltpu
from jax.sharding import PartitionSpec as P


HEAD_DIM = 64
EPSILON = 1e-06
LANES = 128
HALO = 256
F32 = jnp.float32
BF16 = jnp.bfloat16
EXP2_FACTOR = 3.0 / math.sqrt(HEAD_DIM) * math.log2(math.e)


def rms_normed(values):
    values = values.astype(F32)
    factor = lax.rsqrt(jnp.mean(values * values, axis=-1, keepdims=True) + EPSILON)
    return (values * factor).astype(BF16)


def dot(left, right):
    return jnp.dot(left, right, preferred_element_type=F32)


def dot_t(left, right):
    return lax.dot_general(left, right, (((1,), (1,)), ((), ())), preferred_element_type=F32)


def swap_x(value):
    count = lax.axis_size("dp")
    return lax.ppermute(value, "dp", [(i, i ^ 1) for i in range(count)])


def swap_core(value):
    count = lax.axis_size("mp")
    return lax.ppermute(value, "mp", [(i, i ^ 1) for i in range(count)])


def z_groups():
    count = lax.axis_size("dp")
    return [[i + x for i in range(0, count, 2)] for x in range(2)]


def y_groups():
    count = lax.axis_size("mp")
    return [[i + c for i in range(0, count, 2)] for c in range(2)]


def gather_z(value, axis):
    return lax.all_gather(value, "dp", axis_index_groups=z_groups(), axis=axis, tiled=True)


def few_z():
    return lax.axis_size("dp") // 2 <= 4


def swap_z(value, step):
    count = lax.axis_size("dp")
    return lax.ppermute(value, "dp", [(i, i ^ (2 * step)) for i in range(count)])


def z_place(index):
    return index ^ (lax.axis_index("dp") // 2) if few_z() else index


def pieces_z(value, axis):
    if not few_z():
        return [gather_z(value, axis)]
    return [value] + [swap_z(value, step) for step in range(1, lax.axis_size("dp") // 2)]


def meet(*values):
    return lax.optimization_barrier(values)


def swap_y(value):
    return lax.ppermute(value, "mp", [(i, i ^ 2) for i in range(4)])


def gather_y(value):
    size_y = lax.axis_size("mp") // 2
    if size_y == 1:
        return [value]
    if size_y == 2:
        return [value, swap_y(value)]
    pieces = lax.all_gather(value, "mp", axis_index_groups=y_groups(), axis=0)
    return [pieces[i] for i in range(size_y)]


def scatter_y_sum(value):
    size_y = lax.axis_size("mp") // 2
    y = lax.axis_index("mp") // 2
    if size_y == 2:
        other = swap_y(lax.dynamic_index_in_dim(value, 1 - y, 0, keepdims=False))
        own = lax.dynamic_index_in_dim(value, y, 0, keepdims=False)
        return own.astype(F32) + other.astype(F32)
    summed = lax.psum_scatter(
        value, "mp", scatter_dimension=0, axis_index_groups=y_groups(), tiled=True
    )
    return summed[0].astype(F32)


def join_kernel(*refs, axis):
    *pieces, out, sems = refs
    begin, copies = 0, []
    for index, piece in enumerate(pieces):
        size = piece.shape[axis]
        where = (slice(None),) * axis + (pl.ds(begin, size),)
        copies.append(pltpu.make_async_copy(piece, out.at[where], sems.at[index]))
        copies[-1].start()
        begin += size
    for copy in copies:
        copy.wait()


def join(pieces, axis):
    if len(pieces) == 1:
        return pieces[0]
    shape = list(pieces[0].shape)
    shape[axis] = sum(piece.shape[axis] for piece in pieces)
    if axis == len(shape) - 1 and pieces[0].shape[axis] % LANES:
        return jnp.concatenate(pieces, axis=axis)
    return pl.pallas_call(
        functools.partial(join_kernel, axis=axis),
        out_shape=jax.ShapeDtypeStruct(tuple(shape), pieces[0].dtype),
        in_specs=[pl.BlockSpec(memory_space=pl.ANY)] * len(pieces),
        out_specs=pl.BlockSpec(memory_space=pltpu.VMEM),
        scratch_shapes=[pltpu.SemaphoreType.DMA((len(pieces),))],
        cost_estimate=pl.CostEstimate(
            flops=0, bytes_accessed=4 * math.prod(shape), transcendentals=0
        ),
        name="join",
    )(*pieces)


def pick(value, index, count, axis):
    width = value.shape[axis] // count
    return lax.dynamic_slice_in_dim(value, index * width, width, axis)


def in_order(first, own, other, axis):
    return jnp.concatenate(
        [jnp.where(first, own, other), jnp.where(first, other, own)], axis=axis
    )


def spread_near(block):
    return (swap_x(block), swap_y(block)) if lax.axis_size("mp") == 4 else (swap_x(block),)


def spread_far(near, axis):
    if len(near) == 1:
        return ()
    side, over = near
    cut = far_cut(side.shape[axis])
    first = lax.slice_in_dim(over, 0, cut, axis=axis)
    second = lax.slice_in_dim(side, cut, side.shape[axis], axis=axis)
    return (swap_x(first), swap_y(second))


def far_cut(size):
    return -(-(size // 2) // LANES) * LANES


def attn_pieces(block, near, far):
    own = [block, near[0]]
    if len(near) == 1:
        return [own] + [[piece] for piece in gather_y(join(own, 1))[1:]]
    return [own, [near[1], *far]]


def ff_piece(block, near, far):
    own = [(block, 0, block.shape[1]), (near[0], 0, block.shape[1])]
    if len(near) == 1:
        rest = [gather_y(half)[1:] for half in (block, near[0])]
        return [own] + [
            [(mine, 0, mine.shape[1]), (theirs, 0, theirs.shape[1])]
            for mine, theirs in zip(*rest)
        ]
    return [own, [(near[1], 0, near[1].shape[1]), (far[0], 0, near[1].shape[1])]]


def ff_kernel(*refs, chunks, done, last):
    refs, out_ref = refs[:-1], refs[-1]
    if chunks:
        half = refs[0].shape[1] // 2
        mine, theirs = refs[0][:, :half], refs[0][:, half:]

    def weight(place):
        index, lead, begin, count = place
        return refs[index][lead, begin : begin + count, :]

    sums = [None, None]

    def add(hidden, places):
        for k in range(2):
            term = dot(hidden, weight(places[k]))
            sums[k] = term if sums[k] is None else sums[k] + term

    for index, places in done:
        add(refs[index][...], places)
    for gate, up, *down in chunks:
        gated = dot_t(mine, weight(gate[0])) + dot_t(theirs, weight(gate[1]))
        linear = dot_t(mine, weight(up[0])) + dot_t(theirs, weight(up[1]))
        hidden = (jax.nn.gelu(gated, approximate=True) * linear).astype(BF16)
        if last:
            add(hidden, down[0])
        else:
            out_ref[...] = hidden
    if last:
        half = sums[0].shape[1]
        out_ref[:, :half] = sums[0].astype(BF16)
        out_ref[:, half:] = sums[1].astype(BF16)


def ff(h, chunks, done, last):
    rows = h.shape[0]
    block = math.gcd(rows, 384)
    operands, specs, seen = [], [], {}
    if chunks:
        operands.append(h)
        specs.append(pl.BlockSpec((block, h.shape[1]), lambda i: (i, 0)))

    def place(lead, entry):
        array, begin, count, *more = entry
        lead += sum(more)
        if id(array) not in seen:
            seen[id(array)] = len(operands)
            operands.append(array)
            specs.append(pl.BlockSpec(array.shape, lambda i: (0, 0, 0)))
        return seen[id(array)], lead, begin, count

    def places(lead, entries):
        return tuple(place(lead, entry) for entry in entries)

    before = []
    for hidden, (lead, entries) in done:
        operands.append(hidden)
        specs.append(pl.BlockSpec((block, hidden.shape[1]), lambda i: (i, 0)))
        index = len(operands) - 1
        before.append((index, places(lead, entries)))
    plan = [tuple(places(lead, entries) for lead, entries in chunk) for chunk in chunks]
    width = h.shape[1] if last else chunks[0][0][1][0][2]
    flops = 2 * rows * h.shape[1] * sum(
        [(3 if last else 2) * c[0][1][0][2] for c in chunks] + [d[0].shape[1] for d in done]
    )
    return pl.pallas_call(
        functools.partial(ff_kernel, chunks=plan, done=before, last=last),
        out_shape=jax.ShapeDtypeStruct((rows, width), BF16),
        grid=(rows // block,),
        in_specs=specs,
        out_specs=pl.BlockSpec((block, width), lambda i: (i, 0)),
        compiler_params=pltpu.CompilerParams(vmem_limit_bytes=48 * 2**20),
        cost_estimate=pl.CostEstimate(
            flops=flops, bytes_accessed=2 * rows * (h.shape[1] + width), transcendentals=0
        ),
        name="ff",
    )(*operands)


def row_block(rows, most):
    return max(n for n in range(16, most + 1, 16) if rows % n == 0)


def resident(array):
    return pl.BlockSpec(array.shape, lambda i: (0,) * array.ndim)


def out_kernel(*refs, plan, index):
    *refs, out_ref = refs
    cuts = {0, out_ref.shape[1]}
    for _, parts in plan:
        begin = 0
        for part in parts:
            begin += refs[part].shape[1]
            cuts.add(begin)
    cuts = sorted(cuts)
    for low, high in zip(cuts, cuts[1:]):
        total = None
        for mix, parts in plan:
            begin = 0
            for part in parts:
                size = refs[part].shape[1]
                if begin <= low < begin + size:
                    term = dot_t(refs[mix][...], refs[part][index, low - begin : high - begin, :])
                    total = term if total is None else total + term
                begin += size
        out_ref[:, low:high] = total.astype(BF16)


def out_project(mixes, pieces, index):
    rows = mixes[0].shape[0]
    features = sum(part.shape[1] for part in pieces[0])
    block = math.gcd(rows, 384)
    operands, specs, plan = [], [], []
    for mix, parts in zip(mixes, pieces):
        plan.append((len(operands), range(len(operands) + 1, len(operands) + 1 + len(parts))))
        operands += [mix, *parts]
        specs.append(pl.BlockSpec((block, mix.shape[1]), lambda i: (i, 0)))
        specs += [resident(part) for part in parts]
    return pl.pallas_call(
        functools.partial(out_kernel, plan=plan, index=index),
        out_shape=jax.ShapeDtypeStruct((rows, features), BF16),
        grid=(rows // block,),
        in_specs=specs,
        out_specs=pl.BlockSpec((block, features), lambda i: (i, 0)),
        compiler_params=pltpu.CompilerParams(vmem_limit_bytes=32 * 2**20),
        cost_estimate=pl.CostEstimate(
            flops=2 * rows * features * sum(m.shape[1] for m in mixes),
            bytes_accessed=4 * rows * features,
            transcendentals=0,
        ),
        name="out_project",
    )(*operands)


def prepare_kernel(begin_ref, order_ref, x_ref, o_ref, raw_ref, *, width):
    rows, features = o_ref.shape
    chunk = 32

    def step(r, carry):
        begin = pl.multiple_of(r * chunk, chunk)
        blocks, total = [], 0.0
        for p in range(features // width):
            source = pl.multiple_of(order_ref[p] * width, width)
            block = x_ref[pl.ds(begin, chunk), pl.ds(source, width)]
            raw_ref[pl.ds(begin, chunk), p * width : (p + 1) * width] = block
            block = block.astype(F32)
            blocks.append(block)
            total = total + block * block
        mean = jnp.sum(total, axis=1, keepdims=True) / features
        factor = lax.rsqrt(mean + EPSILON)
        for p, block in enumerate(blocks):
            o_ref[pl.ds(begin, chunk), p * width : (p + 1) * width] = (block * factor).astype(BF16)
        return carry

    lax.fori_loop(0, rows // chunk, step, 0, unroll=2)


def prepare(values, begin, rows, order, width):
    features = values.shape[1]
    block = LANES
    spec = pl.BlockSpec((block, features), lambda i, first, order: (i, 0))
    return pl.pallas_call(
        functools.partial(prepare_kernel, width=width),
        out_shape=[jax.ShapeDtypeStruct((rows, features), BF16)] * 2,
        grid_spec=pltpu.PrefetchScalarGridSpec(
            num_scalar_prefetch=2,
            grid=(rows // block,),
            in_specs=[
                pl.BlockSpec((block, features), lambda i, first, order: (first[0] + i, 0))
            ],
            out_specs=[spec, spec],
        ),
        cost_estimate=pl.CostEstimate(
            flops=4 * rows * features, bytes_accessed=6 * rows * features, transcendentals=0
        ),
        name="prepare",
    )((begin // block).reshape(1), order, values)


def own_first(values, x, width, place):
    size_z = values.shape[1] // (2 * width)
    blocks = [
        lax.dynamic_slice_in_dim(values, (2 * place(z) + index) * width, width, 1)
        for index in (x, 1 - x)
        for z in range(size_z)
    ]
    return jnp.concatenate(blocks, axis=1)


def two_heads(q, k, v, allowed, low_half):
    zero, one = jnp.zeros_like(v), jnp.ones_like(v)
    keys = jnp.concatenate([jnp.where(low_half, k, zero), jnp.where(low_half, zero, k)], axis=0)
    vals = jnp.concatenate(
        [
            jnp.concatenate([jnp.where(low_half, v, zero), jnp.where(low_half, one, zero)], axis=1),
            jnp.concatenate([jnp.where(low_half, zero, v), jnp.where(low_half, zero, one)], axis=1),
        ],
        axis=0,
    )
    weights = jnp.exp2(dot_t(q, keys) * EXP2_FACTOR)
    count = k.shape[0]
    if count % LANES == 0:
        weights = jnp.where(jnp.concatenate([allowed, allowed], axis=1), weights, 0.0)
        return dot(weights.astype(BF16), vals)
    first = jnp.where(allowed, weights[:, :count], 0.0).astype(BF16)
    second = jnp.where(allowed, weights[:, count:], 0.0).astype(BF16)
    return dot(first, vals[:count]) + dot(second, vals[count:])


def enc_attention_kernel(
    low_ref, high_ref, first_ref, seg_q_ref, seg_k_ref, q_ref, k_ref, v_ref, o_ref, acc, *, rows
):
    width = q_ref.shape[1]
    first_row = first_ref[0]
    key_rows = seg_k_ref.shape[2]
    last = seg_k_ref.shape[0] - 1
    low_half = lax.broadcasted_iota(jnp.int32, (1, LANES), 1) < HEAD_DIM

    def block(i, carry):
        begin = pl.multiple_of(i * rows, rows)
        query_begin = pl.multiple_of(first_row + i * rows, math.gcd(rows, LANES))
        low, high = low_ref[i], high_ref[i]
        acc[...] = jnp.zeros_like(acc)

        def step(j, inner):
            for p in range(width // LANES):
                columns = slice(p * LANES, (p + 1) * LANES)
                total = None
                for u in range(2):
                    index = low + 2 * j + u
                    clipped = jnp.minimum(index, last)
                    offset = pl.multiple_of(clipped * key_rows, key_rows)
                    seg_k = jnp.where(index < high, seg_k_ref[clipped], -1)
                    allowed = seg_q_ref[pl.ds(begin, rows), :key_rows] == seg_k
                    part = two_heads(
                        q_ref[pl.ds(query_begin, rows), columns],
                        k_ref[pl.ds(offset, key_rows), columns],
                        v_ref[pl.ds(offset, key_rows), columns],
                        allowed,
                        low_half,
                    )
                    total = part if total is None else total + part
                acc[p] += total
            return inner

        lax.fori_loop(0, (high - low + 1) // 2, step, 0)
        for p in range(width // LANES):
            sums = acc[p]
            o_ref[pl.ds(begin, rows), p * LANES : (p + 1) * LANES] = (
                sums[:, :LANES] / sums[:, LANES:]
            ).astype(BF16)
        return carry

    lax.fori_loop(0, low_ref.shape[0], block, 0)


def project_into(h_ref, weights, mats, outs):
    rows = h_ref.shape[0]
    begin = pl.multiple_of(pl.program_id(0) * rows, rows)
    for mat, out in zip(mats, outs):
        total, column = None, 0
        for weight in weights:
            size = weight.shape[1]
            term = dot(h_ref[:, column : column + size], weight[mat])
            total = term if total is None else total + term
            column += size
        out[pl.ds(begin, rows), :] = total.astype(BF16)


def enc_block_kernel(low_ref, high_ref, first_ref, seg_q_ref, seg_k_ref, h_ref, *refs, rows):
    *weights, o_ref, q, k, v, acc = refs
    project_into(h_ref, weights, (0, 1, 2), (q, k, v))

    @pl.when(pl.program_id(0) == pl.num_programs(0) - 1)
    def _():
        enc_attention_kernel(
            low_ref, high_ref, first_ref, seg_q_ref, seg_k_ref, q, k, v, o_ref, acc, rows=rows
        )


def enc_block(low, high, first_row, seg_q, seg_k, h, weights):
    rows, window, width = seg_q.shape[0], h.shape[0], weights[0].shape[2]
    query_rows = rows // low.shape[0]
    step = row_block(window, 400)
    smem = pl.BlockSpec(memory_space=pltpu.SMEM)
    return pl.pallas_call(
        functools.partial(enc_block_kernel, rows=query_rows),
        out_shape=jax.ShapeDtypeStruct((rows, width), BF16),
        grid=(window // step,),
        in_specs=[smem] * 3
        + [resident(seg_q), resident(seg_k)]
        + [pl.BlockSpec((step, h.shape[1]), lambda i: (i, 0))]
        + [resident(weight) for weight in weights],
        out_specs=pl.BlockSpec((rows, width), lambda i: (0, 0)),
        scratch_shapes=[pltpu.VMEM((window, width), BF16)] * 3
        + [pltpu.VMEM((width // LANES, query_rows, 2 * LANES), F32)],
        compiler_params=pltpu.CompilerParams(vmem_limit_bytes=32 * 2**20),
        cost_estimate=pl.CostEstimate(
            flops=window * width * (6 * h.shape[1] + 3072),
            bytes_accessed=2 * h.size,
            transcendentals=0,
        ),
        name="enc_block",
    )(low, high, first_row.reshape(1), seg_q, seg_k, h, *weights)


def cross_block_kernel(begin_ref, end_ref, question_ref, x_ref, *refs, key_rows, count):
    queries, (h_ref, *weights, o_ref, k, v, acc) = refs[:count], refs[count:]
    project_into(h_ref, weights, (0, 1), (k, v))

    @pl.when(pl.program_id(0) == pl.num_programs(0) - 1)
    def _():
        cross_kernel(
            begin_ref, end_ref, question_ref, x_ref, queries, k, v, o_ref, acc, key_rows=key_rows
        )


def cross_kernel(
    begin_ref, end_ref, question_ref, x_ref, queries, k_ref, v_ref, o_ref, acc, *, key_rows
):
    questions, length = queries[0].shape[:2]
    pairs = k_ref.shape[1] // LANES
    own_x = x_ref[0]

    def pair_of(question, p):
        if len(queries) == 1:
            return queries[0][question, :, p * LANES : (p + 1) * LANES]
        own, other = (ref[question] for ref in queries)
        return jnp.where(own_x == p, own, other)

    last = k_ref.shape[0] // key_rows - 1
    acc[...] = jnp.zeros_like(acc)
    low_half = lax.broadcasted_iota(jnp.int32, (1, LANES), 1) < HEAD_DIM

    def passage(s, carry):
        begin, end, question = begin_ref[s], end_ref[s], question_ref[s]
        first = begin // key_rows

        def step(j, inner):
            for p in range(pairs):
                columns = slice(p * LANES, (p + 1) * LANES)
                total = None
                query = pair_of(question, p)
                for u in range(2):
                    index = first + 2 * j + u
                    offset = pl.multiple_of(jnp.minimum(index, last) * key_rows, key_rows)
                    position = index * key_rows + lax.broadcasted_iota(
                        jnp.int32, (1, key_rows), 1
                    )
                    allowed = (position >= begin) & (position < end)
                    part = two_heads(
                        query,
                        k_ref[pl.ds(offset, key_rows), columns],
                        v_ref[pl.ds(offset, key_rows), columns],
                        allowed,
                        low_half,
                    )
                    total = part if total is None else total + part
                acc[question, p] += total
            return inner

        blocks = (end + key_rows - 1) // key_rows - first
        lax.fori_loop(0, jnp.where(end > begin, (blocks + 1) // 2, 0), step, 0)
        return carry

    lax.fori_loop(0, begin_ref.shape[0], passage, 0)
    eye = lax.broadcasted_iota(jnp.int32, (length, LANES), 0) == lax.broadcasted_iota(
        jnp.int32, (length, LANES), 1
    )
    extra = o_ref.shape[2] - 2 * length
    place = lax.broadcasted_iota(jnp.int32, (extra, LANES), 0)

    def finish(z, carry):
        for p in range(pairs):
            totals = jnp.zeros((extra, LANES), F32)
            for x in range(2):
                sums = acc[2 * z + x, p]
                o_ref[z, p, x * length : (x + 1) * length, :] = sums[:, :LANES].astype(BF16)
                total = sums[:, LANES:]
                turned = pltpu.roll(total, HEAD_DIM, 1)
                for h in range(2):
                    own = jnp.where(low_half, total, turned) if h == 0 else jnp.where(low_half, turned, total)
                    row = jnp.sum(jnp.where(eye, own, 0.0), axis=0, keepdims=True)
                    totals = jnp.where(place == 2 * x + h, row, totals)
            o_ref[z, p, 2 * length :, :] = totals.astype(BF16)
        return carry

    lax.fori_loop(0, questions // 2, finish, 0)


def cross_block(begin, end, question, x, queries, h, weights):
    questions, length = queries[0].shape[:2]
    rows, width = h.shape[0], weights[0].shape[2]
    key_rows = math.gcd(rows, LANES)
    pairs = width // LANES
    step = row_block(rows, 400)
    smem = pl.BlockSpec(memory_space=pltpu.SMEM)
    shape = (questions // 2, pairs, 2 * length + 16, LANES)
    return pl.pallas_call(
        functools.partial(cross_block_kernel, key_rows=key_rows, count=len(queries)),
        out_shape=jax.ShapeDtypeStruct(shape, BF16),
        grid=(rows // step,),
        in_specs=[smem] * 4
        + [resident(q) for q in queries]
        + [pl.BlockSpec((step, h.shape[1]), lambda i: (i, 0))]
        + [resident(weight) for weight in weights],
        out_specs=pl.BlockSpec(shape, lambda i: (0, 0, 0, 0)),
        scratch_shapes=[pltpu.VMEM((rows, width), BF16)] * 2
        + [pltpu.VMEM((questions, pairs, length, 2 * LANES), F32)],
        compiler_params=pltpu.CompilerParams(vmem_limit_bytes=40 * 2**20),
        cost_estimate=pl.CostEstimate(
            flops=rows * width * (4 * h.shape[1] + 2048), bytes_accessed=2 * h.size, transcendentals=0
        ),
        name="cross_block",
    )(begin, end, question, x.reshape(1), *queries, h, *weights)


def by_column_x(sums, length):
    size_z, pairs = sums.shape[:2]
    if pairs == 2:
        return sums
    num = sums[:, 0, : 2 * length].reshape(size_z, 2 * length, 2, HEAD_DIM).transpose(0, 2, 1, 3)
    tot = sums[:, 0, 2 * length : 2 * length + 4].reshape(size_z, 2, 2, length)
    tot = tot.transpose(0, 2, 1, 3).reshape(size_z, 2, -1, HEAD_DIM)
    return jnp.concatenate([num, tot], axis=2)


def self_kernel(x_ref, w_ref, o_ref, *, questions):
    rows, width = x_ref.shape[0], w_ref.shape[2]
    length = rows // questions
    q, k, v = (dot(x_ref[...], w_ref[i]).astype(BF16) for i in range(3))
    low_half = lax.broadcasted_iota(jnp.int32, (1, LANES), 1) < HEAD_DIM
    causal = lax.broadcasted_iota(jnp.int32, (length, length), 1) <= lax.broadcasted_iota(
        jnp.int32, (length, length), 0
    )
    for question in range(questions):
        own = slice(question * length, (question + 1) * length)
        total = None
        for p in range(width // LANES):
            columns = slice(p * LANES, (p + 1) * LANES)
            sums = two_heads(
                q[own, columns], k[own, columns], v[own, columns], causal, low_half
            )
            mixture = (sums[:, :LANES] / sums[:, LANES:]).astype(BF16)
            term = dot_t(mixture, w_ref[3, :, columns])
            total = term if total is None else total + term
        o_ref[own, :] = total.astype(BF16)


def self_block(x, weights, questions):
    if weights.shape[2] % LANES:
        q, k, v = (dot(x, weights[i]).astype(BF16) for i in range(3))
        return dot_t(self_attention(q, k, v, questions), weights[3]).astype(BF16)
    vmem = pl.BlockSpec(memory_space=pltpu.VMEM)
    return pl.pallas_call(
        functools.partial(self_kernel, questions=questions),
        out_shape=jax.ShapeDtypeStruct((x.shape[0], weights.shape[1]), BF16),
        in_specs=[vmem, vmem],
        out_specs=vmem,
        cost_estimate=pl.CostEstimate(
            flops=8 * x.size * weights.shape[2], bytes_accessed=2 * weights.size, transcendentals=0
        ),
        name="self_block",
    )(x, weights)


def self_attention(q, k, v, questions):
    rows, width = q.shape
    heads = width // HEAD_DIM
    length = rows // questions
    shape = (questions, length, heads, HEAD_DIM)
    q, k, v = q.reshape(shape), k.reshape(shape), v.reshape(shape)
    scores = jnp.einsum("oqhc,okhc->ohqk", q, k, preferred_element_type=F32)
    causal = jnp.arange(length)[None, :] <= jnp.arange(length)[:, None]
    weights = jnp.where(causal, jnp.exp(scores * (3.0 / math.sqrt(HEAD_DIM))), 0.0)
    totals = jnp.sum(weights, axis=3)
    mixture = jnp.einsum("ohqk,okhc->oqhc", weights.astype(BF16), v, preferred_element_type=F32)
    return (mixture / jnp.transpose(totals, (0, 2, 1))[..., None]).astype(BF16).reshape(rows, width)


def core_rows_sum(partial, core):
    other = swap_core(pick(partial, 1 - core, 2, 0).astype(BF16))
    return pick(partial, core, 2, 0).astype(F32) + other.astype(F32)


def flip(values):
    half = values.shape[1] // 2
    return jnp.concatenate([values[:, half:], values[:, :half]], axis=1)


def answer_start(partial, core, size_y):
    mine = core_rows_sum(partial, core).astype(BF16)
    if size_y != 2:
        return (mine, swap_x(mine))
    rows = mine.shape[0] // 2
    top, bottom = mine[:rows], mine[rows:]
    return top, bottom, swap_x(top), swap_y(bottom)


def answer_turn(values):
    if len(values) == 2:
        mine, other = values
        mine = mine.astype(F32) + flip(other).astype(F32)
        return (lax.psum(mine, "mp", axis_index_groups=y_groups()),)
    top, bottom, other_top, other_bottom = values
    top = (top.astype(F32) + flip(other_top).astype(F32)).astype(BF16)
    bottom = (bottom.astype(F32) + other_bottom.astype(F32)).astype(BF16)
    return top, bottom, swap_y(top), swap_x(bottom)


def answer_end(values):
    if len(values) == 1:
        return values[0]
    top, bottom, other_top, other_bottom = values
    top = top.astype(F32) + other_top.astype(F32)
    bottom = bottom.astype(F32) + flip(other_bottom).astype(F32)
    return jnp.concatenate([top, bottom], axis=0)


def both_cores(values, core):
    return in_order(core == 0, values, swap_core(values), 0)


def local(
    passage_embeds,
    passage_lengths,
    slot_question,
    answer_states,
    w_enc_attn,
    w_enc_ff,
    w_cross_kv,
    w_dec_attn,
    w_dec_ff,
):
    dp_count, mp_count = lax.axis_size("dp"), lax.axis_size("mp")
    size_z, size_y = dp_count // 2, mp_count // 2
    x = lax.axis_index("dp") % 2
    core = lax.axis_index("mp") % 2
    y = lax.axis_index("mp") // 2
    features = passage_embeds.shape[1]
    shard_width = features // dp_count

    length = answer_states.shape[0]
    enc_ff_t = w_enc_ff.transpose(0, 2, 1)
    dec_ff_t = w_dec_ff.transpose(0, 2, 1)
    attn_z = pieces_z(w_enc_attn, 1)
    dec_attn_pair = (pick(w_dec_attn, x, 2, 2), swap_x(pick(w_dec_attn, 1 - x, 2, 2)))
    dec_ff_pair = (pick(dec_ff_t, x, 2, 1), swap_x(pick(dec_ff_t, 1 - x, 2, 1)))
    other_answers = swap_x(answer_states)
    (
        attn_z,
        dec_attn_pair,
        dec_ff_pair,
        other_answers,
        enc_ff_t,
        passage_embeds,
        passage_lengths,
        answer_states,
    ) = meet(
        attn_z,
        dec_attn_pair,
        dec_ff_pair,
        other_answers,
        enc_ff_t,
        passage_embeds,
        passage_lengths,
        answer_states,
    )
    attn_block = join(attn_z, 1)
    attn_near = spread_near(attn_block)
    gate_z = pieces_z(enc_ff_t[0:1], 2)
    row_count = passage_embeds.shape[0]
    rows = row_count // size_y
    sides = min(size_y - 1, 2)
    window = min(row_count, rows + sides * HALO)
    row_begin = y * rows
    window_begin = jnp.clip(row_begin - HALO, 0, row_count - window)
    lengths = passage_lengths[0]
    ends = jnp.cumsum(lengths)
    starts = ends - lengths
    positions = window_begin + jnp.arange(window, dtype=jnp.int32)
    segment = jnp.sum((positions[:, None] >= ends[None, :]).astype(jnp.int32), axis=1)
    query_block = math.gcd(rows, 3 * LANES)
    key_block = math.gcd(window, LANES)
    block_first = row_begin + jnp.arange(rows // query_block, dtype=jnp.int32) * query_block
    block_last = block_first + query_block - 1
    inside_first = jnp.max(
        jnp.where(starts[None, :] <= block_first[:, None], starts[None, :], 0), axis=1
    )
    inside_last = jnp.min(
        jnp.where(ends[None, :] > block_last[:, None], ends[None, :], row_count), axis=1
    )
    low = (inside_first - window_begin) // key_block
    high = (inside_last - window_begin + key_block - 1) // key_block
    seg_k = segment.reshape(window // key_block, 1, key_block)
    seg_q = jnp.broadcast_to(
        lax.dynamic_slice_in_dim(segment, row_begin - window_begin, rows, 0)[:, None],
        (rows, LANES),
    )

    own_begin = row_begin - window_begin
    if shard_width % LANES == 0 and window % LANES == 0 and rows % LANES == 0:
        order = jnp.stack([2 * z_place(z) + i for i in (x, 1 - x) for z in range(size_z)])
        normed, embeds = prepare(passage_embeds, window_begin, window, order, shard_width)
    else:
        embeds = lax.dynamic_slice_in_dim(passage_embeds, window_begin, window, 0)
        embeds = own_first(embeds, x, shard_width, z_place)
        normed = rms_normed(embeds)
    answers = in_order(x == 0, answer_states, other_answers, 0)
    answers = own_first(answers, x, shard_width, z_place)
    answer_normed = rms_normed(answers)

    attn_near, gate_z, normed, enc_ff_t = meet(attn_near, gate_z, normed, enc_ff_t)
    attn_far = spread_far(attn_near, 1)
    gate_block = join(gate_z, 2)
    gate_near = spread_near(gate_block)
    rest_z = pieces_z(enc_ff_t[1:3], 2)

    def attend(parts):
        return enc_block(low, high, own_begin, seg_q, seg_k, normed, parts)

    if size_y == 2:
        mixes = [attend([attn_block, attn_near[0]])]
        attn_far, gate_near, rest_z, mixes, w_cross_kv, dec_attn_pair = meet(
            attn_far, gate_near, rest_z, mixes, w_cross_kv, dec_attn_pair
        )
    rest_block = join(rest_z, 2)
    rest_near = spread_near(rest_block)
    dec_attn_z = pieces_z(jnp.stack(dec_attn_pair, axis=1), 2)
    attn_weights = attn_pieces(attn_block, attn_near, attn_far)
    if size_y == 2:
        mixes.append(attend(attn_weights[1]))
    else:
        mixes = [attend(parts) for parts in attn_weights]
    partial = out_project(mixes, attn_weights, 3)
    own_embeds = lax.dynamic_slice_in_dim(embeds, own_begin + core * (rows // 2), rows // 2, 0)
    first_rows = (own_embeds.astype(F32) + core_rows_sum(partial, core)).astype(BF16)
    normed = both_cores(rms_normed(first_rows), core)

    rest_near, dec_attn_z, normed, w_cross_kv, dec_ff_pair = meet(
        rest_near, dec_attn_z, normed, w_cross_kv, dec_ff_pair
    )
    gate_far = (swap_x(gate_near[1]),) if size_y == 2 else ()
    rest_far = (swap_y(rest_near[0]),) if size_y == 2 else ()
    cross_z = pieces_z(w_cross_kv, 1)
    dec_ff_z = pieces_z(jnp.stack(dec_ff_pair, axis=1).reshape(-1, *dec_ff_pair[0].shape[1:]), 2)
    dec_attn = join(dec_attn_z, 2).reshape(w_dec_attn.shape[0], features, -1)
    self_partial = self_block(answer_normed, dec_attn, 2)
    exchange = answer_start(self_partial, core, size_y)
    gate_own = ff_piece(gate_block, gate_near, gate_near)[0]
    rest_own = ff_piece(rest_block, rest_near, rest_near)[0]
    hidden = [ff(normed, [((0, gate_own), (0, rest_own))], [], False)]

    gate_far, rest_far, hidden, exchange, cross_z = meet(
        gate_far, rest_far, hidden, exchange, cross_z
    )
    gate_ff = ff_piece(gate_block, gate_near, gate_far)
    exchange = answer_turn(exchange)
    cross_block_z = join(cross_z, 1)
    cross_near = spread_near(cross_block_z)
    rest_ff = ff_piece(rest_block, rest_near, rest_far)
    for gate, rest in zip(gate_ff[1:], rest_ff[1:]):
        hidden.append(ff(normed, [((0, gate), (0, rest))], [], False))

    hidden, exchange, cross_near = meet(hidden, exchange, cross_near)
    cross_far = spread_far(cross_near, 1)
    first_answer = (pick(answers, core, 2, 0).astype(F32) + answer_end(exchange)).astype(BF16)
    cross_q = dot(both_cores(rms_normed(first_answer), core), dec_attn[4]).astype(BF16)
    cross_q = pieces_z(cross_q, 0)
    partial = ff(normed, [], [(h, (1, rest)) for h, rest in zip(hidden, rest_ff)], True)

    cross_q, cross_far, partial = meet(cross_q, cross_far, partial)
    cross_q = join(cross_q, 0)
    shape = (dp_count, length, -1)
    if size_y == 2 and cross_q.shape[1] == LANES:
        side, over = swap_x(cross_q), swap_y(cross_q)
        half = cross_q.shape[0] // 2
        far = jnp.concatenate([swap_x(over[:half]), swap_y(side[half:])], axis=0)
        cross_q = [[q.reshape(shape) for q in pair] for pair in ((cross_q, side), (over, far))]
    else:
        cross_q = in_order(x == 0, cross_q, swap_x(cross_q), 1)
        cross_q = [[q] for q in gather_y(cross_q.reshape(shape))]
    second_rows = (first_rows.astype(F32) + core_rows_sum(partial, core)).astype(BF16)
    normed = both_cores(rms_normed(second_rows), core)
    cross_weights = attn_pieces(cross_block_z, cross_near, cross_far)

    begin = jnp.clip(starts - row_begin, 0, rows)
    end = jnp.clip(ends - row_begin, 0, rows)
    questions = slot_question[0]
    questions = z_place(questions // 2) * 2 + questions % 2
    cross_q, normed, dec_ff = meet(cross_q, normed, join(dec_ff_z, 2))

    def answer_part(index):
        sums = cross_block(
            begin, end, questions, x, cross_q[index], normed, cross_weights[index]
        )
        return by_column_x(sums, length)

    if size_y == 2:
        other = answer_part(1)
        other = swap_y(other)
        own = answer_part(0)
        summed = own.astype(F32) + other.astype(F32)
    else:
        packed = [answer_part(index) for index in range(size_y)]
        summed = packed[0].astype(F32) if size_y == 1 else scatter_y_sum(jnp.stack(packed))
    other = swap_x(lax.dynamic_index_in_dim(summed, 1 - x, 1, keepdims=False).astype(BF16))
    summed = lax.dynamic_index_in_dim(summed, x, 1, keepdims=False) + other.astype(F32)
    if few_z():
        own = summed[0]
        for step in range(1, size_z):
            own = own + swap_z(summed[step].astype(BF16), step).astype(F32)
        summed = own
    else:
        exchanged = lax.all_to_all(
            summed.astype(BF16), "dp", 0, 0, axis_index_groups=z_groups(), tiled=True
        )
        summed = jnp.sum(exchanged.astype(F32), axis=0)
    width = summed.shape[1]
    heads = width // HEAD_DIM
    num = summed[: 2 * length].reshape(2, length, heads, HEAD_DIM)
    tot = summed[2 * length : 2 * length + 2 * heads * length // width]
    tot = tot.reshape(2, heads, length).transpose(0, 2, 1)
    cross_mix = (num / tot[..., None]).astype(BF16).reshape(2 * length, width)
    exchange = answer_start(dot_t(cross_mix, dec_attn[5]).astype(BF16), core, size_y)
    second_sum = answer_end(answer_turn(exchange))
    second_answer = (first_answer.astype(F32) + second_sum).astype(BF16)
    answer_normed = both_cores(rms_normed(second_answer), core)
    halves = [(dec_ff, 0, dec_ff.shape[1], half) for half in range(2)]
    partial = ff(answer_normed, [((0, halves), (2, halves), (4, halves))], [], True)
    per_column = size_z // mp_count
    columns = per_column * shard_width

    def columns_of(values, indices):
        values = values.reshape(values.shape[0], 2, size_z, shard_width)
        blocks = [
            lax.dynamic_index_in_dim(values, z_place(index * per_column + i), 2, keepdims=False)
            for index in indices
            for i in range(per_column)
        ]
        return jnp.stack(blocks, axis=2).reshape(values.shape[0], 2, len(indices), columns)

    other = swap_core(columns_of(partial, [2 * i + 1 - core for i in range(size_y)]))
    mine = columns_of(partial, [2 * i + core for i in range(size_y)])
    mine = mine.astype(F32) + other.astype(F32)
    other = swap_x(pick(mine, 1 - x, 2, 0).astype(BF16)).astype(F32)
    mine = pick(mine, x, 2, 0) + jnp.stack([other[:, 1], other[:, 0]], axis=1)
    summed = scatter_y_sum(mine.astype(BF16).transpose(2, 0, 1, 3))
    residual = pick(both_cores(second_answer, core), x, 2, 0)
    residual = columns_of(residual, [lax.axis_index("mp")])[:, :, 0]
    result = (residual.astype(F32) + summed).astype(BF16)
    result = result.reshape(length, 2, per_column, 1, shard_width)
    return in_order(x == 0, result[:, 0], result[:, 1], 2).reshape(length, 2 * columns)


def solution(mesh):
    in_specs = (
        P("dp", None),
        P("dp", None),
        P("dp", None),
        P("dp", None),
        P(None, "dp", "mp"),
        P(None, "dp", "mp"),
        P(None, "dp", "mp"),
        P(None, "dp", "mp"),
        P(None, "dp", "mp"),
    )
    out_specs = P("dp", "mp")

    return jax.shard_map(local, mesh=mesh, in_specs=in_specs, out_specs=out_specs, check_vma=False)
```

```python
import functools
import math

import jax
import jax.numpy as jnp
from jax import lax
from jax.experimental import pallas as pl
from jax.experimental.pallas import tpu as pltpu
from jax.sharding import PartitionSpec as P


HEAD_DIM = 64
EPSILON = 1e-06
LANES = 128
HALO = 256
F32 = jnp.float32
BF16 = jnp.bfloat16
EXP2_FACTOR = 3.0 / math.sqrt(HEAD_DIM) * math.log2(math.e)


def rms_normed(values):
    values = values.astype(F32)
    factor = lax.rsqrt(jnp.mean(values * values, axis=-1, keepdims=True) + EPSILON)
    return (values * factor).astype(BF16)


def dot(left, right):
    return jnp.dot(left, right, preferred_element_type=F32)


def dot_t(left, right):
    return lax.dot_general(left, right, (((1,), (1,)), ((), ())), preferred_element_type=F32)


def swap_x(value):
    count = lax.axis_size("dp")
    return lax.ppermute(value, "dp", [(i, i ^ 1) for i in range(count)])


def swap_core(value):
    count = lax.axis_size("mp")
    return lax.ppermute(value, "mp", [(i, i ^ 1) for i in range(count)])


def z_groups():
    count = lax.axis_size("dp")
    return [[i + x for i in range(0, count, 2)] for x in range(2)]


def y_groups():
    count = lax.axis_size("mp")
    return [[i + c for i in range(0, count, 2)] for c in range(2)]


def gather_z(value, axis):
    return lax.all_gather(value, "dp", axis_index_groups=z_groups(), axis=axis, tiled=True)


def few_z():
    return lax.axis_size("dp") // 2 <= 4


def swap_z(value, step):
    count = lax.axis_size("dp")
    return lax.ppermute(value, "dp", [(i, i ^ (2 * step)) for i in range(count)])


def z_place(index):
    return index ^ (lax.axis_index("dp") // 2) if few_z() else index


def pieces_z(value, axis):
    if not few_z():
        return [gather_z(value, axis)]
    return [value] + [swap_z(value, step) for step in range(1, lax.axis_size("dp") // 2)]


def meet(*values):
    return lax.optimization_barrier(values)


def swap_y(value):
    return lax.ppermute(value, "mp", [(i, i ^ 2) for i in range(4)])


def gather_y(value):
    size_y = lax.axis_size("mp") // 2
    if size_y == 1:
        return [value]
    if size_y == 2:
        return [value, swap_y(value)]
    pieces = lax.all_gather(value, "mp", axis_index_groups=y_groups(), axis=0)
    return [pieces[i] for i in range(size_y)]


def scatter_y_sum(value):
    size_y = lax.axis_size("mp") // 2
    y = lax.axis_index("mp") // 2
    if size_y == 2:
        other = swap_y(lax.dynamic_index_in_dim(value, 1 - y, 0, keepdims=False))
        own = lax.dynamic_index_in_dim(value, y, 0, keepdims=False)
        return own.astype(F32) + other.astype(F32)
    summed = lax.psum_scatter(
        value, "mp", scatter_dimension=0, axis_index_groups=y_groups(), tiled=True
    )
    return summed[0].astype(F32)


def join_kernel(*refs, axis):
    *pieces, out, sems = refs
    begin, copies = 0, []
    for index, piece in enumerate(pieces):
        size = piece.shape[axis]
        where = (slice(None),) * axis + (pl.ds(begin, size),)
        copies.append(pltpu.make_async_copy(piece, out.at[where], sems.at[index]))
        copies[-1].start()
        begin += size
    for copy in copies:
        copy.wait()


def join(pieces, axis):
    if len(pieces) == 1:
        return pieces[0]
    shape = list(pieces[0].shape)
    shape[axis] = sum(piece.shape[axis] for piece in pieces)
    if axis == len(shape) - 1 and pieces[0].shape[axis] % LANES:
        return jnp.concatenate(pieces, axis=axis)
    return pl.pallas_call(
        functools.partial(join_kernel, axis=axis),
        out_shape=jax.ShapeDtypeStruct(tuple(shape), pieces[0].dtype),
        in_specs=[pl.BlockSpec(memory_space=pl.ANY)] * len(pieces),
        out_specs=pl.BlockSpec(memory_space=pltpu.VMEM),
        scratch_shapes=[pltpu.SemaphoreType.DMA((len(pieces),))],
        cost_estimate=pl.CostEstimate(
            flops=0, bytes_accessed=4 * math.prod(shape), transcendentals=0
        ),
        name="join",
    )(*pieces)


def pick(value, index, count, axis):
    width = value.shape[axis] // count
    return lax.dynamic_slice_in_dim(value, index * width, width, axis)


def in_order(first, own, other, axis):
    return jnp.concatenate(
        [jnp.where(first, own, other), jnp.where(first, other, own)], axis=axis
    )


def spread_near(block):
    return (swap_x(block), swap_y(block)) if lax.axis_size("mp") == 4 else (swap_x(block),)


def spread_far(near, axis):
    if len(near) == 1:
        return ()
    side, over = near
    cut = far_cut(side.shape[axis])
    first = lax.slice_in_dim(over, 0, cut, axis=axis)
    second = lax.slice_in_dim(side, cut, side.shape[axis], axis=axis)
    return (swap_x(first), swap_y(second))


def far_cut(size):
    return -(-(size // 2) // LANES) * LANES


def attn_pieces(block, near, far):
    own = [block, near[0]]
    if len(near) == 1:
        return [own] + [[piece] for piece in gather_y(join(own, 1))[1:]]
    return [own, [near[1], *far]]


def ff_piece(block, near, far):
    own = [(block, 0, block.shape[1]), (near[0], 0, block.shape[1])]
    if len(near) == 1:
        rest = [gather_y(half)[1:] for half in (block, near[0])]
        return [own] + [
            [(mine, 0, mine.shape[1]), (theirs, 0, theirs.shape[1])]
            for mine, theirs in zip(*rest)
        ]
    return [own, [(near[1], 0, near[1].shape[1]), (far[0], 0, near[1].shape[1])]]


def ff_kernel(*refs, chunks, done, last):
    refs, out_ref = refs[:-1], refs[-1]
    if chunks:
        half = refs[0].shape[1] // 2
        mine, theirs = refs[0][:, :half], refs[0][:, half:]

    def weight(place):
        index, lead, begin, count = place
        return refs[index][lead, begin : begin + count, :]

    sums = [None, None]

    def add(hidden, places):
        for k in range(2):
            term = dot(hidden, weight(places[k]))
            sums[k] = term if sums[k] is None else sums[k] + term

    for index, places in done:
        add(refs[index][...], places)
    for gate, up, *down in chunks:
        gated = dot_t(mine, weight(gate[0])) + dot_t(theirs, weight(gate[1]))
        linear = dot_t(mine, weight(up[0])) + dot_t(theirs, weight(up[1]))
        hidden = (jax.nn.gelu(gated, approximate=True) * linear).astype(BF16)
        if last:
            add(hidden, down[0])
        else:
            out_ref[...] = hidden
    if last:
        half = sums[0].shape[1]
        out_ref[:, :half] = sums[0].astype(BF16)
        out_ref[:, half:] = sums[1].astype(BF16)


def ff(h, chunks, done, last):
    rows = h.shape[0]
    block = math.gcd(rows, 384)
    operands, specs, seen = [], [], {}
    if chunks:
        operands.append(h)
        specs.append(pl.BlockSpec((block, h.shape[1]), lambda i: (i, 0)))

    def place(lead, entry):
        array, begin, count, *more = entry
        lead += sum(more)
        if id(array) not in seen:
            seen[id(array)] = len(operands)
            operands.append(array)
            specs.append(pl.BlockSpec(array.shape, lambda i: (0, 0, 0)))
        return seen[id(array)], lead, begin, count

    def places(lead, entries):
        return tuple(place(lead, entry) for entry in entries)

    before = []
    for hidden, (lead, entries) in done:
        operands.append(hidden)
        specs.append(pl.BlockSpec((block, hidden.shape[1]), lambda i: (i, 0)))
        index = len(operands) - 1
        before.append((index, places(lead, entries)))
    plan = [tuple(places(lead, entries) for lead, entries in chunk) for chunk in chunks]
    width = h.shape[1] if last else chunks[0][0][1][0][2]
    flops = 2 * rows * h.shape[1] * sum(
        [(3 if last else 2) * c[0][1][0][2] for c in chunks] + [d[0].shape[1] for d in done]
    )
    return pl.pallas_call(
        functools.partial(ff_kernel, chunks=plan, done=before, last=last),
        out_shape=jax.ShapeDtypeStruct((rows, width), BF16),
        grid=(rows // block,),
        in_specs=specs,
        out_specs=pl.BlockSpec((block, width), lambda i: (i, 0)),
        compiler_params=pltpu.CompilerParams(vmem_limit_bytes=48 * 2**20),
        cost_estimate=pl.CostEstimate(
            flops=flops, bytes_accessed=2 * rows * (h.shape[1] + width), transcendentals=0
        ),
        name="ff",
    )(*operands)


def row_block(rows, most):
    return max(n for n in range(16, most + 1, 16) if rows % n == 0)


def resident(array):
    return pl.BlockSpec(array.shape, lambda i: (0,) * array.ndim)


def out_kernel(*refs, plan, index):
    *refs, out_ref = refs
    cuts = {0, out_ref.shape[1]}
    for _, parts in plan:
        begin = 0
        for part in parts:
            begin += refs[part].shape[1]
            cuts.add(begin)
    cuts = sorted(cuts)
    for low, high in zip(cuts, cuts[1:]):
        total = None
        for mix, parts in plan:
            begin = 0
            for part in parts:
                size = refs[part].shape[1]
                if begin <= low < begin + size:
                    term = dot_t(refs[mix][...], refs[part][index, low - begin : high - begin, :])
                    total = term if total is None else total + term
                begin += size
        out_ref[:, low:high] = total.astype(BF16)


def out_project(mixes, pieces, index):
    rows = mixes[0].shape[0]
    features = sum(part.shape[1] for part in pieces[0])
    block = math.gcd(rows, 384)
    operands, specs, plan = [], [], []
    for mix, parts in zip(mixes, pieces):
        plan.append((len(operands), range(len(operands) + 1, len(operands) + 1 + len(parts))))
        operands += [mix, *parts]
        specs.append(pl.BlockSpec((block, mix.shape[1]), lambda i: (i, 0)))
        specs += [resident(part) for part in parts]
    return pl.pallas_call(
        functools.partial(out_kernel, plan=plan, index=index),
        out_shape=jax.ShapeDtypeStruct((rows, features), BF16),
        grid=(rows // block,),
        in_specs=specs,
        out_specs=pl.BlockSpec((block, features), lambda i: (i, 0)),
        compiler_params=pltpu.CompilerParams(vmem_limit_bytes=32 * 2**20),
        cost_estimate=pl.CostEstimate(
            flops=2 * rows * features * sum(m.shape[1] for m in mixes),
            bytes_accessed=4 * rows * features,
            transcendentals=0,
        ),
        name="out_project",
    )(*operands)


def prepare_kernel(begin_ref, order_ref, x_ref, o_ref, raw_ref, *, width):
    rows, features = o_ref.shape
    chunk = 32

    def step(r, carry):
        begin = pl.multiple_of(r * chunk, chunk)
        blocks, total = [], 0.0
        for p in range(features // width):
            source = pl.multiple_of(order_ref[p] * width, width)
            block = x_ref[pl.ds(begin, chunk), pl.ds(source, width)]
            raw_ref[pl.ds(begin, chunk), p * width : (p + 1) * width] = block
            block = block.astype(F32)
            blocks.append(block)
            total = total + block * block
        mean = jnp.sum(total, axis=1, keepdims=True) / features
        factor = lax.rsqrt(mean + EPSILON)
        for p, block in enumerate(blocks):
            o_ref[pl.ds(begin, chunk), p * width : (p + 1) * width] = (block * factor).astype(BF16)
        return carry

    lax.fori_loop(0, rows // chunk, step, 0, unroll=2)


def prepare(values, begin, rows, order, width):
    features = values.shape[1]
    block = LANES
    spec = pl.BlockSpec((block, features), lambda i, first, order: (i, 0))
    return pl.pallas_call(
        functools.partial(prepare_kernel, width=width),
        out_shape=[jax.ShapeDtypeStruct((rows, features), BF16)] * 2,
        grid_spec=pltpu.PrefetchScalarGridSpec(
            num_scalar_prefetch=2,
            grid=(rows // block,),
            in_specs=[
                pl.BlockSpec((block, features), lambda i, first, order: (first[0] + i, 0))
            ],
            out_specs=[spec, spec],
        ),
        cost_estimate=pl.CostEstimate(
            flops=4 * rows * features, bytes_accessed=6 * rows * features, transcendentals=0
        ),
        name="prepare",
    )((begin // block).reshape(1), order, values)


def own_first(values, x, width, place):
    size_z = values.shape[1] // (2 * width)
    blocks = [
        lax.dynamic_slice_in_dim(values, (2 * place(z) + index) * width, width, 1)
        for index in (x, 1 - x)
        for z in range(size_z)
    ]
    return jnp.concatenate(blocks, axis=1)


def two_heads(q, k, v, allowed, low_half):
    zero, one = jnp.zeros_like(v), jnp.ones_like(v)
    keys = jnp.concatenate([jnp.where(low_half, k, zero), jnp.where(low_half, zero, k)], axis=0)
    vals = jnp.concatenate(
        [
            jnp.concatenate([jnp.where(low_half, v, zero), jnp.where(low_half, one, zero)], axis=1),
            jnp.concatenate([jnp.where(low_half, zero, v), jnp.where(low_half, zero, one)], axis=1),
        ],
        axis=0,
    )
    weights = jnp.exp2(dot_t(q, keys) * EXP2_FACTOR)
    count = k.shape[0]
    if count % LANES == 0:
        weights = jnp.where(jnp.concatenate([allowed, allowed], axis=1), weights, 0.0)
        return dot(weights.astype(BF16), vals)
    first = jnp.where(allowed, weights[:, :count], 0.0).astype(BF16)
    second = jnp.where(allowed, weights[:, count:], 0.0).astype(BF16)
    return dot(first, vals[:count]) + dot(second, vals[count:])


def enc_attention_kernel(
    low_ref, high_ref, first_ref, seg_q_ref, seg_k_ref, q_ref, k_ref, v_ref, o_ref, acc, *, rows
):
    width = q_ref.shape[1]
    first_row = first_ref[0]
    key_rows = seg_k_ref.shape[2]
    last = seg_k_ref.shape[0] - 1
    low_half = lax.broadcasted_iota(jnp.int32, (1, LANES), 1) < HEAD_DIM

    def block(i, carry):
        begin = pl.multiple_of(i * rows, rows)
        query_begin = pl.multiple_of(first_row + i * rows, math.gcd(rows, LANES))
        low, high = low_ref[i], high_ref[i]
        acc[...] = jnp.zeros_like(acc)

        def step(j, inner):
            for p in range(width // LANES):
                columns = slice(p * LANES, (p + 1) * LANES)
                total = None
                for u in range(2):
                    index = low + 2 * j + u
                    clipped = jnp.minimum(index, last)
                    offset = pl.multiple_of(clipped * key_rows, key_rows)
                    seg_k = jnp.where(index < high, seg_k_ref[clipped], -1)
                    allowed = seg_q_ref[pl.ds(begin, rows), :key_rows] == seg_k
                    part = two_heads(
                        q_ref[pl.ds(query_begin, rows), columns],
                        k_ref[pl.ds(offset, key_rows), columns],
                        v_ref[pl.ds(offset, key_rows), columns],
                        allowed,
                        low_half,
                    )
                    total = part if total is None else total + part
                acc[p] += total
            return inner

        lax.fori_loop(0, (high - low + 1) // 2, step, 0)
        for p in range(width // LANES):
            sums = acc[p]
            o_ref[pl.ds(begin, rows), p * LANES : (p + 1) * LANES] = (
                sums[:, :LANES] / sums[:, LANES:]
            ).astype(BF16)
        return carry

    lax.fori_loop(0, low_ref.shape[0], block, 0)


def project_into(h_ref, weights, mats, outs):
    rows = h_ref.shape[0]
    begin = pl.multiple_of(pl.program_id(0) * rows, rows)
    for mat, out in zip(mats, outs):
        total, column = None, 0
        for weight in weights:
            size = weight.shape[1]
            term = dot(h_ref[:, column : column + size], weight[mat])
            total = term if total is None else total + term
            column += size
        out[pl.ds(begin, rows), :] = total.astype(BF16)


def enc_block_kernel(low_ref, high_ref, first_ref, seg_q_ref, seg_k_ref, h_ref, *refs, rows):
    *weights, o_ref, q, k, v, acc = refs
    project_into(h_ref, weights, (0, 1, 2), (q, k, v))

    @pl.when(pl.program_id(0) == pl.num_programs(0) - 1)
    def _():
        enc_attention_kernel(
            low_ref, high_ref, first_ref, seg_q_ref, seg_k_ref, q, k, v, o_ref, acc, rows=rows
        )


def enc_block(low, high, first_row, seg_q, seg_k, h, weights):
    rows, window, width = seg_q.shape[0], h.shape[0], weights[0].shape[2]
    query_rows = rows // low.shape[0]
    step = row_block(window, 400)
    smem = pl.BlockSpec(memory_space=pltpu.SMEM)
    return pl.pallas_call(
        functools.partial(enc_block_kernel, rows=query_rows),
        out_shape=jax.ShapeDtypeStruct((rows, width), BF16),
        grid=(window // step,),
        in_specs=[smem] * 3
        + [resident(seg_q), resident(seg_k)]
        + [pl.BlockSpec((step, h.shape[1]), lambda i: (i, 0))]
        + [resident(weight) for weight in weights],
        out_specs=pl.BlockSpec((rows, width), lambda i: (0, 0)),
        scratch_shapes=[pltpu.VMEM((window, width), BF16)] * 3
        + [pltpu.VMEM((width // LANES, query_rows, 2 * LANES), F32)],
        compiler_params=pltpu.CompilerParams(vmem_limit_bytes=32 * 2**20),
        cost_estimate=pl.CostEstimate(
            flops=window * width * (6 * h.shape[1] + 3072),
            bytes_accessed=2 * h.size,
            transcendentals=0,
        ),
        name="enc_block",
    )(low, high, first_row.reshape(1), seg_q, seg_k, h, *weights)


def cross_block_kernel(
    active_ref, begin_ref, end_ref, question_ref, x_ref, *refs, key_rows, count
):
    queries, (h_ref, *weights, o_ref, k, v, acc) = refs[:count], refs[count:]
    project_into(h_ref, weights, (0, 1), (k, v))

    @pl.when(pl.program_id(0) == pl.num_programs(0) - 1)
    def _():
        cross_kernel(
            active_ref,
            begin_ref,
            end_ref,
            question_ref,
            x_ref,
            queries,
            k,
            v,
            o_ref,
            acc,
            key_rows=key_rows,
        )


def cross_kernel(
    active_ref, begin_ref, end_ref, question_ref, x_ref, queries, k_ref, v_ref, o_ref, acc, *, key_rows
):
    questions, length = queries[0].shape[:2]
    pairs = k_ref.shape[1] // LANES
    own_x = x_ref[0]

    def pair_of(question, p):
        if len(queries) == 1:
            return queries[0][question, :, p * LANES : (p + 1) * LANES]
        own, other = (ref[question] for ref in queries)
        return jnp.where(own_x == p, own, other)

    acc[...] = jnp.zeros_like(acc)
    low_half = lax.broadcasted_iota(jnp.int32, (1, LANES), 1) < HEAD_DIM
    rows = k_ref.shape[0]

    def bounds(s):
        begin = begin_ref[s]
        end = jnp.where(s < active_ref[1], end_ref[s], begin)
        return begin, end, question_ref[s], begin // 16 * 16

    def sums_of(place, j):
        begin, end, question, tile = place
        low = tile + j * key_rows
        offset = pl.multiple_of(jnp.minimum(low, rows - key_rows), 16)
        position = offset + lax.broadcasted_iota(jnp.int32, (1, key_rows), 1)
        allowed = (position >= jnp.maximum(begin, low)) & (position < end)
        return [
            two_heads(
                pair_of(question, p),
                k_ref[pl.ds(offset, key_rows), p * LANES : (p + 1) * LANES],
                v_ref[pl.ds(offset, key_rows), p * LANES : (p + 1) * LANES],
                allowed,
                low_half,
            )
            for p in range(pairs)
        ]

    def add(place, sums):
        for p in range(pairs):
            acc[place[2], p] += sums[p]

    def two_passages(i, carry):
        first = active_ref[0] + 2 * i
        places = [bounds(first), bounds(jnp.minimum(first + 1, begin_ref.shape[0] - 1))]
        places[1] = (
            places[1][0],
            jnp.where(first + 1 < active_ref[1], places[1][1], places[1][0]),
            *places[1][2:],
        )
        both = [sums_of(place, 0) for place in places]
        for place, sums in zip(places, both):
            add(place, sums)
        for place in places:

            def more(j, inner, place=place):
                add(place, sums_of(place, j))
                return inner

            lax.fori_loop(1, (place[1] - place[3] + key_rows - 1) // key_rows, more, 0)
        return carry

    lax.fori_loop(0, (active_ref[1] - active_ref[0] + 1) // 2, two_passages, 0)
    eye = lax.broadcasted_iota(jnp.int32, (length, LANES), 0) == lax.broadcasted_iota(
        jnp.int32, (length, LANES), 1
    )
    extra = o_ref.shape[2] - 2 * length
    place = lax.broadcasted_iota(jnp.int32, (extra, LANES), 0)

    def finish(z, carry):
        for p in range(pairs):
            totals = jnp.zeros((extra, LANES), F32)
            for x in range(2):
                sums = acc[2 * z + x, p]
                o_ref[z, p, x * length : (x + 1) * length, :] = sums[:, :LANES].astype(BF16)
                total = sums[:, LANES:]
                turned = pltpu.roll(total, HEAD_DIM, 1)
                for h in range(2):
                    own = jnp.where(low_half, total, turned) if h == 0 else jnp.where(low_half, turned, total)
                    row = jnp.sum(jnp.where(eye, own, 0.0), axis=0, keepdims=True)
                    totals = jnp.where(place == 2 * x + h, row, totals)
            o_ref[z, p, 2 * length :, :] = totals.astype(BF16)
        return carry

    lax.fori_loop(0, questions // 2, finish, 0)


def cross_block(begin, end, question, x, queries, h, weights):
    questions, length = queries[0].shape[:2]
    rows, width = h.shape[0], weights[0].shape[2]
    key_rows = min(rows, LANES)
    pairs = width // LANES
    step = row_block(rows, 400)
    place = jnp.arange(begin.shape[0], dtype=jnp.int32)
    here = end > begin
    active = jnp.stack(
        [
            jnp.min(jnp.where(here, place, begin.shape[0])),
            jnp.max(jnp.where(here, place + 1, 0)),
        ]
    )
    smem = pl.BlockSpec(memory_space=pltpu.SMEM)
    shape = (questions // 2, pairs, 2 * length + 16, LANES)
    return pl.pallas_call(
        functools.partial(cross_block_kernel, key_rows=key_rows, count=len(queries)),
        out_shape=jax.ShapeDtypeStruct(shape, BF16),
        grid=(rows // step,),
        in_specs=[smem] * 5
        + [resident(q) for q in queries]
        + [pl.BlockSpec((step, h.shape[1]), lambda i: (i, 0))]
        + [resident(weight) for weight in weights],
        out_specs=pl.BlockSpec(shape, lambda i: (0, 0, 0, 0)),
        scratch_shapes=[pltpu.VMEM((rows, width), BF16)] * 2
        + [pltpu.VMEM((questions, pairs, length, 2 * LANES), F32)],
        compiler_params=pltpu.CompilerParams(vmem_limit_bytes=40 * 2**20),
        cost_estimate=pl.CostEstimate(
            flops=rows * width * (4 * h.shape[1] + 2048), bytes_accessed=2 * h.size, transcendentals=0
        ),
        name="cross_block",
    )(active, begin, end, question, x.reshape(1), *queries, h, *weights)


def by_column_x(sums, length):
    size_z, pairs = sums.shape[:2]
    if pairs == 2:
        return sums
    num = sums[:, 0, : 2 * length].reshape(size_z, 2 * length, 2, HEAD_DIM).transpose(0, 2, 1, 3)
    tot = sums[:, 0, 2 * length : 2 * length + 4].reshape(size_z, 2, 2, length)
    tot = tot.transpose(0, 2, 1, 3).reshape(size_z, 2, -1, HEAD_DIM)
    return jnp.concatenate([num, tot], axis=2)


def self_kernel(x_ref, w_ref, o_ref, *, questions):
    rows, width = x_ref.shape[0], w_ref.shape[2]
    length = rows // questions
    q, k, v = (dot(x_ref[...], w_ref[i]).astype(BF16) for i in range(3))
    low_half = lax.broadcasted_iota(jnp.int32, (1, LANES), 1) < HEAD_DIM
    causal = lax.broadcasted_iota(jnp.int32, (length, length), 1) <= lax.broadcasted_iota(
        jnp.int32, (length, length), 0
    )
    for question in range(questions):
        own = slice(question * length, (question + 1) * length)
        total = None
        for p in range(width // LANES):
            columns = slice(p * LANES, (p + 1) * LANES)
            sums = two_heads(
                q[own, columns], k[own, columns], v[own, columns], causal, low_half
            )
            mixture = (sums[:, :LANES] / sums[:, LANES:]).astype(BF16)
            term = dot_t(mixture, w_ref[3, :, columns])
            total = term if total is None else total + term
        o_ref[own, :] = total.astype(BF16)


def self_block(x, weights, questions):
    if weights.shape[2] % LANES:
        q, k, v = (dot(x, weights[i]).astype(BF16) for i in range(3))
        return dot_t(self_attention(q, k, v, questions), weights[3]).astype(BF16)
    vmem = pl.BlockSpec(memory_space=pltpu.VMEM)
    return pl.pallas_call(
        functools.partial(self_kernel, questions=questions),
        out_shape=jax.ShapeDtypeStruct((x.shape[0], weights.shape[1]), BF16),
        in_specs=[vmem, vmem],
        out_specs=vmem,
        cost_estimate=pl.CostEstimate(
            flops=8 * x.size * weights.shape[2], bytes_accessed=2 * weights.size, transcendentals=0
        ),
        name="self_block",
    )(x, weights)


def self_attention(q, k, v, questions):
    rows, width = q.shape
    heads = width // HEAD_DIM
    length = rows // questions
    shape = (questions, length, heads, HEAD_DIM)
    q, k, v = q.reshape(shape), k.reshape(shape), v.reshape(shape)
    scores = jnp.einsum("oqhc,okhc->ohqk", q, k, preferred_element_type=F32)
    causal = jnp.arange(length)[None, :] <= jnp.arange(length)[:, None]
    weights = jnp.where(causal, jnp.exp(scores * (3.0 / math.sqrt(HEAD_DIM))), 0.0)
    totals = jnp.sum(weights, axis=3)
    mixture = jnp.einsum("ohqk,okhc->oqhc", weights.astype(BF16), v, preferred_element_type=F32)
    return (mixture / jnp.transpose(totals, (0, 2, 1))[..., None]).astype(BF16).reshape(rows, width)


def core_rows_sum(partial, core):
    other = swap_core(pick(partial, 1 - core, 2, 0).astype(BF16))
    return pick(partial, core, 2, 0).astype(F32) + other.astype(F32)


def flip(values):
    half = values.shape[1] // 2
    return jnp.concatenate([values[:, half:], values[:, :half]], axis=1)


def answer_start(partial, core, size_y):
    mine = core_rows_sum(partial, core).astype(BF16)
    if size_y != 2:
        return (mine, swap_x(mine))
    rows = mine.shape[0] // 2
    top, bottom = mine[:rows], mine[rows:]
    return top, bottom, swap_x(top), swap_y(bottom)


def answer_turn(values):
    if len(values) == 2:
        mine, other = values
        mine = mine.astype(F32) + flip(other).astype(F32)
        return (lax.psum(mine, "mp", axis_index_groups=y_groups()),)
    top, bottom, other_top, other_bottom = values
    top = (top.astype(F32) + flip(other_top).astype(F32)).astype(BF16)
    bottom = (bottom.astype(F32) + other_bottom.astype(F32)).astype(BF16)
    return top, bottom, swap_y(top), swap_x(bottom)


def answer_end(values):
    if len(values) == 1:
        return values[0]
    top, bottom, other_top, other_bottom = values
    top = top.astype(F32) + other_top.astype(F32)
    bottom = bottom.astype(F32) + flip(other_bottom).astype(F32)
    return jnp.concatenate([top, bottom], axis=0)


def both_cores(values, core):
    return in_order(core == 0, values, swap_core(values), 0)


def local(
    passage_embeds,
    passage_lengths,
    slot_question,
    answer_states,
    w_enc_attn,
    w_enc_ff,
    w_cross_kv,
    w_dec_attn,
    w_dec_ff,
):
    dp_count, mp_count = lax.axis_size("dp"), lax.axis_size("mp")
    size_z, size_y = dp_count // 2, mp_count // 2
    x = lax.axis_index("dp") % 2
    core = lax.axis_index("mp") % 2
    y = lax.axis_index("mp") // 2
    features = passage_embeds.shape[1]
    shard_width = features // dp_count

    length = answer_states.shape[0]
    enc_ff_t = w_enc_ff.transpose(0, 2, 1)
    dec_ff_t = w_dec_ff.transpose(0, 2, 1)
    attn_z = pieces_z(w_enc_attn, 1)
    dec_attn_pair = (pick(w_dec_attn, x, 2, 2), swap_x(pick(w_dec_attn, 1 - x, 2, 2)))
    dec_ff_pair = (pick(dec_ff_t, x, 2, 1), swap_x(pick(dec_ff_t, 1 - x, 2, 1)))
    other_answers = swap_x(answer_states)
    (
        attn_z,
        dec_attn_pair,
        dec_ff_pair,
        other_answers,
        enc_ff_t,
        passage_embeds,
        passage_lengths,
        answer_states,
    ) = meet(
        attn_z,
        dec_attn_pair,
        dec_ff_pair,
        other_answers,
        enc_ff_t,
        passage_embeds,
        passage_lengths,
        answer_states,
    )
    attn_block = join(attn_z, 1)
    attn_near = spread_near(attn_block)
    gate_z = pieces_z(enc_ff_t[0:1], 2)
    row_count = passage_embeds.shape[0]
    rows = row_count // size_y
    sides = min(size_y - 1, 2)
    window = min(row_count, rows + sides * HALO)
    row_begin = y * rows
    window_begin = jnp.clip(row_begin - HALO, 0, row_count - window)
    lengths = passage_lengths[0]
    ends = jnp.cumsum(lengths)
    starts = ends - lengths
    positions = window_begin + jnp.arange(window, dtype=jnp.int32)
    segment = jnp.sum((positions[:, None] >= ends[None, :]).astype(jnp.int32), axis=1)
    query_block = math.gcd(rows, 3 * LANES)
    key_block = math.gcd(window, LANES)
    block_first = row_begin + jnp.arange(rows // query_block, dtype=jnp.int32) * query_block
    block_last = block_first + query_block - 1
    inside_first = jnp.max(
        jnp.where(starts[None, :] <= block_first[:, None], starts[None, :], 0), axis=1
    )
    inside_last = jnp.min(
        jnp.where(ends[None, :] > block_last[:, None], ends[None, :], row_count), axis=1
    )
    low = (inside_first - window_begin) // key_block
    high = (inside_last - window_begin + key_block - 1) // key_block
    seg_k = segment.reshape(window // key_block, 1, key_block)
    seg_q = jnp.broadcast_to(
        lax.dynamic_slice_in_dim(segment, row_begin - window_begin, rows, 0)[:, None],
        (rows, LANES),
    )

    own_begin = row_begin - window_begin
    if shard_width % LANES == 0 and window % LANES == 0 and rows % LANES == 0:
        order = jnp.stack([2 * z_place(z) + i for i in (x, 1 - x) for z in range(size_z)])
        normed, embeds = prepare(passage_embeds, window_begin, window, order, shard_width)
    else:
        embeds = lax.dynamic_slice_in_dim(passage_embeds, window_begin, window, 0)
        embeds = own_first(embeds, x, shard_width, z_place)
        normed = rms_normed(embeds)
    answers = in_order(x == 0, answer_states, other_answers, 0)
    answers = own_first(answers, x, shard_width, z_place)
    answer_normed = rms_normed(answers)

    gate_z, rest_shard = meet(gate_z, enc_ff_t[1:3])
    rest_z = pieces_z(rest_shard, 2)

    attn_near, gate_z, normed = meet(attn_near, gate_z, normed)
    attn_far = spread_far(attn_near, 1)
    gate_block = join(gate_z, 2)
    gate_near = spread_near(gate_block)

    def attend(parts):
        return enc_block(low, high, own_begin, seg_q, seg_k, normed, parts)

    if size_y == 2:
        mixes = [attend([attn_block, attn_near[0]])]
        attn_far, gate_near, rest_z, mixes, w_cross_kv, dec_attn_pair = meet(
            attn_far, gate_near, rest_z, mixes, w_cross_kv, dec_attn_pair
        )
    rest_block = join(rest_z, 2)
    rest_near = spread_near(rest_block)
    dec_attn_z = pieces_z(jnp.stack(dec_attn_pair, axis=1), 2)
    attn_weights = attn_pieces(attn_block, attn_near, attn_far)
    if size_y == 2:
        mixes.append(attend(attn_weights[1]))
    else:
        mixes = [attend(parts) for parts in attn_weights]
    partial = out_project(mixes, attn_weights, 3)
    own_embeds = lax.dynamic_slice_in_dim(embeds, own_begin + core * (rows // 2), rows // 2, 0)
    first_rows = (own_embeds.astype(F32) + core_rows_sum(partial, core)).astype(BF16)
    normed = both_cores(rms_normed(first_rows), core)

    rest_near, dec_attn_z, normed, w_cross_kv, dec_ff_pair = meet(
        rest_near, dec_attn_z, normed, w_cross_kv, dec_ff_pair
    )
    gate_far = (swap_x(gate_near[1]),) if size_y == 2 else ()
    rest_far = (swap_y(rest_near[0]),) if size_y == 2 else ()
    cross_z = pieces_z(w_cross_kv, 1)
    dec_ff_z = pieces_z(jnp.stack(dec_ff_pair, axis=1).reshape(-1, *dec_ff_pair[0].shape[1:]), 2)
    dec_attn = join(dec_attn_z, 2).reshape(w_dec_attn.shape[0], features, -1)
    self_partial = self_block(answer_normed, dec_attn, 2)
    exchange = answer_start(self_partial, core, size_y)
    gate_own = ff_piece(gate_block, gate_near, gate_near)[0]
    rest_own = ff_piece(rest_block, rest_near, rest_near)[0]
    hidden = [ff(normed, [((0, gate_own), (0, rest_own))], [], False)]

    gate_far, rest_far, hidden, exchange, cross_z = meet(
        gate_far, rest_far, hidden, exchange, cross_z
    )
    gate_ff = ff_piece(gate_block, gate_near, gate_far)
    exchange = answer_turn(exchange)
    cross_block_z = join(cross_z, 1)
    cross_near = spread_near(cross_block_z)
    rest_ff = ff_piece(rest_block, rest_near, rest_far)
    for gate, rest in zip(gate_ff[1:], rest_ff[1:]):
        hidden.append(ff(normed, [((0, gate), (0, rest))], [], False))

    hidden, exchange, cross_near = meet(hidden, exchange, cross_near)
    cross_far = spread_far(cross_near, 1)
    first_answer = (pick(answers, core, 2, 0).astype(F32) + answer_end(exchange)).astype(BF16)
    cross_q = dot(both_cores(rms_normed(first_answer), core), dec_attn[4]).astype(BF16)
    cross_q = pieces_z(cross_q, 0)
    partial = ff(normed, [], [(h, (1, rest)) for h, rest in zip(hidden, rest_ff)], True)

    cross_q, cross_far, partial = meet(cross_q, cross_far, partial)
    cross_q = join(cross_q, 0)
    shape = (dp_count, length, -1)
    if size_y == 2 and cross_q.shape[1] == LANES:
        side, over = swap_x(cross_q), swap_y(cross_q)
        half = cross_q.shape[0] // 2
        far = jnp.concatenate([swap_x(over[:half]), swap_y(side[half:])], axis=0)
        cross_q = [[q.reshape(shape) for q in pair] for pair in ((cross_q, side), (over, far))]
    else:
        cross_q = in_order(x == 0, cross_q, swap_x(cross_q), 1)
        cross_q = [[q] for q in gather_y(cross_q.reshape(shape))]
    second_rows = (first_rows.astype(F32) + core_rows_sum(partial, core)).astype(BF16)
    normed = both_cores(rms_normed(second_rows), core)
    cross_weights = attn_pieces(cross_block_z, cross_near, cross_far)

    begin = jnp.clip(starts - row_begin, 0, rows)
    end = jnp.clip(ends - row_begin, 0, rows)
    questions = slot_question[0]
    questions = z_place(questions // 2) * 2 + questions % 2
    cross_q, normed, dec_ff = meet(cross_q, normed, join(dec_ff_z, 2))

    def answer_part(index):
        sums = cross_block(
            begin, end, questions, x, cross_q[index], normed, cross_weights[index]
        )
        return by_column_x(sums, length)

    if size_y == 2:
        other = answer_part(1)
        other = swap_y(other)
        own = answer_part(0)
        summed = own.astype(F32) + other.astype(F32)
    else:
        packed = [answer_part(index) for index in range(size_y)]
        summed = packed[0].astype(F32) if size_y == 1 else scatter_y_sum(jnp.stack(packed))
    other = swap_x(lax.dynamic_index_in_dim(summed, 1 - x, 1, keepdims=False).astype(BF16))
    summed = lax.dynamic_index_in_dim(summed, x, 1, keepdims=False) + other.astype(F32)
    if few_z():
        own = summed[0]
        for step in range(1, size_z):
            own = own + swap_z(summed[step].astype(BF16), step).astype(F32)
        summed = own
    else:
        exchanged = lax.all_to_all(
            summed.astype(BF16), "dp", 0, 0, axis_index_groups=z_groups(), tiled=True
        )
        summed = jnp.sum(exchanged.astype(F32), axis=0)
    width = summed.shape[1]
    heads = width // HEAD_DIM
    num = summed[: 2 * length].reshape(2, length, heads, HEAD_DIM)
    tot = summed[2 * length : 2 * length + 2 * heads * length // width]
    tot = tot.reshape(2, heads, length).transpose(0, 2, 1)
    cross_mix = (num / tot[..., None]).astype(BF16).reshape(2 * length, width)
    exchange = answer_start(dot_t(cross_mix, dec_attn[5]).astype(BF16), core, size_y)
    second_sum = answer_end(answer_turn(exchange))
    second_answer = (first_answer.astype(F32) + second_sum).astype(BF16)
    answer_normed = both_cores(rms_normed(second_answer), core)
    halves = [(dec_ff, 0, dec_ff.shape[1], half) for half in range(2)]
    partial = ff(answer_normed, [((0, halves), (2, halves), (4, halves))], [], True)
    per_column = size_z // mp_count
    columns = per_column * shard_width

    def columns_of(values, indices):
        values = values.reshape(values.shape[0], 2, size_z, shard_width)
        blocks = [
            lax.dynamic_index_in_dim(values, z_place(index * per_column + i), 2, keepdims=False)
            for index in indices
            for i in range(per_column)
        ]
        return jnp.stack(blocks, axis=2).reshape(values.shape[0], 2, len(indices), columns)

    other = swap_core(columns_of(partial, [2 * i + 1 - core for i in range(size_y)]))
    mine = columns_of(partial, [2 * i + core for i in range(size_y)])
    mine = mine.astype(F32) + other.astype(F32)
    other = swap_x(pick(mine, 1 - x, 2, 0).astype(BF16)).astype(F32)
    mine = pick(mine, x, 2, 0) + jnp.stack([other[:, 1], other[:, 0]], axis=1)
    summed = scatter_y_sum(mine.astype(BF16).transpose(2, 0, 1, 3))
    residual = pick(both_cores(second_answer, core), x, 2, 0)
    residual = columns_of(residual, [lax.axis_index("mp")])[:, :, 0]
    result = (residual.astype(F32) + summed).astype(BF16)
    result = result.reshape(length, 2, per_column, 1, shard_width)
    return in_order(x == 0, result[:, 0], result[:, 1], 2).reshape(length, 2 * columns)


def solution(mesh):
    in_specs = (
        P("dp", None),
        P("dp", None),
        P("dp", None),
        P("dp", None),
        P(None, "dp", "mp"),
        P(None, "dp", "mp"),
        P(None, "dp", "mp"),
        P(None, "dp", "mp"),
        P(None, "dp", "mp"),
    )
    out_specs = P("dp", "mp")

    return jax.shard_map(local, mesh=mesh, in_specs=in_specs, out_specs=out_specs, check_vma=False)
```

```python
import functools
import math

import jax
import jax.numpy as jnp
from jax import lax
from jax.experimental import pallas as pl
from jax.experimental.pallas import tpu as pltpu
from jax.sharding import PartitionSpec as P


HEAD_DIM = 64
EPSILON = 1e-06
LANES = 128
HALO = 256
F32 = jnp.float32
BF16 = jnp.bfloat16
EXP2_FACTOR = 3.0 / math.sqrt(HEAD_DIM) * math.log2(math.e)


def rms_normed(values):
    values = values.astype(F32)
    factor = lax.rsqrt(jnp.mean(values * values, axis=-1, keepdims=True) + EPSILON)
    return (values * factor).astype(BF16)


def dot(left, right):
    return jnp.dot(left, right, preferred_element_type=F32)


def dot_t(left, right):
    return lax.dot_general(left, right, (((1,), (1,)), ((), ())), preferred_element_type=F32)


def swap_x(value):
    count = lax.axis_size("dp")
    return lax.ppermute(value, "dp", [(i, i ^ 1) for i in range(count)])


def swap_core(value):
    count = lax.axis_size("mp")
    return lax.ppermute(value, "mp", [(i, i ^ 1) for i in range(count)])


def z_groups():
    count = lax.axis_size("dp")
    return [[i + x for i in range(0, count, 2)] for x in range(2)]


def y_groups():
    count = lax.axis_size("mp")
    return [[i + c for i in range(0, count, 2)] for c in range(2)]


def gather_z(value, axis):
    return lax.all_gather(value, "dp", axis_index_groups=z_groups(), axis=axis, tiled=True)


def few_z():
    return lax.axis_size("dp") // 2 <= 4


def swap_z(value, step):
    count = lax.axis_size("dp")
    return lax.ppermute(value, "dp", [(i, i ^ (2 * step)) for i in range(count)])


def z_place(index):
    return index ^ (lax.axis_index("dp") // 2) if few_z() else index


def pieces_z(value, axis):
    if not few_z():
        return [gather_z(value, axis)]
    return [value] + [swap_z(value, step) for step in range(1, lax.axis_size("dp") // 2)]


def meet(*values):
    return lax.optimization_barrier(values)


def swap_y(value):
    return lax.ppermute(value, "mp", [(i, i ^ 2) for i in range(4)])


def gather_y(value):
    size_y = lax.axis_size("mp") // 2
    if size_y == 1:
        return [value]
    if size_y == 2:
        return [value, swap_y(value)]
    pieces = lax.all_gather(value, "mp", axis_index_groups=y_groups(), axis=0)
    return [pieces[i] for i in range(size_y)]


def scatter_y_sum(value):
    size_y = lax.axis_size("mp") // 2
    y = lax.axis_index("mp") // 2
    if size_y == 2:
        other = swap_y(lax.dynamic_index_in_dim(value, 1 - y, 0, keepdims=False))
        own = lax.dynamic_index_in_dim(value, y, 0, keepdims=False)
        return own.astype(F32) + other.astype(F32)
    summed = lax.psum_scatter(
        value, "mp", scatter_dimension=0, axis_index_groups=y_groups(), tiled=True
    )
    return summed[0].astype(F32)


def join_kernel(*refs, axis):
    *pieces, out, sems = refs
    begin, copies = 0, []
    for index, piece in enumerate(pieces):
        size = piece.shape[axis]
        where = (slice(None),) * axis + (pl.ds(begin, size),)
        copies.append(pltpu.make_async_copy(piece, out.at[where], sems.at[index]))
        copies[-1].start()
        begin += size
    for copy in copies:
        copy.wait()


def join(pieces, axis):
    if len(pieces) == 1:
        return pieces[0]
    shape = list(pieces[0].shape)
    shape[axis] = sum(piece.shape[axis] for piece in pieces)
    if axis == len(shape) - 1 and pieces[0].shape[axis] % LANES:
        return jnp.concatenate(pieces, axis=axis)
    return pl.pallas_call(
        functools.partial(join_kernel, axis=axis),
        out_shape=jax.ShapeDtypeStruct(tuple(shape), pieces[0].dtype),
        in_specs=[pl.BlockSpec(memory_space=pl.ANY)] * len(pieces),
        out_specs=pl.BlockSpec(memory_space=pltpu.VMEM),
        scratch_shapes=[pltpu.SemaphoreType.DMA((len(pieces),))],
        cost_estimate=pl.CostEstimate(
            flops=0, bytes_accessed=4 * math.prod(shape), transcendentals=0
        ),
        name="join",
    )(*pieces)


def pick(value, index, count, axis):
    width = value.shape[axis] // count
    return lax.dynamic_slice_in_dim(value, index * width, width, axis)


def in_order(first, own, other, axis):
    return jnp.concatenate(
        [jnp.where(first, own, other), jnp.where(first, other, own)], axis=axis
    )


def spread_near(block):
    return (swap_x(block), swap_y(block)) if lax.axis_size("mp") == 4 else (swap_x(block),)


def spread_far(near, axis):
    if len(near) == 1:
        return ()
    side, over = near
    cut = far_cut(side.shape[axis])
    first = lax.slice_in_dim(over, 0, cut, axis=axis)
    second = lax.slice_in_dim(side, cut, side.shape[axis], axis=axis)
    return (swap_x(first), swap_y(second))


def far_cut(size):
    return -(-(size // 2) // LANES) * LANES


def attn_pieces(block, near, far):
    own = [block, near[0]]
    if len(near) == 1:
        return [own] + [[piece] for piece in gather_y(join(own, 1))[1:]]
    return [own, [near[1], *far]]


def ff_piece(block, near, far):
    own = [(block, 0, block.shape[1]), (near[0], 0, block.shape[1])]
    if len(near) == 1:
        rest = [gather_y(half)[1:] for half in (block, near[0])]
        return [own] + [
            [(mine, 0, mine.shape[1]), (theirs, 0, theirs.shape[1])]
            for mine, theirs in zip(*rest)
        ]
    return [own, [(near[1], 0, near[1].shape[1]), (far[0], 0, near[1].shape[1])]]


def ff_kernel(*refs, chunks, done, last):
    refs, out_ref = refs[:-1], refs[-1]
    if chunks:
        half = refs[0].shape[1] // 2
        mine, theirs = refs[0][:, :half], refs[0][:, half:]

    def weight(place):
        index, lead, begin, count = place
        return refs[index][lead, begin : begin + count, :]

    sums = [None, None]

    def add(hidden, places):
        for k in range(2):
            term = dot(hidden, weight(places[k]))
            sums[k] = term if sums[k] is None else sums[k] + term

    for index, places in done:
        add(refs[index][...], places)
    for gate, up, *down in chunks:
        gated = dot_t(mine, weight(gate[0])) + dot_t(theirs, weight(gate[1]))
        linear = dot_t(mine, weight(up[0])) + dot_t(theirs, weight(up[1]))
        hidden = (jax.nn.gelu(gated, approximate=True) * linear).astype(BF16)
        if last:
            add(hidden, down[0])
        else:
            out_ref[...] = hidden
    if last:
        half = sums[0].shape[1]
        out_ref[:, :half] = sums[0].astype(BF16)
        out_ref[:, half:] = sums[1].astype(BF16)


def ff(h, chunks, done, last):
    rows = h.shape[0]
    block = math.gcd(rows, 384)
    operands, specs, seen = [], [], {}
    if chunks:
        operands.append(h)
        specs.append(pl.BlockSpec((block, h.shape[1]), lambda i: (i, 0)))

    def place(lead, entry):
        array, begin, count, *more = entry
        lead += sum(more)
        if id(array) not in seen:
            seen[id(array)] = len(operands)
            operands.append(array)
            specs.append(pl.BlockSpec(array.shape, lambda i: (0, 0, 0)))
        return seen[id(array)], lead, begin, count

    def places(lead, entries):
        return tuple(place(lead, entry) for entry in entries)

    before = []
    for hidden, (lead, entries) in done:
        operands.append(hidden)
        specs.append(pl.BlockSpec((block, hidden.shape[1]), lambda i: (i, 0)))
        index = len(operands) - 1
        before.append((index, places(lead, entries)))
    plan = [tuple(places(lead, entries) for lead, entries in chunk) for chunk in chunks]
    width = h.shape[1] if last else chunks[0][0][1][0][2]
    flops = 2 * rows * h.shape[1] * sum(
        [(3 if last else 2) * c[0][1][0][2] for c in chunks] + [d[0].shape[1] for d in done]
    )
    return pl.pallas_call(
        functools.partial(ff_kernel, chunks=plan, done=before, last=last),
        out_shape=jax.ShapeDtypeStruct((rows, width), BF16),
        grid=(rows // block,),
        in_specs=specs,
        out_specs=pl.BlockSpec((block, width), lambda i: (i, 0)),
        compiler_params=pltpu.CompilerParams(vmem_limit_bytes=48 * 2**20),
        cost_estimate=pl.CostEstimate(
            flops=flops, bytes_accessed=2 * rows * (h.shape[1] + width), transcendentals=0
        ),
        name="ff",
    )(*operands)


def row_block(rows, most):
    return max(n for n in range(16, most + 1, 16) if rows % n == 0)


def resident(array):
    return pl.BlockSpec(array.shape, lambda i: (0,) * array.ndim)


def out_kernel(*refs, plan, index):
    *refs, out_ref = refs
    cuts = {0, out_ref.shape[1]}
    for _, parts in plan:
        begin = 0
        for part in parts:
            begin += refs[part].shape[1]
            cuts.add(begin)
    cuts = sorted(cuts)
    for low, high in zip(cuts, cuts[1:]):
        total = None
        for mix, parts in plan:
            begin = 0
            for part in parts:
                size = refs[part].shape[1]
                if begin <= low < begin + size:
                    term = dot_t(refs[mix][...], refs[part][index, low - begin : high - begin, :])
                    total = term if total is None else total + term
                begin += size
        out_ref[:, low:high] = total.astype(BF16)


def out_project(mixes, pieces, index):
    rows = mixes[0].shape[0]
    features = sum(part.shape[1] for part in pieces[0])
    block = math.gcd(rows, 384)
    operands, specs, plan = [], [], []
    for mix, parts in zip(mixes, pieces):
        plan.append((len(operands), range(len(operands) + 1, len(operands) + 1 + len(parts))))
        operands += [mix, *parts]
        specs.append(pl.BlockSpec((block, mix.shape[1]), lambda i: (i, 0)))
        specs += [resident(part) for part in parts]
    return pl.pallas_call(
        functools.partial(out_kernel, plan=plan, index=index),
        out_shape=jax.ShapeDtypeStruct((rows, features), BF16),
        grid=(rows // block,),
        in_specs=specs,
        out_specs=pl.BlockSpec((block, features), lambda i: (i, 0)),
        compiler_params=pltpu.CompilerParams(vmem_limit_bytes=32 * 2**20),
        cost_estimate=pl.CostEstimate(
            flops=2 * rows * features * sum(m.shape[1] for m in mixes),
            bytes_accessed=4 * rows * features,
            transcendentals=0,
        ),
        name="out_project",
    )(*operands)


def prepare_kernel(begin_ref, order_ref, x_ref, o_ref, raw_ref, *, width):
    rows, features = o_ref.shape
    chunk = 32

    def step(r, carry):
        begin = pl.multiple_of(r * chunk, chunk)
        blocks, total = [], 0.0
        for p in range(features // width):
            source = pl.multiple_of(order_ref[p] * width, width)
            block = x_ref[pl.ds(begin, chunk), pl.ds(source, width)]
            raw_ref[pl.ds(begin, chunk), p * width : (p + 1) * width] = block
            block = block.astype(F32)
            blocks.append(block)
            total = total + block * block
        mean = jnp.sum(total, axis=1, keepdims=True) / features
        factor = lax.rsqrt(mean + EPSILON)
        for p, block in enumerate(blocks):
            o_ref[pl.ds(begin, chunk), p * width : (p + 1) * width] = (block * factor).astype(BF16)
        return carry

    lax.fori_loop(0, rows // chunk, step, 0, unroll=2)


def prepare(values, begin, rows, order, width):
    features = values.shape[1]
    block = LANES
    spec = pl.BlockSpec((block, features), lambda i, first, order: (i, 0))
    return pl.pallas_call(
        functools.partial(prepare_kernel, width=width),
        out_shape=[jax.ShapeDtypeStruct((rows, features), BF16)] * 2,
        grid_spec=pltpu.PrefetchScalarGridSpec(
            num_scalar_prefetch=2,
            grid=(rows // block,),
            in_specs=[
                pl.BlockSpec((block, features), lambda i, first, order: (first[0] + i, 0))
            ],
            out_specs=[spec, spec],
        ),
        cost_estimate=pl.CostEstimate(
            flops=4 * rows * features, bytes_accessed=6 * rows * features, transcendentals=0
        ),
        name="prepare",
    )((begin // block).reshape(1), order, values)


def own_first(values, x, width, place):
    size_z = values.shape[1] // (2 * width)
    blocks = [
        lax.dynamic_slice_in_dim(values, (2 * place(z) + index) * width, width, 1)
        for index in (x, 1 - x)
        for z in range(size_z)
    ]
    return jnp.concatenate(blocks, axis=1)


def two_heads(q, k, v, allowed, low_half):
    zero, one = jnp.zeros_like(v), jnp.ones_like(v)
    keys = jnp.concatenate([jnp.where(low_half, k, zero), jnp.where(low_half, zero, k)], axis=0)
    vals = jnp.concatenate(
        [
            jnp.concatenate([jnp.where(low_half, v, zero), jnp.where(low_half, one, zero)], axis=1),
            jnp.concatenate([jnp.where(low_half, zero, v), jnp.where(low_half, zero, one)], axis=1),
        ],
        axis=0,
    )
    weights = jnp.exp2(dot_t(q, keys) * EXP2_FACTOR)
    count = k.shape[0]
    if count % LANES == 0:
        weights = jnp.where(jnp.concatenate([allowed, allowed], axis=1), weights, 0.0)
        return dot(weights.astype(BF16), vals)
    first = jnp.where(allowed, weights[:, :count], 0.0).astype(BF16)
    second = jnp.where(allowed, weights[:, count:], 0.0).astype(BF16)
    return dot(first, vals[:count]) + dot(second, vals[count:])


def enc_attention_kernel(
    low_ref, high_ref, first_ref, seg_q_ref, seg_k_ref, q_ref, k_ref, v_ref, o_ref, acc, *, rows
):
    width = q_ref.shape[1]
    first_row = first_ref[0]
    key_rows = seg_k_ref.shape[2]
    last = seg_k_ref.shape[0] - 1
    low_half = lax.broadcasted_iota(jnp.int32, (1, LANES), 1) < HEAD_DIM

    def block(i, carry):
        begin = pl.multiple_of(i * rows, rows)
        query_begin = pl.multiple_of(first_row + i * rows, math.gcd(rows, LANES))
        low, high = low_ref[i], high_ref[i]
        acc[...] = jnp.zeros_like(acc)

        def step(j, inner):
            for p in range(width // LANES):
                columns = slice(p * LANES, (p + 1) * LANES)
                total = None
                for u in range(2):
                    index = low + 2 * j + u
                    clipped = jnp.minimum(index, last)
                    offset = pl.multiple_of(clipped * key_rows, key_rows)
                    seg_k = jnp.where(index < high, seg_k_ref[clipped], -1)
                    allowed = seg_q_ref[pl.ds(begin, rows), :key_rows] == seg_k
                    part = two_heads(
                        q_ref[pl.ds(query_begin, rows), columns],
                        k_ref[pl.ds(offset, key_rows), columns],
                        v_ref[pl.ds(offset, key_rows), columns],
                        allowed,
                        low_half,
                    )
                    total = part if total is None else total + part
                acc[p] += total
            return inner

        lax.fori_loop(0, (high - low + 1) // 2, step, 0)
        for p in range(width // LANES):
            sums = acc[p]
            o_ref[pl.ds(begin, rows), p * LANES : (p + 1) * LANES] = (
                sums[:, :LANES] / sums[:, LANES:]
            ).astype(BF16)
        return carry

    lax.fori_loop(0, low_ref.shape[0], block, 0)


def project_into(h_ref, weights, mats, outs):
    rows = h_ref.shape[0]
    begin = pl.multiple_of(pl.program_id(0) * rows, rows)
    for mat, out in zip(mats, outs):
        total, column = None, 0
        for weight in weights:
            size = weight.shape[1]
            term = dot(h_ref[:, column : column + size], weight[mat])
            total = term if total is None else total + term
            column += size
        out[pl.ds(begin, rows), :] = total.astype(BF16)


def enc_block_kernel(low_ref, high_ref, first_ref, seg_q_ref, seg_k_ref, h_ref, *refs, rows):
    *weights, o_ref, q, k, v, acc = refs
    project_into(h_ref, weights, (0, 1, 2), (q, k, v))

    @pl.when(pl.program_id(0) == pl.num_programs(0) - 1)
    def _():
        enc_attention_kernel(
            low_ref, high_ref, first_ref, seg_q_ref, seg_k_ref, q, k, v, o_ref, acc, rows=rows
        )


def enc_block(low, high, first_row, seg_q, seg_k, h, weights):
    rows, window, width = seg_q.shape[0], h.shape[0], weights[0].shape[2]
    query_rows = rows // low.shape[0]
    step = row_block(window, 400)
    smem = pl.BlockSpec(memory_space=pltpu.SMEM)
    return pl.pallas_call(
        functools.partial(enc_block_kernel, rows=query_rows),
        out_shape=jax.ShapeDtypeStruct((rows, width), BF16),
        grid=(window // step,),
        in_specs=[smem] * 3
        + [resident(seg_q), resident(seg_k)]
        + [pl.BlockSpec((step, h.shape[1]), lambda i: (i, 0))]
        + [resident(weight) for weight in weights],
        out_specs=pl.BlockSpec((rows, width), lambda i: (0, 0)),
        scratch_shapes=[pltpu.VMEM((window, width), BF16)] * 3
        + [pltpu.VMEM((width // LANES, query_rows, 2 * LANES), F32)],
        compiler_params=pltpu.CompilerParams(vmem_limit_bytes=32 * 2**20),
        cost_estimate=pl.CostEstimate(
            flops=window * width * (6 * h.shape[1] + 3072),
            bytes_accessed=2 * h.size,
            transcendentals=0,
        ),
        name="enc_block",
    )(low, high, first_row.reshape(1), seg_q, seg_k, h, *weights)


def cross_block_kernel(
    active_ref, begin_ref, end_ref, question_ref, x_ref, *refs, key_rows, count
):
    queries, (h_ref, *weights, o_ref, k, v, acc) = refs[:count], refs[count:]
    project_into(h_ref, weights, (0, 1), (k, v))

    @pl.when(pl.program_id(0) == pl.num_programs(0) - 1)
    def _():
        cross_kernel(
            active_ref,
            begin_ref,
            end_ref,
            question_ref,
            x_ref,
            queries,
            k,
            v,
            o_ref,
            acc,
            key_rows=key_rows,
        )


def cross_kernel(
    active_ref, begin_ref, end_ref, question_ref, x_ref, queries, k_ref, v_ref, o_ref, acc, *, key_rows
):
    questions, length = queries[0].shape[:2]
    pairs = k_ref.shape[1] // LANES
    own_x = x_ref[0]

    def pair_of(question, p):
        if len(queries) == 1:
            return queries[0][question, :, p * LANES : (p + 1) * LANES]
        own, other = (ref[question] for ref in queries)
        return jnp.where(own_x == p, own, other)

    acc[...] = jnp.zeros_like(acc)
    low_half = lax.broadcasted_iota(jnp.int32, (1, LANES), 1) < HEAD_DIM
    rows = k_ref.shape[0]

    def bounds(s):
        begin = begin_ref[s]
        end = jnp.where(s < active_ref[1], end_ref[s], begin)
        return begin, end, question_ref[s], begin // 16 * 16

    def sums_of(place, j):
        begin, end, question, tile = place
        low = tile + j * key_rows
        offset = pl.multiple_of(jnp.minimum(low, rows - key_rows), 16)
        position = offset + lax.broadcasted_iota(jnp.int32, (1, key_rows), 1)
        allowed = (position >= jnp.maximum(begin, low)) & (position < end)
        return [
            two_heads(
                pair_of(question, p),
                k_ref[pl.ds(offset, key_rows), p * LANES : (p + 1) * LANES],
                v_ref[pl.ds(offset, key_rows), p * LANES : (p + 1) * LANES],
                allowed,
                low_half,
            )
            for p in range(pairs)
        ]

    def add(place, sums):
        for p in range(pairs):
            acc[place[2], p] += sums[p]

    def two_passages(i, carry):
        first = active_ref[0] + 2 * i
        places = [bounds(first), bounds(jnp.minimum(first + 1, begin_ref.shape[0] - 1))]
        places[1] = (
            places[1][0],
            jnp.where(first + 1 < active_ref[1], places[1][1], places[1][0]),
            *places[1][2:],
        )
        both = [sums_of(place, 0) for place in places]
        for place, sums in zip(places, both):
            add(place, sums)
        for place in places:

            def more(j, inner, place=place):
                add(place, sums_of(place, j))
                return inner

            lax.fori_loop(1, (place[1] - place[3] + key_rows - 1) // key_rows, more, 0)
        return carry

    lax.fori_loop(0, (active_ref[1] - active_ref[0] + 1) // 2, two_passages, 0)
    eye = lax.broadcasted_iota(jnp.int32, (length, LANES), 0) == lax.broadcasted_iota(
        jnp.int32, (length, LANES), 1
    )
    extra = o_ref.shape[2] - 2 * length
    place = lax.broadcasted_iota(jnp.int32, (extra, LANES), 0)

    def finish(z, carry):
        for p in range(pairs):
            totals = jnp.zeros((extra, LANES), F32)
            for x in range(2):
                sums = acc[2 * z + x, p]
                o_ref[z, p, x * length : (x + 1) * length, :] = sums[:, :LANES].astype(BF16)
                total = sums[:, LANES:]
                turned = pltpu.roll(total, HEAD_DIM, 1)
                for h in range(2):
                    own = jnp.where(low_half, total, turned) if h == 0 else jnp.where(low_half, turned, total)
                    row = jnp.sum(jnp.where(eye, own, 0.0), axis=0, keepdims=True)
                    totals = jnp.where(place == 2 * x + h, row, totals)
            o_ref[z, p, 2 * length :, :] = totals.astype(BF16)
        return carry

    lax.fori_loop(0, questions // 2, finish, 0)


def cross_block(begin, end, question, x, queries, h, weights):
    questions, length = queries[0].shape[:2]
    rows, width = h.shape[0], weights[0].shape[2]
    key_rows = min(rows, LANES)
    pairs = width // LANES
    step = row_block(rows, 400)
    place = jnp.arange(begin.shape[0], dtype=jnp.int32)
    here = end > begin
    active = jnp.stack(
        [
            jnp.min(jnp.where(here, place, begin.shape[0])),
            jnp.max(jnp.where(here, place + 1, 0)),
        ]
    )
    smem = pl.BlockSpec(memory_space=pltpu.SMEM)
    shape = (questions // 2, pairs, 2 * length + 16, LANES)
    return pl.pallas_call(
        functools.partial(cross_block_kernel, key_rows=key_rows, count=len(queries)),
        out_shape=jax.ShapeDtypeStruct(shape, BF16),
        grid=(rows // step,),
        in_specs=[smem] * 5
        + [resident(q) for q in queries]
        + [pl.BlockSpec((step, h.shape[1]), lambda i: (i, 0))]
        + [resident(weight) for weight in weights],
        out_specs=pl.BlockSpec(shape, lambda i: (0, 0, 0, 0)),
        scratch_shapes=[pltpu.VMEM((rows, width), BF16)] * 2
        + [pltpu.VMEM((questions, pairs, length, 2 * LANES), F32)],
        compiler_params=pltpu.CompilerParams(vmem_limit_bytes=40 * 2**20),
        cost_estimate=pl.CostEstimate(
            flops=rows * width * (4 * h.shape[1] + 2048), bytes_accessed=2 * h.size, transcendentals=0
        ),
        name="cross_block",
    )(active, begin, end, question, x.reshape(1), *queries, h, *weights)


def by_column_x(sums, length):
    size_z, pairs = sums.shape[:2]
    if pairs == 2:
        return sums
    num = sums[:, 0, : 2 * length].reshape(size_z, 2 * length, 2, HEAD_DIM).transpose(0, 2, 1, 3)
    tot = sums[:, 0, 2 * length : 2 * length + 4].reshape(size_z, 2, 2, length)
    tot = tot.transpose(0, 2, 1, 3).reshape(size_z, 2, -1, HEAD_DIM)
    return jnp.concatenate([num, tot], axis=2)


def self_kernel(x_ref, w_ref, o_ref, *, questions):
    rows, width = x_ref.shape[0], w_ref.shape[2]
    length = rows // questions
    q, k, v = (dot(x_ref[...], w_ref[i]).astype(BF16) for i in range(3))
    low_half = lax.broadcasted_iota(jnp.int32, (1, LANES), 1) < HEAD_DIM
    causal = lax.broadcasted_iota(jnp.int32, (length, length), 1) <= lax.broadcasted_iota(
        jnp.int32, (length, length), 0
    )
    for question in range(questions):
        own = slice(question * length, (question + 1) * length)
        total = None
        for p in range(width // LANES):
            columns = slice(p * LANES, (p + 1) * LANES)
            sums = two_heads(
                q[own, columns], k[own, columns], v[own, columns], causal, low_half
            )
            mixture = (sums[:, :LANES] / sums[:, LANES:]).astype(BF16)
            term = dot_t(mixture, w_ref[3, :, columns])
            total = term if total is None else total + term
        o_ref[own, :] = total.astype(BF16)


def self_block(x, weights, questions):
    if weights.shape[2] % LANES:
        q, k, v = (dot(x, weights[i]).astype(BF16) for i in range(3))
        return dot_t(self_attention(q, k, v, questions), weights[3]).astype(BF16)
    vmem = pl.BlockSpec(memory_space=pltpu.VMEM)
    return pl.pallas_call(
        functools.partial(self_kernel, questions=questions),
        out_shape=jax.ShapeDtypeStruct((x.shape[0], weights.shape[1]), BF16),
        in_specs=[vmem, vmem],
        out_specs=vmem,
        cost_estimate=pl.CostEstimate(
            flops=8 * x.size * weights.shape[2], bytes_accessed=2 * weights.size, transcendentals=0
        ),
        name="self_block",
    )(x, weights)


def self_attention(q, k, v, questions):
    rows, width = q.shape
    heads = width // HEAD_DIM
    length = rows // questions
    shape = (questions, length, heads, HEAD_DIM)
    q, k, v = q.reshape(shape), k.reshape(shape), v.reshape(shape)
    scores = jnp.einsum("oqhc,okhc->ohqk", q, k, preferred_element_type=F32)
    causal = jnp.arange(length)[None, :] <= jnp.arange(length)[:, None]
    weights = jnp.where(causal, jnp.exp(scores * (3.0 / math.sqrt(HEAD_DIM))), 0.0)
    totals = jnp.sum(weights, axis=3)
    mixture = jnp.einsum("ohqk,okhc->oqhc", weights.astype(BF16), v, preferred_element_type=F32)
    return (mixture / jnp.transpose(totals, (0, 2, 1))[..., None]).astype(BF16).reshape(rows, width)


def core_rows_sum(partial, core):
    other = swap_core(pick(partial, 1 - core, 2, 0).astype(BF16))
    return pick(partial, core, 2, 0).astype(F32) + other.astype(F32)


def flip(values):
    half = values.shape[1] // 2
    return jnp.concatenate([values[:, half:], values[:, :half]], axis=1)


def answer_start(partial, core, size_y):
    mine = core_rows_sum(partial, core).astype(BF16)
    if size_y != 2:
        return (mine, swap_x(mine))
    rows = mine.shape[0] // 2
    top, bottom = mine[:rows], mine[rows:]
    return top, bottom, swap_x(top), swap_y(bottom)


def answer_turn(values):
    if len(values) == 2:
        mine, other = values
        mine = mine.astype(F32) + flip(other).astype(F32)
        return (lax.psum(mine, "mp", axis_index_groups=y_groups()),)
    top, bottom, other_top, other_bottom = values
    top = (top.astype(F32) + flip(other_top).astype(F32)).astype(BF16)
    bottom = (bottom.astype(F32) + other_bottom.astype(F32)).astype(BF16)
    return top, bottom, swap_y(top), swap_x(bottom)


def answer_end(values):
    if len(values) == 1:
        return values[0]
    top, bottom, other_top, other_bottom = values
    top = top.astype(F32) + other_top.astype(F32)
    bottom = bottom.astype(F32) + flip(other_bottom).astype(F32)
    return jnp.concatenate([top, bottom], axis=0)


def both_cores(values, core):
    return in_order(core == 0, values, swap_core(values), 0)


def local(
    passage_embeds,
    passage_lengths,
    slot_question,
    answer_states,
    w_enc_attn,
    w_enc_ff,
    w_cross_kv,
    w_dec_attn,
    w_dec_ff,
):
    dp_count, mp_count = lax.axis_size("dp"), lax.axis_size("mp")
    size_z, size_y = dp_count // 2, mp_count // 2
    x = lax.axis_index("dp") % 2
    core = lax.axis_index("mp") % 2
    y = lax.axis_index("mp") // 2
    features = passage_embeds.shape[1]
    shard_width = features // dp_count

    length = answer_states.shape[0]
    enc_ff_t = w_enc_ff.transpose(0, 2, 1)
    dec_ff_t = w_dec_ff.transpose(0, 2, 1)
    attn_z = pieces_z(w_enc_attn, 1)
    dec_attn_pair = (pick(w_dec_attn, x, 2, 2), swap_x(pick(w_dec_attn, 1 - x, 2, 2)))
    dec_ff_pair = (pick(dec_ff_t, x, 2, 1), swap_x(pick(dec_ff_t, 1 - x, 2, 1)))
    other_answers = swap_x(answer_states)
    (
        attn_z,
        dec_attn_pair,
        dec_ff_pair,
        other_answers,
        enc_ff_t,
        passage_embeds,
        passage_lengths,
        answer_states,
    ) = meet(
        attn_z,
        dec_attn_pair,
        dec_ff_pair,
        other_answers,
        enc_ff_t,
        passage_embeds,
        passage_lengths,
        answer_states,
    )
    attn_block = join(attn_z, 1)
    attn_near = spread_near(attn_block)
    gate_z = pieces_z(enc_ff_t[0:1], 2)
    row_count = passage_embeds.shape[0]
    rows = row_count // size_y
    sides = min(size_y - 1, 2)
    window = min(row_count, rows + sides * HALO)
    row_begin = y * rows
    window_begin = jnp.clip(row_begin - HALO, 0, row_count - window)
    lengths = passage_lengths[0]
    ends = jnp.cumsum(lengths)
    starts = ends - lengths
    positions = window_begin + jnp.arange(window, dtype=jnp.int32)
    segment = jnp.sum((positions[:, None] >= ends[None, :]).astype(jnp.int32), axis=1)
    query_block = math.gcd(rows, 3 * LANES)
    key_block = math.gcd(window, LANES)
    block_first = row_begin + jnp.arange(rows // query_block, dtype=jnp.int32) * query_block
    block_last = block_first + query_block - 1
    inside_first = jnp.max(
        jnp.where(starts[None, :] <= block_first[:, None], starts[None, :], 0), axis=1
    )
    inside_last = jnp.min(
        jnp.where(ends[None, :] > block_last[:, None], ends[None, :], row_count), axis=1
    )
    low = (inside_first - window_begin) // key_block
    high = (inside_last - window_begin + key_block - 1) // key_block
    seg_k = segment.reshape(window // key_block, 1, key_block)
    seg_q = jnp.broadcast_to(
        lax.dynamic_slice_in_dim(segment, row_begin - window_begin, rows, 0)[:, None],
        (rows, LANES),
    )

    own_begin = row_begin - window_begin
    if shard_width % LANES == 0 and window % LANES == 0 and rows % LANES == 0:
        order = jnp.stack([2 * z_place(z) + i for i in (x, 1 - x) for z in range(size_z)])
        normed, embeds = prepare(passage_embeds, window_begin, window, order, shard_width)
    else:
        embeds = lax.dynamic_slice_in_dim(passage_embeds, window_begin, window, 0)
        embeds = own_first(embeds, x, shard_width, z_place)
        normed = rms_normed(embeds)
    answers = in_order(x == 0, answer_states, other_answers, 0)
    answers = own_first(answers, x, shard_width, z_place)
    answer_normed = rms_normed(answers)

    gate_z, rest_shard = meet(gate_z, enc_ff_t[1:3])
    rest_z = pieces_z(rest_shard, 2)

    attn_near, gate_z, normed = meet(attn_near, gate_z, normed)
    attn_far = spread_far(attn_near, 1)
    gate_block = join(gate_z, 2)
    gate_near = spread_near(gate_block)

    def attend(parts):
        return enc_block(low, high, own_begin, seg_q, seg_k, normed, parts)

    if size_y == 2:
        mixes = [attend([attn_block, attn_near[0]])]
        attn_far, gate_near, rest_z, mixes, w_cross_kv, dec_attn_pair = meet(
            attn_far, gate_near, rest_z, mixes, w_cross_kv, dec_attn_pair
        )
    rest_block = join(rest_z, 2)
    rest_near = spread_near(rest_block)
    dec_attn_z = pieces_z(jnp.stack(dec_attn_pair, axis=1), 2)
    attn_weights = attn_pieces(attn_block, attn_near, attn_far)
    if size_y == 2:
        mixes.append(attend(attn_weights[1]))
    else:
        mixes = [attend(parts) for parts in attn_weights]
    partial = out_project(mixes, attn_weights, 3)
    own_embeds = lax.dynamic_slice_in_dim(embeds, own_begin + core * (rows // 2), rows // 2, 0)
    first_rows = (own_embeds.astype(F32) + core_rows_sum(partial, core)).astype(BF16)
    normed = both_cores(rms_normed(first_rows), core)

    rest_near, dec_attn_z, normed, w_cross_kv, dec_ff_pair = meet(
        rest_near, dec_attn_z, normed, w_cross_kv, dec_ff_pair
    )
    gate_far = (swap_x(gate_near[1]),) if size_y == 2 else ()
    rest_far = (swap_y(rest_near[0]),) if size_y == 2 else ()
    cross_z = pieces_z(w_cross_kv, 1)
    dec_ff_z = pieces_z(jnp.stack(dec_ff_pair, axis=1).reshape(-1, *dec_ff_pair[0].shape[1:]), 2)
    dec_attn = join(dec_attn_z, 2).reshape(w_dec_attn.shape[0], features, -1)
    self_partial = self_block(answer_normed, dec_attn, 2)
    exchange = answer_start(self_partial, core, size_y)
    gate_own = ff_piece(gate_block, gate_near, gate_near)[0]
    rest_own = ff_piece(rest_block, rest_near, rest_near)[0]
    hidden = [ff(normed, [((0, gate_own), (0, rest_own))], [], False)]

    gate_far, rest_far, hidden, exchange, cross_z = meet(
        gate_far, rest_far, hidden, exchange, cross_z
    )
    gate_ff = ff_piece(gate_block, gate_near, gate_far)
    exchange = answer_turn(exchange)
    cross_block_z = join(cross_z, 1)
    cross_near = spread_near(cross_block_z)
    rest_ff = ff_piece(rest_block, rest_near, rest_far)
    for gate, rest in zip(gate_ff[1:], rest_ff[1:]):
        hidden.append(ff(normed, [((0, gate), (0, rest))], [], False))

    hidden, exchange, cross_near = meet(hidden, exchange, cross_near)
    cross_far = spread_far(cross_near, 1)
    first_answer = (pick(answers, core, 2, 0).astype(F32) + answer_end(exchange)).astype(BF16)
    cross_q = dot(both_cores(rms_normed(first_answer), core), dec_attn[4]).astype(BF16)
    cross_q = pieces_z(cross_q, 0)
    partial = ff(normed, [], [(h, (1, rest)) for h, rest in zip(hidden, rest_ff)], True)

    cross_q, cross_far, partial = meet(cross_q, cross_far, partial)
    cross_q = join(cross_q, 0)
    shape = (dp_count, length, -1)
    if size_y == 2 and cross_q.shape[1] == LANES:
        side, over = swap_x(cross_q), swap_y(cross_q)
        half = cross_q.shape[0] // 2
        far = (swap_x(over[:half]), swap_y(side[half:]))
        far = jnp.concatenate(far, axis=0)
        cross_q = [[q.reshape(shape) for q in pair] for pair in ((cross_q, side), (over, far))]
    else:
        cross_q = in_order(x == 0, cross_q, swap_x(cross_q), 1)
        cross_q = [[q] for q in gather_y(cross_q.reshape(shape))]
    second_rows = (first_rows.astype(F32) + core_rows_sum(partial, core)).astype(BF16)
    normed = rms_normed(second_rows)
    dec_ff = join(dec_ff_z, 2)
    normed = both_cores(normed, core)
    cross_weights = attn_pieces(cross_block_z, cross_near, cross_far)

    begin = jnp.clip(starts - row_begin, 0, rows)
    end = jnp.clip(ends - row_begin, 0, rows)
    questions = slot_question[0]
    questions = z_place(questions // 2) * 2 + questions % 2
    cross_q, normed, dec_ff = meet(cross_q, normed, dec_ff)

    def answer_part(index):
        sums = cross_block(
            begin, end, questions, x, cross_q[index], normed, cross_weights[index]
        )
        return by_column_x(sums, length)

    def of_x(values, index):
        return lax.dynamic_index_in_dim(values, index, 1, keepdims=False)

    if size_y == 2:
        other = answer_part(1)
        other_far = swap_y(of_x(other, 1 - x))
        other_near = of_x(other, x)
        own = answer_part(0)
        own, other_near = meet(own, other_near)
        other_near = swap_y(other_near)
        far = of_x(own, 1 - x).astype(F32) + other_far.astype(F32)
        far = swap_x(far.astype(BF16))
        summed = of_x(own, x).astype(F32) + other_near.astype(F32) + far.astype(F32)
    else:
        packed = [answer_part(index) for index in range(size_y)]
        summed = packed[0].astype(F32) if size_y == 1 else scatter_y_sum(jnp.stack(packed))
        far = swap_x(of_x(summed, 1 - x).astype(BF16))
        summed = of_x(summed, x) + far.astype(F32)
    if few_z():
        own = summed[0]
        for step in range(1, size_z):
            own = own + swap_z(summed[step].astype(BF16), step).astype(F32)
        summed = own
    else:
        exchanged = lax.all_to_all(
            summed.astype(BF16), "dp", 0, 0, axis_index_groups=z_groups(), tiled=True
        )
        summed = jnp.sum(exchanged.astype(F32), axis=0)
    width = summed.shape[1]
    heads = width // HEAD_DIM
    num = summed[: 2 * length].reshape(2, length, heads, HEAD_DIM)
    tot = summed[2 * length : 2 * length + 2 * heads * length // width]
    tot = tot.reshape(2, heads, length).transpose(0, 2, 1)
    cross_mix = (num / tot[..., None]).astype(BF16).reshape(2 * length, width)
    exchange = answer_start(dot_t(cross_mix, dec_attn[5]).astype(BF16), core, size_y)
    second_sum = answer_end(answer_turn(exchange))
    second_answer = (first_answer.astype(F32) + second_sum).astype(BF16)
    answer_normed = both_cores(rms_normed(second_answer), core)
    halves = [(dec_ff, 0, dec_ff.shape[1], half) for half in range(2)]
    partial = ff(answer_normed, [((0, halves), (2, halves), (4, halves))], [], True)
    per_column = size_z // mp_count
    columns = per_column * shard_width

    def columns_of(values, indices):
        values = values.reshape(values.shape[0], 2, size_z, shard_width)
        blocks = [
            lax.dynamic_index_in_dim(values, z_place(index * per_column + i), 2, keepdims=False)
            for index in indices
            for i in range(per_column)
        ]
        return jnp.stack(blocks, axis=2).reshape(values.shape[0], 2, len(indices), columns)

    other = swap_core(columns_of(partial, [2 * i + 1 - core for i in range(size_y)]))
    mine = columns_of(partial, [2 * i + core for i in range(size_y)])
    mine = mine.astype(F32) + other.astype(F32)
    other = swap_x(pick(mine, 1 - x, 2, 0).astype(BF16)).astype(F32)
    mine = pick(mine, x, 2, 0) + jnp.stack([other[:, 1], other[:, 0]], axis=1)
    summed = scatter_y_sum(mine.astype(BF16).transpose(2, 0, 1, 3))
    residual = pick(both_cores(second_answer, core), x, 2, 0)
    residual = columns_of(residual, [lax.axis_index("mp")])[:, :, 0]
    result = (residual.astype(F32) + summed).astype(BF16)
    result = result.reshape(length, 2, per_column, 1, shard_width)
    return in_order(x == 0, result[:, 0], result[:, 1], 2).reshape(length, 2 * columns)


def solution(mesh):
    in_specs = (
        P("dp", None),
        P("dp", None),
        P("dp", None),
        P("dp", None),
        P(None, "dp", "mp"),
        P(None, "dp", "mp"),
        P(None, "dp", "mp"),
        P(None, "dp", "mp"),
        P(None, "dp", "mp"),
    )
    out_specs = P("dp", "mp")

    return jax.shard_map(local, mesh=mesh, in_specs=in_specs, out_specs=out_specs, check_vma=False)
```

```python
import functools
import math

import jax
import jax.numpy as jnp
from jax import lax
from jax.experimental import pallas as pl
from jax.experimental.pallas import tpu as pltpu
from jax.sharding import PartitionSpec as P


HEAD_DIM = 64
EPSILON = 1e-06
LANES = 128
HALO = 256
F32 = jnp.float32
BF16 = jnp.bfloat16
EXP2_FACTOR = 3.0 / math.sqrt(HEAD_DIM) * math.log2(math.e)


def rms_normed(values):
    values = values.astype(F32)
    factor = lax.rsqrt(jnp.mean(values * values, axis=-1, keepdims=True) + EPSILON)
    return (values * factor).astype(BF16)


def dot(left, right):
    return jnp.dot(left, right, preferred_element_type=F32)


def dot_t(left, right):
    return lax.dot_general(left, right, (((1,), (1,)), ((), ())), preferred_element_type=F32)


def swap_x(value):
    count = lax.axis_size("dp")
    return lax.ppermute(value, "dp", [(i, i ^ 1) for i in range(count)])


def swap_core(value):
    count = lax.axis_size("mp")
    return lax.ppermute(value, "mp", [(i, i ^ 1) for i in range(count)])


def z_groups():
    count = lax.axis_size("dp")
    return [[i + x for i in range(0, count, 2)] for x in range(2)]


def y_groups():
    count = lax.axis_size("mp")
    return [[i + c for i in range(0, count, 2)] for c in range(2)]


def gather_z(value, axis):
    return lax.all_gather(value, "dp", axis_index_groups=z_groups(), axis=axis, tiled=True)


def few_z():
    return lax.axis_size("dp") // 2 <= 4


def swap_z(value, step):
    count = lax.axis_size("dp")
    return lax.ppermute(value, "dp", [(i, i ^ (2 * step)) for i in range(count)])


def z_place(index):
    return index ^ (lax.axis_index("dp") // 2) if few_z() else index


def pieces_z(value, axis):
    if not few_z():
        return [gather_z(value, axis)]
    return [value] + [swap_z(value, step) for step in range(1, lax.axis_size("dp") // 2)]


def meet(*values):
    return lax.optimization_barrier(values)


def swap_y(value):
    return lax.ppermute(value, "mp", [(i, i ^ 2) for i in range(4)])


def gather_y(value):
    size_y = lax.axis_size("mp") // 2
    if size_y == 1:
        return [value]
    if size_y == 2:
        return [value, swap_y(value)]
    pieces = lax.all_gather(value, "mp", axis_index_groups=y_groups(), axis=0)
    return [pieces[i] for i in range(size_y)]


def scatter_y_sum(value):
    size_y = lax.axis_size("mp") // 2
    y = lax.axis_index("mp") // 2
    if size_y == 2:
        other = swap_y(lax.dynamic_index_in_dim(value, 1 - y, 0, keepdims=False))
        own = lax.dynamic_index_in_dim(value, y, 0, keepdims=False)
        return own.astype(F32) + other.astype(F32)
    summed = lax.psum_scatter(
        value, "mp", scatter_dimension=0, axis_index_groups=y_groups(), tiled=True
    )
    return summed[0].astype(F32)


def join_kernel(*refs, axis):
    *pieces, out, sems = refs
    begin, copies = 0, []
    for index, piece in enumerate(pieces):
        size = piece.shape[axis]
        where = (slice(None),) * axis + (pl.ds(begin, size),)
        copies.append(pltpu.make_async_copy(piece, out.at[where], sems.at[index]))
        copies[-1].start()
        begin += size
    for copy in copies:
        copy.wait()


def join(pieces, axis):
    if len(pieces) == 1:
        return pieces[0]
    shape = list(pieces[0].shape)
    shape[axis] = sum(piece.shape[axis] for piece in pieces)
    if axis == len(shape) - 1 and pieces[0].shape[axis] % LANES:
        return jnp.concatenate(pieces, axis=axis)
    return pl.pallas_call(
        functools.partial(join_kernel, axis=axis),
        out_shape=jax.ShapeDtypeStruct(tuple(shape), pieces[0].dtype),
        in_specs=[pl.BlockSpec(memory_space=pl.ANY)] * len(pieces),
        out_specs=pl.BlockSpec(memory_space=pltpu.VMEM),
        scratch_shapes=[pltpu.SemaphoreType.DMA((len(pieces),))],
        cost_estimate=pl.CostEstimate(
            flops=0, bytes_accessed=4 * math.prod(shape), transcendentals=0
        ),
        name="join",
    )(*pieces)


def pick(value, index, count, axis):
    width = value.shape[axis] // count
    return lax.dynamic_slice_in_dim(value, index * width, width, axis)


def in_order(first, own, other, axis):
    return jnp.concatenate(
        [jnp.where(first, own, other), jnp.where(first, other, own)], axis=axis
    )


def spread_near(block):
    return (swap_x(block), swap_y(block)) if lax.axis_size("mp") == 4 else (swap_x(block),)


def spread_far(near, axis):
    if len(near) == 1:
        return ()
    side, over = near
    cut = far_cut(side.shape[axis])
    first = lax.slice_in_dim(over, 0, cut, axis=axis)
    second = lax.slice_in_dim(side, cut, side.shape[axis], axis=axis)
    return (swap_x(first), swap_y(second))


def far_cut(size):
    return -(-(size // 2) // LANES) * LANES


def attn_pieces(block, near, far):
    own = [block, near[0]]
    if len(near) == 1:
        return [own] + [[piece] for piece in gather_y(join(own, 1))[1:]]
    return [own, [near[1], *far]]


def ff_piece(block, near, far):
    own = [(block, 0, block.shape[1]), (near[0], 0, block.shape[1])]
    if len(near) == 1:
        rest = [gather_y(half)[1:] for half in (block, near[0])]
        return [own] + [
            [(mine, 0, mine.shape[1]), (theirs, 0, theirs.shape[1])]
            for mine, theirs in zip(*rest)
        ]
    return [own, [(near[1], 0, near[1].shape[1]), (far[0], 0, near[1].shape[1])]]


def ff_kernel(*refs, chunks, done, last):
    refs, out_ref = refs[:-1], refs[-1]
    if chunks:
        half = refs[0].shape[1] // 2
        mine, theirs = refs[0][:, :half], refs[0][:, half:]

    def weight(place):
        index, lead, begin, count = place
        return refs[index][lead, begin : begin + count, :]

    sums = [None, None]

    def add(hidden, places):
        for k in range(2):
            term = dot(hidden, weight(places[k]))
            sums[k] = term if sums[k] is None else sums[k] + term

    for index, places in done:
        add(refs[index][...], places)
    for gate, up, *down in chunks:
        gated = dot_t(mine, weight(gate[0])) + dot_t(theirs, weight(gate[1]))
        linear = dot_t(mine, weight(up[0])) + dot_t(theirs, weight(up[1]))
        hidden = (jax.nn.gelu(gated, approximate=True) * linear).astype(BF16)
        if last:
            add(hidden, down[0])
        else:
            out_ref[...] = hidden
    if last:
        half = sums[0].shape[1]
        out_ref[:, :half] = sums[0].astype(BF16)
        out_ref[:, half:] = sums[1].astype(BF16)


def ff(h, chunks, done, last):
    rows = h.shape[0]
    block = math.gcd(rows, 384)
    operands, specs, seen = [], [], {}
    if chunks:
        operands.append(h)
        specs.append(pl.BlockSpec((block, h.shape[1]), lambda i: (i, 0)))

    def place(lead, entry):
        array, begin, count, *more = entry
        lead += sum(more)
        if id(array) not in seen:
            seen[id(array)] = len(operands)
            operands.append(array)
            specs.append(pl.BlockSpec(array.shape, lambda i: (0, 0, 0)))
        return seen[id(array)], lead, begin, count

    def places(lead, entries):
        return tuple(place(lead, entry) for entry in entries)

    before = []
    for hidden, (lead, entries) in done:
        operands.append(hidden)
        specs.append(pl.BlockSpec((block, hidden.shape[1]), lambda i: (i, 0)))
        index = len(operands) - 1
        before.append((index, places(lead, entries)))
    plan = [tuple(places(lead, entries) for lead, entries in chunk) for chunk in chunks]
    width = h.shape[1] if last else chunks[0][0][1][0][2]
    flops = 2 * rows * h.shape[1] * sum(
        [(3 if last else 2) * c[0][1][0][2] for c in chunks] + [d[0].shape[1] for d in done]
    )
    return pl.pallas_call(
        functools.partial(ff_kernel, chunks=plan, done=before, last=last),
        out_shape=jax.ShapeDtypeStruct((rows, width), BF16),
        grid=(rows // block,),
        in_specs=specs,
        out_specs=pl.BlockSpec((block, width), lambda i: (i, 0)),
        compiler_params=pltpu.CompilerParams(vmem_limit_bytes=48 * 2**20),
        cost_estimate=pl.CostEstimate(
            flops=flops, bytes_accessed=2 * rows * (h.shape[1] + width), transcendentals=0
        ),
        name="ff",
    )(*operands)


def row_block(rows, most):
    return max(n for n in range(16, most + 1, 16) if rows % n == 0)


def resident(array):
    return pl.BlockSpec(array.shape, lambda i: (0,) * array.ndim)


def out_kernel(*refs, plan, index):
    *refs, out_ref = refs
    cuts = {0, out_ref.shape[1]}
    for _, parts in plan:
        begin = 0
        for part in parts:
            begin += refs[part].shape[1]
            cuts.add(begin)
    cuts = sorted(cuts)
    for low, high in zip(cuts, cuts[1:]):
        total = None
        for mix, parts in plan:
            begin = 0
            for part in parts:
                size = refs[part].shape[1]
                if begin <= low < begin + size:
                    term = dot_t(refs[mix][...], refs[part][index, low - begin : high - begin, :])
                    total = term if total is None else total + term
                begin += size
        out_ref[:, low:high] = total.astype(BF16)


def out_project(mixes, pieces, index):
    rows = mixes[0].shape[0]
    features = sum(part.shape[1] for part in pieces[0])
    block = math.gcd(rows, 384)
    operands, specs, plan = [], [], []
    for mix, parts in zip(mixes, pieces):
        plan.append((len(operands), range(len(operands) + 1, len(operands) + 1 + len(parts))))
        operands += [mix, *parts]
        specs.append(pl.BlockSpec((block, mix.shape[1]), lambda i: (i, 0)))
        specs += [resident(part) for part in parts]
    return pl.pallas_call(
        functools.partial(out_kernel, plan=plan, index=index),
        out_shape=jax.ShapeDtypeStruct((rows, features), BF16),
        grid=(rows // block,),
        in_specs=specs,
        out_specs=pl.BlockSpec((block, features), lambda i: (i, 0)),
        compiler_params=pltpu.CompilerParams(vmem_limit_bytes=32 * 2**20),
        cost_estimate=pl.CostEstimate(
            flops=2 * rows * features * sum(m.shape[1] for m in mixes),
            bytes_accessed=4 * rows * features,
            transcendentals=0,
        ),
        name="out_project",
    )(*operands)


def prepare_kernel(begin_ref, order_ref, x_ref, o_ref, raw_ref, *, width):
    rows, features = o_ref.shape
    chunk = 32

    def step(r, carry):
        begin = pl.multiple_of(r * chunk, chunk)
        blocks, total = [], 0.0
        for p in range(features // width):
            source = pl.multiple_of(order_ref[p] * width, width)
            block = x_ref[pl.ds(begin, chunk), pl.ds(source, width)]
            raw_ref[pl.ds(begin, chunk), p * width : (p + 1) * width] = block
            block = block.astype(F32)
            blocks.append(block)
            total = total + block * block
        mean = jnp.sum(total, axis=1, keepdims=True) / features
        factor = lax.rsqrt(mean + EPSILON)
        for p, block in enumerate(blocks):
            o_ref[pl.ds(begin, chunk), p * width : (p + 1) * width] = (block * factor).astype(BF16)
        return carry

    lax.fori_loop(0, rows // chunk, step, 0, unroll=2)


def prepare(values, begin, rows, order, width):
    features = values.shape[1]
    block = LANES
    spec = pl.BlockSpec((block, features), lambda i, first, order: (i, 0))
    return pl.pallas_call(
        functools.partial(prepare_kernel, width=width),
        out_shape=[jax.ShapeDtypeStruct((rows, features), BF16)] * 2,
        grid_spec=pltpu.PrefetchScalarGridSpec(
            num_scalar_prefetch=2,
            grid=(rows // block,),
            in_specs=[
                pl.BlockSpec((block, features), lambda i, first, order: (first[0] + i, 0))
            ],
            out_specs=[spec, spec],
        ),
        cost_estimate=pl.CostEstimate(
            flops=4 * rows * features, bytes_accessed=6 * rows * features, transcendentals=0
        ),
        name="prepare",
    )((begin // block).reshape(1), order, values)


def own_first(values, x, width, place):
    size_z = values.shape[1] // (2 * width)
    blocks = [
        lax.dynamic_slice_in_dim(values, (2 * place(z) + index) * width, width, 1)
        for index in (x, 1 - x)
        for z in range(size_z)
    ]
    return jnp.concatenate(blocks, axis=1)


def two_heads(q, k, v, allowed, low_half):
    zero, one = jnp.zeros_like(v), jnp.ones_like(v)
    keys = jnp.concatenate([jnp.where(low_half, k, zero), jnp.where(low_half, zero, k)], axis=0)
    vals = jnp.concatenate(
        [
            jnp.concatenate([jnp.where(low_half, v, zero), jnp.where(low_half, one, zero)], axis=1),
            jnp.concatenate([jnp.where(low_half, zero, v), jnp.where(low_half, zero, one)], axis=1),
        ],
        axis=0,
    )
    weights = jnp.exp2(dot_t(q, keys) * EXP2_FACTOR)
    count = k.shape[0]
    if count % LANES == 0:
        weights = jnp.where(jnp.concatenate([allowed, allowed], axis=1), weights, 0.0)
        return dot(weights.astype(BF16), vals)
    first = jnp.where(allowed, weights[:, :count], 0.0).astype(BF16)
    second = jnp.where(allowed, weights[:, count:], 0.0).astype(BF16)
    return dot(first, vals[:count]) + dot(second, vals[count:])


def active_range(begin, end):
    place = jnp.arange(begin.shape[0], dtype=jnp.int32)
    here = end > begin
    first = jnp.min(jnp.where(here, place, begin.shape[0]))
    return jnp.stack([first, jnp.max(jnp.where(here, place + 1, 0))])


def enc_attention_kernel(active_ref, query_ref, key_ref, first_ref, q_ref, k_ref, v_ref, o_ref, acc):
    window, width = q_ref.shape
    pairs = width // LANES
    acc[...] = jnp.zeros_like(acc)
    low_half = lax.broadcasted_iota(jnp.int32, (1, LANES), 1) < HEAD_DIM
    row = lax.broadcasted_iota(jnp.int32, (LANES, 1), 0)
    column = lax.broadcasted_iota(jnp.int32, (1, LANES), 1)
    count = query_ref.shape[1]

    def bounds(s):
        clipped = jnp.minimum(s, count - 1)
        begin = query_ref[0, clipped]
        end = jnp.where(s < active_ref[1], query_ref[1, clipped], begin)
        return begin, end, key_ref[0, clipped], key_ref[1, clipped]

    def tiles(begin, end):
        return (end - begin // 16 * 16 + LANES - 1) // LANES

    def offset_of(begin, index):
        low = begin // 16 * 16 + index * LANES
        return low, pl.multiple_of(jnp.minimum(low, window - LANES), 16)

    def sums_of(place, i, j):
        begin, end, key_begin, key_end = place
        low, offset = offset_of(begin, i)
        key_low, key_offset = offset_of(key_begin, j)
        rows = offset + row
        keys = key_offset + column
        least = jnp.where((rows >= jnp.maximum(begin, low)) & (rows < end), 0, window)
        keys = jnp.where((keys >= jnp.maximum(key_begin, key_low)) & (keys < key_end), keys, -1)
        allowed = keys >= least
        return offset, [
            two_heads(
                q_ref[pl.ds(offset, LANES), p * LANES : (p + 1) * LANES],
                k_ref[pl.ds(key_offset, LANES), p * LANES : (p + 1) * LANES],
                v_ref[pl.ds(key_offset, LANES), p * LANES : (p + 1) * LANES],
                allowed,
                low_half,
            )
            for p in range(pairs)
        ]

    def add(offset, sums):
        for p in range(pairs):
            acc[p, pl.ds(offset, LANES), :] += sums[p]

    def two_passages(n, carry):
        first = active_ref[0] + 2 * n
        places = [bounds(first), bounds(first + 1)]
        both = [sums_of(place, 0, 0) for place in places]
        for offset, sums in both:
            add(offset, sums)
        for place in places:
            key_tiles = tiles(place[2], place[3])

            def over_rows(i, outer, place=place, key_tiles=key_tiles):
                def over_keys(j, inner):
                    add(*sums_of(place, i, j))
                    return inner

                lax.fori_loop(jnp.where(i == 0, 1, 0), key_tiles, over_keys, 0)
                return outer

            lax.fori_loop(0, jnp.where(place[1] > place[0], tiles(place[0], place[1]), 0), over_rows, 0)
        return carry

    lax.fori_loop(0, (active_ref[1] - active_ref[0] + 1) // 2, two_passages, 0)
    block = math.gcd(o_ref.shape[0], LANES)

    def finish(n, carry):
        begin = pl.multiple_of(n * block, block)
        source = pl.multiple_of(first_ref[0] + n * block, block)
        for p in range(pairs):
            sums = acc[p, pl.ds(source, block), :]
            o_ref[pl.ds(begin, block), p * LANES : (p + 1) * LANES] = (
                sums[:, :LANES] / sums[:, LANES:]
            ).astype(BF16)
        return carry

    lax.fori_loop(0, o_ref.shape[0] // block, finish, 0)


def project_into(h_ref, weights, mats, outs):
    rows = h_ref.shape[0]
    begin = pl.multiple_of(pl.program_id(0) * rows, rows)
    for mat, out in zip(mats, outs):
        total, column = None, 0
        for weight in weights:
            size = weight.shape[1]
            term = dot(h_ref[:, column : column + size], weight[mat])
            total = term if total is None else total + term
            column += size
        out[pl.ds(begin, rows), :] = total.astype(BF16)


def enc_block_kernel(active_ref, query_ref, key_ref, first_ref, h_ref, *refs):
    *weights, o_ref, q, k, v, acc = refs
    project_into(h_ref, weights, (0, 1, 2), (q, k, v))

    @pl.when(pl.program_id(0) == pl.num_programs(0) - 1)
    def _():
        enc_attention_kernel(active_ref, query_ref, key_ref, first_ref, q, k, v, o_ref, acc)


def enc_block(query_range, key_range, first_row, rows, h, weights):
    window, width = h.shape[0], weights[0].shape[2]
    step = row_block(window, 400)
    smem = pl.BlockSpec(memory_space=pltpu.SMEM)
    return pl.pallas_call(
        enc_block_kernel,
        out_shape=jax.ShapeDtypeStruct((rows, width), BF16),
        grid=(window // step,),
        in_specs=[smem] * 4
        + [pl.BlockSpec((step, h.shape[1]), lambda i: (i, 0))]
        + [resident(weight) for weight in weights],
        out_specs=pl.BlockSpec((rows, width), lambda i: (0, 0)),
        scratch_shapes=[pltpu.VMEM((window, width), BF16)] * 3
        + [pltpu.VMEM((width // LANES, window, 2 * LANES), F32)],
        compiler_params=pltpu.CompilerParams(vmem_limit_bytes=32 * 2**20),
        cost_estimate=pl.CostEstimate(
            flops=window * width * (6 * h.shape[1] + 3072),
            bytes_accessed=2 * h.size,
            transcendentals=0,
        ),
        name="enc_block",
    )(active_range(*query_range), query_range, key_range, first_row.reshape(1), h, *weights)


def cross_block_kernel(
    active_ref, begin_ref, end_ref, question_ref, x_ref, *refs, key_rows, count
):
    queries, (h_ref, *weights, o_ref, k, v, acc) = refs[:count], refs[count:]
    project_into(h_ref, weights, (0, 1), (k, v))

    @pl.when(pl.program_id(0) == pl.num_programs(0) - 1)
    def _():
        cross_kernel(
            active_ref,
            begin_ref,
            end_ref,
            question_ref,
            x_ref,
            queries,
            k,
            v,
            o_ref,
            acc,
            key_rows=key_rows,
        )


def cross_kernel(
    active_ref, begin_ref, end_ref, question_ref, x_ref, queries, k_ref, v_ref, o_ref, acc, *, key_rows
):
    questions, length = queries[0].shape[:2]
    pairs = k_ref.shape[1] // LANES
    own_x = x_ref[0]

    def pair_of(question, p):
        if len(queries) == 1:
            return queries[0][question, :, p * LANES : (p + 1) * LANES]
        own, other = (ref[question] for ref in queries)
        return jnp.where(own_x == p, own, other)

    acc[...] = jnp.zeros_like(acc)
    low_half = lax.broadcasted_iota(jnp.int32, (1, LANES), 1) < HEAD_DIM
    rows = k_ref.shape[0]

    def bounds(s):
        begin = begin_ref[s]
        end = jnp.where(s < active_ref[1], end_ref[s], begin)
        return begin, end, question_ref[s], begin // 16 * 16

    def sums_of(place, j):
        begin, end, question, tile = place
        low = tile + j * key_rows
        offset = pl.multiple_of(jnp.minimum(low, rows - key_rows), 16)
        position = offset + lax.broadcasted_iota(jnp.int32, (1, key_rows), 1)
        allowed = (position >= jnp.maximum(begin, low)) & (position < end)
        return [
            two_heads(
                pair_of(question, p),
                k_ref[pl.ds(offset, key_rows), p * LANES : (p + 1) * LANES],
                v_ref[pl.ds(offset, key_rows), p * LANES : (p + 1) * LANES],
                allowed,
                low_half,
            )
            for p in range(pairs)
        ]

    def add(place, sums):
        for p in range(pairs):
            acc[place[2], p] += sums[p]

    def two_passages(i, carry):
        first = active_ref[0] + 2 * i
        places = [bounds(first), bounds(jnp.minimum(first + 1, begin_ref.shape[0] - 1))]
        places[1] = (
            places[1][0],
            jnp.where(first + 1 < active_ref[1], places[1][1], places[1][0]),
            *places[1][2:],
        )
        both = [sums_of(place, 0) for place in places]
        for place, sums in zip(places, both):
            add(place, sums)
        for place in places:

            def more(j, inner, place=place):
                add(place, sums_of(place, j))
                return inner

            lax.fori_loop(1, (place[1] - place[3] + key_rows - 1) // key_rows, more, 0)
        return carry

    lax.fori_loop(0, (active_ref[1] - active_ref[0] + 1) // 2, two_passages, 0)
    eye = lax.broadcasted_iota(jnp.int32, (length, LANES), 0) == lax.broadcasted_iota(
        jnp.int32, (length, LANES), 1
    )
    extra = o_ref.shape[2] - 2 * length
    place = lax.broadcasted_iota(jnp.int32, (extra, LANES), 0)

    def finish(z, carry):
        for p in range(pairs):
            totals = jnp.zeros((extra, LANES), F32)
            for x in range(2):
                sums = acc[2 * z + x, p]
                o_ref[z, p, x * length : (x + 1) * length, :] = sums[:, :LANES].astype(BF16)
                total = sums[:, LANES:]
                turned = pltpu.roll(total, HEAD_DIM, 1)
                for h in range(2):
                    own = jnp.where(low_half, total, turned) if h == 0 else jnp.where(low_half, turned, total)
                    row = jnp.sum(jnp.where(eye, own, 0.0), axis=0, keepdims=True)
                    totals = jnp.where(place == 2 * x + h, row, totals)
            o_ref[z, p, 2 * length :, :] = totals.astype(BF16)
        return carry

    lax.fori_loop(0, questions // 2, finish, 0)


def cross_block(begin, end, question, x, queries, h, weights):
    questions, length = queries[0].shape[:2]
    rows, width = h.shape[0], weights[0].shape[2]
    key_rows = min(rows, LANES)
    pairs = width // LANES
    step = row_block(rows, 400)
    active = active_range(begin, end)
    smem = pl.BlockSpec(memory_space=pltpu.SMEM)
    shape = (questions // 2, pairs, 2 * length + 16, LANES)
    return pl.pallas_call(
        functools.partial(cross_block_kernel, key_rows=key_rows, count=len(queries)),
        out_shape=jax.ShapeDtypeStruct(shape, BF16),
        grid=(rows // step,),
        in_specs=[smem] * 5
        + [resident(q) for q in queries]
        + [pl.BlockSpec((step, h.shape[1]), lambda i: (i, 0))]
        + [resident(weight) for weight in weights],
        out_specs=pl.BlockSpec(shape, lambda i: (0, 0, 0, 0)),
        scratch_shapes=[pltpu.VMEM((rows, width), BF16)] * 2
        + [pltpu.VMEM((questions, pairs, length, 2 * LANES), F32)],
        compiler_params=pltpu.CompilerParams(vmem_limit_bytes=40 * 2**20),
        cost_estimate=pl.CostEstimate(
            flops=rows * width * (4 * h.shape[1] + 2048), bytes_accessed=2 * h.size, transcendentals=0
        ),
        name="cross_block",
    )(active, begin, end, question, x.reshape(1), *queries, h, *weights)


def by_column_x(sums, length):
    size_z, pairs = sums.shape[:2]
    if pairs == 2:
        return sums
    num = sums[:, 0, : 2 * length].reshape(size_z, 2 * length, 2, HEAD_DIM).transpose(0, 2, 1, 3)
    tot = sums[:, 0, 2 * length : 2 * length + 4].reshape(size_z, 2, 2, length)
    tot = tot.transpose(0, 2, 1, 3).reshape(size_z, 2, -1, HEAD_DIM)
    return jnp.concatenate([num, tot], axis=2)


def self_kernel(x_ref, w_ref, o_ref, *, questions):
    rows, width = x_ref.shape[0], w_ref.shape[2]
    length = rows // questions
    q, k, v = (dot(x_ref[...], w_ref[i]).astype(BF16) for i in range(3))
    low_half = lax.broadcasted_iota(jnp.int32, (1, LANES), 1) < HEAD_DIM
    causal = lax.broadcasted_iota(jnp.int32, (length, length), 1) <= lax.broadcasted_iota(
        jnp.int32, (length, length), 0
    )
    for question in range(questions):
        own = slice(question * length, (question + 1) * length)
        total = None
        for p in range(width // LANES):
            columns = slice(p * LANES, (p + 1) * LANES)
            sums = two_heads(
                q[own, columns], k[own, columns], v[own, columns], causal, low_half
            )
            mixture = (sums[:, :LANES] / sums[:, LANES:]).astype(BF16)
            term = dot_t(mixture, w_ref[3, :, columns])
            total = term if total is None else total + term
        o_ref[own, :] = total.astype(BF16)


def self_block(x, weights, questions):
    if weights.shape[2] % LANES:
        q, k, v = (dot(x, weights[i]).astype(BF16) for i in range(3))
        return dot_t(self_attention(q, k, v, questions), weights[3]).astype(BF16)
    vmem = pl.BlockSpec(memory_space=pltpu.VMEM)
    return pl.pallas_call(
        functools.partial(self_kernel, questions=questions),
        out_shape=jax.ShapeDtypeStruct((x.shape[0], weights.shape[1]), BF16),
        in_specs=[vmem, vmem],
        out_specs=vmem,
        cost_estimate=pl.CostEstimate(
            flops=8 * x.size * weights.shape[2], bytes_accessed=2 * weights.size, transcendentals=0
        ),
        name="self_block",
    )(x, weights)


def self_attention(q, k, v, questions):
    rows, width = q.shape
    heads = width // HEAD_DIM
    length = rows // questions
    shape = (questions, length, heads, HEAD_DIM)
    q, k, v = q.reshape(shape), k.reshape(shape), v.reshape(shape)
    scores = jnp.einsum("oqhc,okhc->ohqk", q, k, preferred_element_type=F32)
    causal = jnp.arange(length)[None, :] <= jnp.arange(length)[:, None]
    weights = jnp.where(causal, jnp.exp(scores * (3.0 / math.sqrt(HEAD_DIM))), 0.0)
    totals = jnp.sum(weights, axis=3)
    mixture = jnp.einsum("ohqk,okhc->oqhc", weights.astype(BF16), v, preferred_element_type=F32)
    return (mixture / jnp.transpose(totals, (0, 2, 1))[..., None]).astype(BF16).reshape(rows, width)


def core_rows_sum(partial, core):
    other = swap_core(pick(partial, 1 - core, 2, 0).astype(BF16))
    return pick(partial, core, 2, 0).astype(F32) + other.astype(F32)


def flip(values):
    half = values.shape[1] // 2
    return jnp.concatenate([values[:, half:], values[:, :half]], axis=1)


def answer_start(partial, core, size_y):
    mine = core_rows_sum(partial, core).astype(BF16)
    if size_y != 2:
        return (mine, swap_x(mine))
    rows = mine.shape[0] // 2
    top, bottom = mine[:rows], mine[rows:]
    return top, bottom, swap_x(top), swap_y(bottom)


def answer_turn(values):
    if len(values) == 2:
        mine, other = values
        mine = mine.astype(F32) + flip(other).astype(F32)
        return (lax.psum(mine, "mp", axis_index_groups=y_groups()),)
    top, bottom, other_top, other_bottom = values
    top = (top.astype(F32) + flip(other_top).astype(F32)).astype(BF16)
    bottom = (bottom.astype(F32) + other_bottom.astype(F32)).astype(BF16)
    return top, bottom, swap_y(top), swap_x(bottom)


def answer_end(values):
    if len(values) == 1:
        return values[0]
    top, bottom, other_top, other_bottom = values
    top = top.astype(F32) + other_top.astype(F32)
    bottom = bottom.astype(F32) + flip(other_bottom).astype(F32)
    return jnp.concatenate([top, bottom], axis=0)


def both_cores(values, core):
    return in_order(core == 0, values, swap_core(values), 0)


def local(
    passage_embeds,
    passage_lengths,
    slot_question,
    answer_states,
    w_enc_attn,
    w_enc_ff,
    w_cross_kv,
    w_dec_attn,
    w_dec_ff,
):
    dp_count, mp_count = lax.axis_size("dp"), lax.axis_size("mp")
    size_z, size_y = dp_count // 2, mp_count // 2
    x = lax.axis_index("dp") % 2
    core = lax.axis_index("mp") % 2
    y = lax.axis_index("mp") // 2
    features = passage_embeds.shape[1]
    shard_width = features // dp_count

    length = answer_states.shape[0]
    enc_ff_t = w_enc_ff.transpose(0, 2, 1)
    dec_ff_t = w_dec_ff.transpose(0, 2, 1)
    attn_z = pieces_z(w_enc_attn, 1)
    dec_attn_pair = (pick(w_dec_attn, x, 2, 2), swap_x(pick(w_dec_attn, 1 - x, 2, 2)))
    dec_ff_pair = (pick(dec_ff_t, x, 2, 1), swap_x(pick(dec_ff_t, 1 - x, 2, 1)))
    other_answers = swap_x(answer_states)
    (
        attn_z,
        dec_attn_pair,
        dec_ff_pair,
        other_answers,
        enc_ff_t,
        passage_embeds,
        passage_lengths,
        answer_states,
    ) = meet(
        attn_z,
        dec_attn_pair,
        dec_ff_pair,
        other_answers,
        enc_ff_t,
        passage_embeds,
        passage_lengths,
        answer_states,
    )
    attn_block = join(attn_z, 1)
    attn_near = spread_near(attn_block)
    gate_z = pieces_z(enc_ff_t[0:1], 2)
    row_count = passage_embeds.shape[0]
    rows = row_count // size_y
    sides = min(size_y - 1, 2)
    window = min(row_count, rows + sides * HALO)
    row_begin = y * rows
    window_begin = jnp.clip(row_begin - HALO, 0, row_count - window)
    lengths = passage_lengths[0]
    ends = jnp.cumsum(lengths)
    starts = ends - lengths
    limits = jnp.stack([starts, ends]) - window_begin
    query_range = jnp.clip(limits, row_begin - window_begin, row_begin - window_begin + rows)
    key_range = jnp.clip(limits, 0, window)

    own_begin = row_begin - window_begin
    if shard_width % LANES == 0 and window % LANES == 0 and rows % LANES == 0:
        order = jnp.stack([2 * z_place(z) + i for i in (x, 1 - x) for z in range(size_z)])
        normed, embeds = prepare(passage_embeds, window_begin, window, order, shard_width)
    else:
        embeds = lax.dynamic_slice_in_dim(passage_embeds, window_begin, window, 0)
        embeds = own_first(embeds, x, shard_width, z_place)
        normed = rms_normed(embeds)
    answers = in_order(x == 0, answer_states, other_answers, 0)
    answers = own_first(answers, x, shard_width, z_place)
    answer_normed = rms_normed(answers)

    gate_z, rest_shard = meet(gate_z, enc_ff_t[1:3])
    rest_z = pieces_z(rest_shard, 2)

    attn_near, gate_z, normed = meet(attn_near, gate_z, normed)
    attn_far = spread_far(attn_near, 1)
    gate_block = join(gate_z, 2)
    gate_near = spread_near(gate_block)

    def attend(parts):
        return enc_block(query_range, key_range, own_begin, rows, normed, parts)

    if size_y == 2:
        mixes = [attend([attn_block, attn_near[0]])]
        attn_far, gate_near, rest_z, mixes, w_cross_kv, dec_attn_pair = meet(
            attn_far, gate_near, rest_z, mixes, w_cross_kv, dec_attn_pair
        )
    rest_block = join(rest_z, 2)
    rest_near = spread_near(rest_block)
    dec_attn_z = pieces_z(jnp.stack(dec_attn_pair, axis=1), 2)
    attn_weights = attn_pieces(attn_block, attn_near, attn_far)
    if size_y == 2:
        mixes.append(attend(attn_weights[1]))
    else:
        mixes = [attend(parts) for parts in attn_weights]
    partial = out_project(mixes, attn_weights, 3)
    own_embeds = lax.dynamic_slice_in_dim(embeds, own_begin + core * (rows // 2), rows // 2, 0)
    first_rows = (own_embeds.astype(F32) + core_rows_sum(partial, core)).astype(BF16)
    normed = both_cores(rms_normed(first_rows), core)

    rest_near, dec_attn_z, normed, w_cross_kv, dec_ff_pair = meet(
        rest_near, dec_attn_z, normed, w_cross_kv, dec_ff_pair
    )
    gate_far = (swap_x(gate_near[1]),) if size_y == 2 else ()
    rest_far = (swap_y(rest_near[0]),) if size_y == 2 else ()
    cross_z = pieces_z(w_cross_kv, 1)
    dec_ff_z = pieces_z(jnp.stack(dec_ff_pair, axis=1).reshape(-1, *dec_ff_pair[0].shape[1:]), 2)
    dec_attn = join(dec_attn_z, 2).reshape(w_dec_attn.shape[0], features, -1)
    self_partial = self_block(answer_normed, dec_attn, 2)
    exchange = answer_start(self_partial, core, size_y)
    gate_own = ff_piece(gate_block, gate_near, gate_near)[0]
    rest_own = ff_piece(rest_block, rest_near, rest_near)[0]
    hidden = [ff(normed, [((0, gate_own), (0, rest_own))], [], False)]

    gate_far, rest_far, hidden, exchange, cross_z = meet(
        gate_far, rest_far, hidden, exchange, cross_z
    )
    gate_ff = ff_piece(gate_block, gate_near, gate_far)
    exchange = answer_turn(exchange)
    cross_block_z = join(cross_z, 1)
    cross_near = spread_near(cross_block_z)
    rest_ff = ff_piece(rest_block, rest_near, rest_far)
    for gate, rest in zip(gate_ff[1:], rest_ff[1:]):
        hidden.append(ff(normed, [((0, gate), (0, rest))], [], False))

    hidden, exchange, cross_near = meet(hidden, exchange, cross_near)
    cross_far = spread_far(cross_near, 1)
    first_answer = (pick(answers, core, 2, 0).astype(F32) + answer_end(exchange)).astype(BF16)
    cross_q = dot(both_cores(rms_normed(first_answer), core), dec_attn[4]).astype(BF16)
    cross_q = pieces_z(cross_q, 0)
    partial = ff(normed, [], [(h, (1, rest)) for h, rest in zip(hidden, rest_ff)], True)

    cross_q, cross_far, partial = meet(cross_q, cross_far, partial)
    cross_q = join(cross_q, 0)
    shape = (dp_count, length, -1)
    if size_y == 2 and cross_q.shape[1] == LANES:
        side, over = swap_x(cross_q), swap_y(cross_q)
        half = cross_q.shape[0] // 2
        far = (swap_x(over[:half]), swap_y(side[half:]))
        far = jnp.concatenate(far, axis=0)
        cross_q = [[q.reshape(shape) for q in pair] for pair in ((cross_q, side), (over, far))]
    else:
        cross_q = in_order(x == 0, cross_q, swap_x(cross_q), 1)
        cross_q = [[q] for q in gather_y(cross_q.reshape(shape))]
    second_rows = (first_rows.astype(F32) + core_rows_sum(partial, core)).astype(BF16)
    normed = rms_normed(second_rows)
    dec_ff = join(dec_ff_z, 2)
    normed = both_cores(normed, core)
    cross_weights = attn_pieces(cross_block_z, cross_near, cross_far)

    begin = jnp.clip(starts - row_begin, 0, rows)
    end = jnp.clip(ends - row_begin, 0, rows)
    questions = slot_question[0]
    questions = z_place(questions // 2) * 2 + questions % 2
    cross_q, normed, dec_ff = meet(cross_q, normed, dec_ff)

    def answer_part(index):
        sums = cross_block(
            begin, end, questions, x, cross_q[index], normed, cross_weights[index]
        )
        return by_column_x(sums, length)

    def of_x(values, index):
        return lax.dynamic_index_in_dim(values, index, 1, keepdims=False)

    if size_y == 2:
        other = answer_part(1)
        other_far = swap_y(of_x(other, 1 - x))
        other_near = of_x(other, x)
        own = answer_part(0)
        own, other_near = meet(own, other_near)
        other_near = swap_y(other_near)
        far = of_x(own, 1 - x).astype(F32) + other_far.astype(F32)
        far = swap_x(far.astype(BF16))
        summed = of_x(own, x).astype(F32) + other_near.astype(F32) + far.astype(F32)
    else:
        packed = [answer_part(index) for index in range(size_y)]
        summed = packed[0].astype(F32) if size_y == 1 else scatter_y_sum(jnp.stack(packed))
        far = swap_x(of_x(summed, 1 - x).astype(BF16))
        summed = of_x(summed, x) + far.astype(F32)
    if few_z():
        own = summed[0]
        for step in range(1, size_z):
            own = own + swap_z(summed[step].astype(BF16), step).astype(F32)
        summed = own
    else:
        exchanged = lax.all_to_all(
            summed.astype(BF16), "dp", 0, 0, axis_index_groups=z_groups(), tiled=True
        )
        summed = jnp.sum(exchanged.astype(F32), axis=0)
    width = summed.shape[1]
    heads = width // HEAD_DIM
    num = summed[: 2 * length].reshape(2, length, heads, HEAD_DIM)
    tot = summed[2 * length : 2 * length + 2 * heads * length // width]
    tot = tot.reshape(2, heads, length).transpose(0, 2, 1)
    cross_mix = (num / tot[..., None]).astype(BF16).reshape(2 * length, width)
    exchange = answer_start(dot_t(cross_mix, dec_attn[5]).astype(BF16), core, size_y)
    second_sum = answer_end(answer_turn(exchange))
    second_answer = (first_answer.astype(F32) + second_sum).astype(BF16)
    answer_normed = both_cores(rms_normed(second_answer), core)
    halves = [(dec_ff, 0, dec_ff.shape[1], half) for half in range(2)]
    partial = ff(answer_normed, [((0, halves), (2, halves), (4, halves))], [], True)
    per_column = size_z // mp_count
    columns = per_column * shard_width

    def columns_of(values, indices):
        values = values.reshape(values.shape[0], 2, size_z, shard_width)
        blocks = [
            lax.dynamic_index_in_dim(values, z_place(index * per_column + i), 2, keepdims=False)
            for index in indices
            for i in range(per_column)
        ]
        return jnp.stack(blocks, axis=2).reshape(values.shape[0], 2, len(indices), columns)

    other = swap_core(columns_of(partial, [2 * i + 1 - core for i in range(size_y)]))
    mine = columns_of(partial, [2 * i + core for i in range(size_y)])
    mine = mine.astype(F32) + other.astype(F32)
    other = swap_x(pick(mine, 1 - x, 2, 0).astype(BF16)).astype(F32)
    mine = pick(mine, x, 2, 0) + jnp.stack([other[:, 1], other[:, 0]], axis=1)
    summed = scatter_y_sum(mine.astype(BF16).transpose(2, 0, 1, 3))
    residual = pick(both_cores(second_answer, core), x, 2, 0)
    residual = columns_of(residual, [lax.axis_index("mp")])[:, :, 0]
    result = (residual.astype(F32) + summed).astype(BF16)
    result = result.reshape(length, 2, per_column, 1, shard_width)
    return in_order(x == 0, result[:, 0], result[:, 1], 2).reshape(length, 2 * columns)


def solution(mesh):
    in_specs = (
        P("dp", None),
        P("dp", None),
        P("dp", None),
        P("dp", None),
        P(None, "dp", "mp"),
        P(None, "dp", "mp"),
        P(None, "dp", "mp"),
        P(None, "dp", "mp"),
        P(None, "dp", "mp"),
    )
    out_specs = P("dp", "mp")

    return jax.shard_map(local, mesh=mesh, in_specs=in_specs, out_specs=out_specs, check_vma=False)
```

```python
import functools
import math

import jax
import jax.numpy as jnp
from jax import lax
from jax.experimental import pallas as pl
from jax.experimental.pallas import tpu as pltpu
from jax.sharding import PartitionSpec as P


HEAD_DIM = 64
EPSILON = 1e-06
LANES = 128
HALO = 256
F32 = jnp.float32
BF16 = jnp.bfloat16
EXP2_FACTOR = 3.0 / math.sqrt(HEAD_DIM) * math.log2(math.e)


def rms_normed(values):
    values = values.astype(F32)
    factor = lax.rsqrt(jnp.mean(values * values, axis=-1, keepdims=True) + EPSILON)
    return (values * factor).astype(BF16)


def dot(left, right):
    return jnp.dot(left, right, preferred_element_type=F32)


def dot_t(left, right):
    return lax.dot_general(left, right, (((1,), (1,)), ((), ())), preferred_element_type=F32)


def swap_x(value):
    count = lax.axis_size("dp")
    return lax.ppermute(value, "dp", [(i, i ^ 1) for i in range(count)])


def swap_core(value):
    count = lax.axis_size("mp")
    return lax.ppermute(value, "mp", [(i, i ^ 1) for i in range(count)])


def z_groups():
    count = lax.axis_size("dp")
    return [[i + x for i in range(0, count, 2)] for x in range(2)]


def y_groups():
    count = lax.axis_size("mp")
    return [[i + c for i in range(0, count, 2)] for c in range(2)]


def gather_z(value, axis):
    return lax.all_gather(value, "dp", axis_index_groups=z_groups(), axis=axis, tiled=True)


def few_z():
    return lax.axis_size("dp") // 2 <= 4


def swap_z(value, step):
    count = lax.axis_size("dp")
    return lax.ppermute(value, "dp", [(i, i ^ (2 * step)) for i in range(count)])


def z_place(index):
    return index ^ (lax.axis_index("dp") // 2) if few_z() else index


def pieces_z(value, axis):
    if not few_z():
        return [gather_z(value, axis)]
    return [value] + [swap_z(value, step) for step in range(1, lax.axis_size("dp") // 2)]


def meet(*values):
    return lax.optimization_barrier(values)


def swap_y(value):
    return lax.ppermute(value, "mp", [(i, i ^ 2) for i in range(4)])


def gather_y(value):
    size_y = lax.axis_size("mp") // 2
    if size_y == 1:
        return [value]
    if size_y == 2:
        return [value, swap_y(value)]
    pieces = lax.all_gather(value, "mp", axis_index_groups=y_groups(), axis=0)
    return [pieces[i] for i in range(size_y)]


def scatter_y_sum(value):
    size_y = lax.axis_size("mp") // 2
    y = lax.axis_index("mp") // 2
    if size_y == 2:
        other = swap_y(lax.dynamic_index_in_dim(value, 1 - y, 0, keepdims=False))
        own = lax.dynamic_index_in_dim(value, y, 0, keepdims=False)
        return own.astype(F32) + other.astype(F32)
    summed = lax.psum_scatter(
        value, "mp", scatter_dimension=0, axis_index_groups=y_groups(), tiled=True
    )
    return summed[0].astype(F32)


def join_kernel(*refs, axis):
    *pieces, out, sems = refs
    begin, copies = 0, []
    for index, piece in enumerate(pieces):
        size = piece.shape[axis]
        where = (slice(None),) * axis + (pl.ds(begin, size),)
        copies.append(pltpu.make_async_copy(piece, out.at[where], sems.at[index]))
        copies[-1].start()
        begin += size
    for copy in copies:
        copy.wait()


def join(pieces, axis):
    if len(pieces) == 1:
        return pieces[0]
    shape = list(pieces[0].shape)
    shape[axis] = sum(piece.shape[axis] for piece in pieces)
    if axis == len(shape) - 1 and pieces[0].shape[axis] % LANES:
        return jnp.concatenate(pieces, axis=axis)
    return pl.pallas_call(
        functools.partial(join_kernel, axis=axis),
        out_shape=jax.ShapeDtypeStruct(tuple(shape), pieces[0].dtype),
        in_specs=[pl.BlockSpec(memory_space=pl.ANY)] * len(pieces),
        out_specs=pl.BlockSpec(memory_space=pltpu.VMEM),
        scratch_shapes=[pltpu.SemaphoreType.DMA((len(pieces),))],
        cost_estimate=pl.CostEstimate(
            flops=0, bytes_accessed=4 * math.prod(shape), transcendentals=0
        ),
        name="join",
    )(*pieces)


def pick(value, index, count, axis):
    width = value.shape[axis] // count
    return lax.dynamic_slice_in_dim(value, index * width, width, axis)


def in_order(first, own, other, axis):
    return jnp.concatenate(
        [jnp.where(first, own, other), jnp.where(first, other, own)], axis=axis
    )


def spread_near(block):
    return (swap_x(block), swap_y(block)) if lax.axis_size("mp") == 4 else (swap_x(block),)


def spread_far(near, axis):
    if len(near) == 1:
        return ()
    side, over = near
    cut = far_cut(side.shape[axis])
    first = lax.slice_in_dim(over, 0, cut, axis=axis)
    second = lax.slice_in_dim(side, cut, side.shape[axis], axis=axis)
    return (swap_x(first), swap_y(second))


def far_cut(size):
    return -(-(size // 2) // LANES) * LANES


def attn_pieces(block, near, far):
    own = [block, near[0]]
    if len(near) == 1:
        return [own] + [[piece] for piece in gather_y(join(own, 1))[1:]]
    return [own, [near[1], *far]]


def ff_piece(block, near, far):
    own = [(block, 0, block.shape[1]), (near[0], 0, block.shape[1])]
    if len(near) == 1:
        rest = [gather_y(half)[1:] for half in (block, near[0])]
        return [own] + [
            [(mine, 0, mine.shape[1]), (theirs, 0, theirs.shape[1])]
            for mine, theirs in zip(*rest)
        ]
    return [own, [(near[1], 0, near[1].shape[1]), (far[0], 0, near[1].shape[1])]]


def ff_kernel(*refs, chunks, done, last):
    refs, out_ref = refs[:-1], refs[-1]
    if chunks:
        half = refs[0].shape[1] // 2
        mine, theirs = refs[0][:, :half], refs[0][:, half:]

    def weight(place):
        index, lead, begin, count = place
        return refs[index][lead, begin : begin + count, :]

    sums = [None, None]

    def add(hidden, places):
        for k in range(2):
            term = dot(hidden, weight(places[k]))
            sums[k] = term if sums[k] is None else sums[k] + term

    for index, places in done:
        add(refs[index][...], places)
    for gate, up, *down in chunks:
        gated = dot_t(mine, weight(gate[0])) + dot_t(theirs, weight(gate[1]))
        linear = dot_t(mine, weight(up[0])) + dot_t(theirs, weight(up[1]))
        hidden = (jax.nn.gelu(gated, approximate=True) * linear).astype(BF16)
        if last:
            add(hidden, down[0])
        else:
            out_ref[...] = hidden
    if last:
        half = sums[0].shape[1]
        out_ref[:, :half] = sums[0].astype(BF16)
        out_ref[:, half:] = sums[1].astype(BF16)


def ff(h, chunks, done, last):
    rows = h.shape[0]
    block = math.gcd(rows, 384)
    operands, specs, seen = [], [], {}
    if chunks:
        operands.append(h)
        specs.append(pl.BlockSpec((block, h.shape[1]), lambda i: (i, 0)))

    def place(lead, entry):
        array, begin, count, *more = entry
        lead += sum(more)
        if id(array) not in seen:
            seen[id(array)] = len(operands)
            operands.append(array)
            specs.append(pl.BlockSpec(array.shape, lambda i: (0, 0, 0)))
        return seen[id(array)], lead, begin, count

    def places(lead, entries):
        return tuple(place(lead, entry) for entry in entries)

    before = []
    for hidden, (lead, entries) in done:
        operands.append(hidden)
        specs.append(pl.BlockSpec((block, hidden.shape[1]), lambda i: (i, 0)))
        index = len(operands) - 1
        before.append((index, places(lead, entries)))
    plan = [tuple(places(lead, entries) for lead, entries in chunk) for chunk in chunks]
    width = h.shape[1] if last else chunks[0][0][1][0][2]
    flops = 2 * rows * h.shape[1] * sum(
        [(3 if last else 2) * c[0][1][0][2] for c in chunks] + [d[0].shape[1] for d in done]
    )
    return pl.pallas_call(
        functools.partial(ff_kernel, chunks=plan, done=before, last=last),
        out_shape=jax.ShapeDtypeStruct((rows, width), BF16),
        grid=(rows // block,),
        in_specs=specs,
        out_specs=pl.BlockSpec((block, width), lambda i: (i, 0)),
        compiler_params=pltpu.CompilerParams(vmem_limit_bytes=48 * 2**20),
        cost_estimate=pl.CostEstimate(
            flops=flops, bytes_accessed=2 * rows * (h.shape[1] + width), transcendentals=0
        ),
        name="ff",
    )(*operands)


def row_block(rows, most):
    return max(n for n in range(16, most + 1, 16) if rows % n == 0)


def resident(array):
    return pl.BlockSpec(array.shape, lambda i: (0,) * array.ndim)


def out_kernel(*refs, plan, index):
    *refs, out_ref = refs
    cuts = {0, out_ref.shape[1]}
    for _, parts in plan:
        begin = 0
        for part in parts:
            begin += refs[part].shape[1]
            cuts.add(begin)
    cuts = sorted(cuts)
    for low, high in zip(cuts, cuts[1:]):
        total = None
        for mix, parts in plan:
            begin = 0
            for part in parts:
                size = refs[part].shape[1]
                if begin <= low < begin + size:
                    term = dot_t(refs[mix][...], refs[part][index, low - begin : high - begin, :])
                    total = term if total is None else total + term
                begin += size
        out_ref[:, low:high] = total.astype(BF16)


def out_project(mixes, pieces, index):
    rows = mixes[0].shape[0]
    features = sum(part.shape[1] for part in pieces[0])
    block = math.gcd(rows, 384)
    operands, specs, plan = [], [], []
    for mix, parts in zip(mixes, pieces):
        plan.append((len(operands), range(len(operands) + 1, len(operands) + 1 + len(parts))))
        operands += [mix, *parts]
        specs.append(pl.BlockSpec((block, mix.shape[1]), lambda i: (i, 0)))
        specs += [resident(part) for part in parts]
    return pl.pallas_call(
        functools.partial(out_kernel, plan=plan, index=index),
        out_shape=jax.ShapeDtypeStruct((rows, features), BF16),
        grid=(rows // block,),
        in_specs=specs,
        out_specs=pl.BlockSpec((block, features), lambda i: (i, 0)),
        compiler_params=pltpu.CompilerParams(vmem_limit_bytes=32 * 2**20),
        cost_estimate=pl.CostEstimate(
            flops=2 * rows * features * sum(m.shape[1] for m in mixes),
            bytes_accessed=4 * rows * features,
            transcendentals=0,
        ),
        name="out_project",
    )(*operands)


def prepare_kernel(begin_ref, order_ref, x_ref, o_ref, raw_ref, *, width):
    rows, features = o_ref.shape
    chunk = 32

    def step(r, carry):
        begin = pl.multiple_of(r * chunk, chunk)
        blocks, total = [], 0.0
        for p in range(features // width):
            source = pl.multiple_of(order_ref[p] * width, width)
            block = x_ref[pl.ds(begin, chunk), pl.ds(source, width)]
            raw_ref[pl.ds(begin, chunk), p * width : (p + 1) * width] = block
            block = block.astype(F32)
            blocks.append(block)
            total = total + block * block
        mean = jnp.sum(total, axis=1, keepdims=True) / features
        factor = lax.rsqrt(mean + EPSILON)
        for p, block in enumerate(blocks):
            o_ref[pl.ds(begin, chunk), p * width : (p + 1) * width] = (block * factor).astype(BF16)
        return carry

    lax.fori_loop(0, rows // chunk, step, 0, unroll=2)


def prepare(values, begin, rows, order, width):
    features = values.shape[1]
    block = LANES
    spec = pl.BlockSpec((block, features), lambda i, first, order: (i, 0))
    return pl.pallas_call(
        functools.partial(prepare_kernel, width=width),
        out_shape=[jax.ShapeDtypeStruct((rows, features), BF16)] * 2,
        grid_spec=pltpu.PrefetchScalarGridSpec(
            num_scalar_prefetch=2,
            grid=(rows // block,),
            in_specs=[
                pl.BlockSpec((block, features), lambda i, first, order: (first[0] + i, 0))
            ],
            out_specs=[spec, spec],
        ),
        cost_estimate=pl.CostEstimate(
            flops=4 * rows * features, bytes_accessed=6 * rows * features, transcendentals=0
        ),
        name="prepare",
    )((begin // block).reshape(1), order, values)


def own_first(values, x, width, place):
    size_z = values.shape[1] // (2 * width)
    blocks = [
        lax.dynamic_slice_in_dim(values, (2 * place(z) + index) * width, width, 1)
        for index in (x, 1 - x)
        for z in range(size_z)
    ]
    return jnp.concatenate(blocks, axis=1)


def two_heads(q, k, v, allowed, low_half):
    zero, one = jnp.zeros_like(v), jnp.ones_like(v)
    keys = jnp.concatenate([jnp.where(low_half, k, zero), jnp.where(low_half, zero, k)], axis=0)
    vals = jnp.concatenate(
        [
            jnp.concatenate([jnp.where(low_half, v, zero), jnp.where(low_half, one, zero)], axis=1),
            jnp.concatenate([jnp.where(low_half, zero, v), jnp.where(low_half, zero, one)], axis=1),
        ],
        axis=0,
    )
    weights = jnp.exp2(dot_t(q, keys) * EXP2_FACTOR)
    count = k.shape[0]
    if count % LANES == 0:
        weights = jnp.where(jnp.concatenate([allowed, allowed], axis=1), weights, 0.0)
        return dot(weights.astype(BF16), vals)
    first = jnp.where(allowed, weights[:, :count], 0.0).astype(BF16)
    second = jnp.where(allowed, weights[:, count:], 0.0).astype(BF16)
    return dot(first, vals[:count]) + dot(second, vals[count:])


def enc_attention_kernel(
    low_ref, high_ref, first_ref, seg_q_ref, seg_k_ref, q_ref, k_ref, v_ref, o_ref, acc, *, rows
):
    width = q_ref.shape[1]
    first_row = first_ref[0]
    key_rows = seg_k_ref.shape[2]
    last = seg_k_ref.shape[0] - 1
    low_half = lax.broadcasted_iota(jnp.int32, (1, LANES), 1) < HEAD_DIM

    def block(i, carry):
        begin = pl.multiple_of(i * rows, rows)
        query_begin = pl.multiple_of(first_row + i * rows, math.gcd(rows, LANES))
        low, high = low_ref[i], high_ref[i]
        acc[...] = jnp.zeros_like(acc)

        def step(j, inner):
            for p in range(width // LANES):
                columns = slice(p * LANES, (p + 1) * LANES)
                total = None
                for u in range(2):
                    index = low + 2 * j + u
                    clipped = jnp.minimum(index, last)
                    offset = pl.multiple_of(clipped * key_rows, key_rows)
                    seg_k = jnp.where(index < high, seg_k_ref[clipped], -1)
                    allowed = seg_q_ref[pl.ds(begin, rows), :key_rows] == seg_k
                    part = two_heads(
                        q_ref[pl.ds(query_begin, rows), columns],
                        k_ref[pl.ds(offset, key_rows), columns],
                        v_ref[pl.ds(offset, key_rows), columns],
                        allowed,
                        low_half,
                    )
                    total = part if total is None else total + part
                acc[p] += total
            return inner

        lax.fori_loop(0, (high - low + 1) // 2, step, 0)
        for p in range(width // LANES):
            sums = acc[p]
            o_ref[pl.ds(begin, rows), p * LANES : (p + 1) * LANES] = (
                sums[:, :LANES] / sums[:, LANES:]
            ).astype(BF16)
        return carry

    lax.fori_loop(0, low_ref.shape[0], block, 0)


def project_into(h_ref, weights, mats, outs):
    rows = h_ref.shape[0]
    begin = pl.multiple_of(pl.program_id(0) * rows, rows)
    for mat, out in zip(mats, outs):
        total, column = None, 0
        for weight in weights:
            size = weight.shape[1]
            term = dot(h_ref[:, column : column + size], weight[mat])
            total = term if total is None else total + term
            column += size
        out[pl.ds(begin, rows), :] = total.astype(BF16)


def enc_block_kernel(low_ref, high_ref, first_ref, seg_q_ref, seg_k_ref, h_ref, *refs, rows):
    *weights, o_ref, q, k, v, acc = refs
    project_into(h_ref, weights, (0, 1, 2), (q, k, v))

    @pl.when(pl.program_id(0) == pl.num_programs(0) - 1)
    def _():
        enc_attention_kernel(
            low_ref, high_ref, first_ref, seg_q_ref, seg_k_ref, q, k, v, o_ref, acc, rows=rows
        )


def enc_block(low, high, first_row, seg_q, seg_k, h, weights):
    rows, window, width = seg_q.shape[0], h.shape[0], weights[0].shape[2]
    query_rows = rows // low.shape[0]
    step = row_block(window, 400)
    smem = pl.BlockSpec(memory_space=pltpu.SMEM)
    return pl.pallas_call(
        functools.partial(enc_block_kernel, rows=query_rows),
        out_shape=jax.ShapeDtypeStruct((rows, width), BF16),
        grid=(window // step,),
        in_specs=[smem] * 3
        + [resident(seg_q), resident(seg_k)]
        + [pl.BlockSpec((step, h.shape[1]), lambda i: (i, 0))]
        + [resident(weight) for weight in weights],
        out_specs=pl.BlockSpec((rows, width), lambda i: (0, 0)),
        scratch_shapes=[pltpu.VMEM((window, width), BF16)] * 3
        + [pltpu.VMEM((width // LANES, query_rows, 2 * LANES), F32)],
        compiler_params=pltpu.CompilerParams(vmem_limit_bytes=32 * 2**20),
        cost_estimate=pl.CostEstimate(
            flops=window * width * (6 * h.shape[1] + 3072),
            bytes_accessed=2 * h.size,
            transcendentals=0,
        ),
        name="enc_block",
    )(low, high, first_row.reshape(1), seg_q, seg_k, h, *weights)


def cross_block_kernel(
    active_ref, begin_ref, end_ref, question_ref, x_ref, *refs, key_rows, count
):
    queries, (h_ref, *weights, o_ref, k, v, acc) = refs[:count], refs[count:]
    project_into(h_ref, weights, (0, 1), (k, v))

    @pl.when(pl.program_id(0) == pl.num_programs(0) - 1)
    def _():
        cross_kernel(
            active_ref,
            begin_ref,
            end_ref,
            question_ref,
            x_ref,
            queries,
            k,
            v,
            o_ref,
            acc,
            key_rows=key_rows,
        )


def cross_kernel(
    active_ref, begin_ref, end_ref, question_ref, x_ref, queries, k_ref, v_ref, o_ref, acc, *, key_rows
):
    questions, length = queries[0].shape[:2]
    pairs = k_ref.shape[1] // LANES
    own_x = x_ref[0]

    def pair_of(question, p):
        if len(queries) == 1:
            return queries[0][question, :, p * LANES : (p + 1) * LANES]
        own, other = (ref[question] for ref in queries)
        return jnp.where(own_x == p, own, other)

    acc[...] = jnp.zeros_like(acc)
    low_half = lax.broadcasted_iota(jnp.int32, (1, LANES), 1) < HEAD_DIM
    rows = k_ref.shape[0]

    def bounds(s):
        begin = begin_ref[s]
        end = jnp.where(s < active_ref[1], end_ref[s], begin)
        return begin, end, question_ref[s], begin // 16 * 16

    def sums_of(place, j):
        begin, end, question, tile = place
        low = tile + j * key_rows
        offset = pl.multiple_of(jnp.minimum(low, rows - key_rows), 16)
        position = offset + lax.broadcasted_iota(jnp.int32, (1, key_rows), 1)
        allowed = (position >= jnp.maximum(begin, low)) & (position < end)
        return [
            two_heads(
                pair_of(question, p),
                k_ref[pl.ds(offset, key_rows), p * LANES : (p + 1) * LANES],
                v_ref[pl.ds(offset, key_rows), p * LANES : (p + 1) * LANES],
                allowed,
                low_half,
            )
            for p in range(pairs)
        ]

    def add(place, sums):
        for p in range(pairs):
            acc[place[2], p] += sums[p]

    def two_passages(i, carry):
        first = active_ref[0] + 2 * i
        places = [bounds(first), bounds(jnp.minimum(first + 1, begin_ref.shape[0] - 1))]
        places[1] = (
            places[1][0],
            jnp.where(first + 1 < active_ref[1], places[1][1], places[1][0]),
            *places[1][2:],
        )
        both = [sums_of(place, 0) for place in places]
        for place, sums in zip(places, both):
            add(place, sums)
        for place in places:

            def more(j, inner, place=place):
                add(place, sums_of(place, j))
                return inner

            lax.fori_loop(1, (place[1] - place[3] + key_rows - 1) // key_rows, more, 0)
        return carry

    lax.fori_loop(0, (active_ref[1] - active_ref[0] + 1) // 2, two_passages, 0)
    eye = lax.broadcasted_iota(jnp.int32, (length, LANES), 0) == lax.broadcasted_iota(
        jnp.int32, (length, LANES), 1
    )
    extra = o_ref.shape[2] - 2 * length
    place = lax.broadcasted_iota(jnp.int32, (extra, LANES), 0)

    def finish(z, carry):
        for p in range(pairs):
            totals = jnp.zeros((extra, LANES), F32)
            for x in range(2):
                sums = acc[2 * z + x, p]
                o_ref[z, p, x * length : (x + 1) * length, :] = sums[:, :LANES].astype(BF16)
                total = sums[:, LANES:]
                turned = pltpu.roll(total, HEAD_DIM, 1)
                for h in range(2):
                    own = jnp.where(low_half, total, turned) if h == 0 else jnp.where(low_half, turned, total)
                    row = jnp.sum(jnp.where(eye, own, 0.0), axis=0, keepdims=True)
                    totals = jnp.where(place == 2 * x + h, row, totals)
            o_ref[z, p, 2 * length :, :] = totals.astype(BF16)
        return carry

    lax.fori_loop(0, questions // 2, finish, 0)


def cross_block(begin, end, question, x, queries, h, weights):
    questions, length = queries[0].shape[:2]
    rows, width = h.shape[0], weights[0].shape[2]
    key_rows = min(rows, LANES)
    pairs = width // LANES
    step = row_block(rows, 400)
    place = jnp.arange(begin.shape[0], dtype=jnp.int32)
    here = end > begin
    active = jnp.stack(
        [
            jnp.min(jnp.where(here, place, begin.shape[0])),
            jnp.max(jnp.where(here, place + 1, 0)),
        ]
    )
    smem = pl.BlockSpec(memory_space=pltpu.SMEM)
    shape = (questions // 2, pairs, 2 * length + 16, LANES)
    return pl.pallas_call(
        functools.partial(cross_block_kernel, key_rows=key_rows, count=len(queries)),
        out_shape=jax.ShapeDtypeStruct(shape, BF16),
        grid=(rows // step,),
        in_specs=[smem] * 5
        + [resident(q) for q in queries]
        + [pl.BlockSpec((step, h.shape[1]), lambda i: (i, 0))]
        + [resident(weight) for weight in weights],
        out_specs=pl.BlockSpec(shape, lambda i: (0, 0, 0, 0)),
        scratch_shapes=[pltpu.VMEM((rows, width), BF16)] * 2
        + [pltpu.VMEM((questions, pairs, length, 2 * LANES), F32)],
        compiler_params=pltpu.CompilerParams(vmem_limit_bytes=40 * 2**20),
        cost_estimate=pl.CostEstimate(
            flops=rows * width * (4 * h.shape[1] + 2048), bytes_accessed=2 * h.size, transcendentals=0
        ),
        name="cross_block",
    )(active, begin, end, question, x.reshape(1), *queries, h, *weights)


def by_column_x(sums, length):
    size_z, pairs = sums.shape[:2]
    if pairs == 2:
        return sums
    num = sums[:, 0, : 2 * length].reshape(size_z, 2 * length, 2, HEAD_DIM).transpose(0, 2, 1, 3)
    tot = sums[:, 0, 2 * length : 2 * length + 4].reshape(size_z, 2, 2, length)
    tot = tot.transpose(0, 2, 1, 3).reshape(size_z, 2, -1, HEAD_DIM)
    return jnp.concatenate([num, tot], axis=2)


def self_kernel(x_ref, w_ref, o_ref, *, questions):
    rows, width = x_ref.shape[0], w_ref.shape[2]
    length = rows // questions
    q, k, v = (dot(x_ref[...], w_ref[i]).astype(BF16) for i in range(3))
    low_half = lax.broadcasted_iota(jnp.int32, (1, LANES), 1) < HEAD_DIM
    causal = lax.broadcasted_iota(jnp.int32, (length, length), 1) <= lax.broadcasted_iota(
        jnp.int32, (length, length), 0
    )
    for question in range(questions):
        own = slice(question * length, (question + 1) * length)
        total = None
        for p in range(width // LANES):
            columns = slice(p * LANES, (p + 1) * LANES)
            sums = two_heads(
                q[own, columns], k[own, columns], v[own, columns], causal, low_half
            )
            mixture = (sums[:, :LANES] / sums[:, LANES:]).astype(BF16)
            term = dot_t(mixture, w_ref[3, :, columns])
            total = term if total is None else total + term
        o_ref[own, :] = total.astype(BF16)


def self_block(x, weights, questions):
    if weights.shape[2] % LANES:
        q, k, v = (dot(x, weights[i]).astype(BF16) for i in range(3))
        return dot_t(self_attention(q, k, v, questions), weights[3]).astype(BF16)
    vmem = pl.BlockSpec(memory_space=pltpu.VMEM)
    return pl.pallas_call(
        functools.partial(self_kernel, questions=questions),
        out_shape=jax.ShapeDtypeStruct((x.shape[0], weights.shape[1]), BF16),
        in_specs=[vmem, vmem],
        out_specs=vmem,
        cost_estimate=pl.CostEstimate(
            flops=8 * x.size * weights.shape[2], bytes_accessed=2 * weights.size, transcendentals=0
        ),
        name="self_block",
    )(x, weights)


def self_attention(q, k, v, questions):
    rows, width = q.shape
    heads = width // HEAD_DIM
    length = rows // questions
    shape = (questions, length, heads, HEAD_DIM)
    q, k, v = q.reshape(shape), k.reshape(shape), v.reshape(shape)
    scores = jnp.einsum("oqhc,okhc->ohqk", q, k, preferred_element_type=F32)
    causal = jnp.arange(length)[None, :] <= jnp.arange(length)[:, None]
    weights = jnp.where(causal, jnp.exp(scores * (3.0 / math.sqrt(HEAD_DIM))), 0.0)
    totals = jnp.sum(weights, axis=3)
    mixture = jnp.einsum("ohqk,okhc->oqhc", weights.astype(BF16), v, preferred_element_type=F32)
    return (mixture / jnp.transpose(totals, (0, 2, 1))[..., None]).astype(BF16).reshape(rows, width)


def core_rows_sum(partial, core):
    other = swap_core(pick(partial, 1 - core, 2, 0).astype(BF16))
    return pick(partial, core, 2, 0).astype(F32) + other.astype(F32)


def flip(values):
    half = values.shape[1] // 2
    return jnp.concatenate([values[:, half:], values[:, :half]], axis=1)


def answer_start(partial, core, size_y):
    mine = core_rows_sum(partial, core).astype(BF16)
    if size_y != 2:
        return (mine, swap_x(mine))
    rows = mine.shape[0] // 2
    top, bottom = mine[:rows], mine[rows:]
    return top, bottom, swap_x(top), swap_y(bottom)


def answer_turn(values):
    if len(values) == 2:
        mine, other = values
        mine = mine.astype(F32) + flip(other).astype(F32)
        return (lax.psum(mine, "mp", axis_index_groups=y_groups()),)
    top, bottom, other_top, other_bottom = values
    top = (top.astype(F32) + flip(other_top).astype(F32)).astype(BF16)
    bottom = (bottom.astype(F32) + other_bottom.astype(F32)).astype(BF16)
    return top, bottom, swap_y(top), swap_x(bottom)


def answer_end(values):
    if len(values) == 1:
        return values[0]
    top, bottom, other_top, other_bottom = values
    top = top.astype(F32) + other_top.astype(F32)
    bottom = bottom.astype(F32) + flip(other_bottom).astype(F32)
    return jnp.concatenate([top, bottom], axis=0)


def both_cores(values, core):
    return in_order(core == 0, values, swap_core(values), 0)


def local(
    passage_embeds,
    passage_lengths,
    slot_question,
    answer_states,
    w_enc_attn,
    w_enc_ff,
    w_cross_kv,
    w_dec_attn,
    w_dec_ff,
):
    dp_count, mp_count = lax.axis_size("dp"), lax.axis_size("mp")
    size_z, size_y = dp_count // 2, mp_count // 2
    x = lax.axis_index("dp") % 2
    core = lax.axis_index("mp") % 2
    y = lax.axis_index("mp") // 2
    features = passage_embeds.shape[1]
    shard_width = features // dp_count

    length = answer_states.shape[0]
    enc_ff_t = w_enc_ff.transpose(0, 2, 1)
    dec_ff_t = w_dec_ff.transpose(0, 2, 1)
    attn_z = pieces_z(w_enc_attn, 1)
    dec_attn_pair = (pick(w_dec_attn, x, 2, 2), swap_x(pick(w_dec_attn, 1 - x, 2, 2)))
    dec_ff_pair = (pick(dec_ff_t, x, 2, 1), swap_x(pick(dec_ff_t, 1 - x, 2, 1)))
    other_answers = swap_x(answer_states)
    (
        attn_z,
        dec_attn_pair,
        dec_ff_pair,
        other_answers,
        enc_ff_t,
        passage_embeds,
        passage_lengths,
        answer_states,
    ) = meet(
        attn_z,
        dec_attn_pair,
        dec_ff_pair,
        other_answers,
        enc_ff_t,
        passage_embeds,
        passage_lengths,
        answer_states,
    )
    attn_block = join(attn_z, 1)
    attn_near = spread_near(attn_block)
    gate_z = pieces_z(enc_ff_t[0:1], 2)
    row_count = passage_embeds.shape[0]
    rows = row_count // size_y
    sides = min(size_y - 1, 2)
    window = min(row_count, rows + sides * HALO)
    row_begin = y * rows
    window_begin = jnp.clip(row_begin - HALO, 0, row_count - window)
    lengths = passage_lengths[0]
    ends = jnp.cumsum(lengths)
    starts = ends - lengths
    positions = window_begin + jnp.arange(window, dtype=jnp.int32)
    segment = jnp.sum((positions[:, None] >= ends[None, :]).astype(jnp.int32), axis=1)
    query_block = math.gcd(rows, 3 * LANES)
    key_block = math.gcd(window, LANES)
    block_first = row_begin + jnp.arange(rows // query_block, dtype=jnp.int32) * query_block
    block_last = block_first + query_block - 1
    inside_first = jnp.max(
        jnp.where(starts[None, :] <= block_first[:, None], starts[None, :], 0), axis=1
    )
    inside_last = jnp.min(
        jnp.where(ends[None, :] > block_last[:, None], ends[None, :], row_count), axis=1
    )
    low = (inside_first - window_begin) // key_block
    high = (inside_last - window_begin + key_block - 1) // key_block
    seg_k = segment.reshape(window // key_block, 1, key_block)
    seg_q = jnp.broadcast_to(
        lax.dynamic_slice_in_dim(segment, row_begin - window_begin, rows, 0)[:, None],
        (rows, LANES),
    )

    own_begin = row_begin - window_begin
    if shard_width % LANES == 0 and window % LANES == 0 and rows % LANES == 0:
        order = jnp.stack([2 * z_place(z) + i for i in (x, 1 - x) for z in range(size_z)])
        normed, embeds = prepare(passage_embeds, window_begin, window, order, shard_width)
    else:
        embeds = lax.dynamic_slice_in_dim(passage_embeds, window_begin, window, 0)
        embeds = own_first(embeds, x, shard_width, z_place)
        normed = rms_normed(embeds)
    answers = in_order(x == 0, answer_states, other_answers, 0)
    answers = own_first(answers, x, shard_width, z_place)
    answer_normed = rms_normed(answers)

    gate_z, rest_shard = meet(gate_z, enc_ff_t[1:3])
    rest_z = pieces_z(rest_shard, 2)

    attn_near, gate_z, normed = meet(attn_near, gate_z, normed)
    attn_far = spread_far(attn_near, 1)
    gate_block = join(gate_z, 2)
    gate_near = spread_near(gate_block)

    def attend(parts):
        return enc_block(low, high, own_begin, seg_q, seg_k, normed, parts)

    dec_attn_own = jnp.stack(dec_attn_pair, axis=1)
    dec_ff_own = jnp.stack(dec_ff_pair, axis=1).reshape(-1, *dec_ff_pair[0].shape[1:])
    if size_y == 2:
        mixes = [attend([attn_block, attn_near[0]])]
        attn_far, gate_near, rest_z, mixes, w_cross_kv, dec_attn_own, dec_ff_own, answer_normed = meet(
            attn_far, gate_near, rest_z, mixes, w_cross_kv, dec_attn_own, dec_ff_own, answer_normed
        )
    rest_block = join(rest_z, 2)
    rest_near = spread_near(rest_block)
    dec_attn_z = pieces_z(dec_attn_own, 2)
    attn_weights = attn_pieces(attn_block, attn_near, attn_far)
    if size_y == 2:
        mixes.append(attend(attn_weights[1]))
    else:
        mixes = [attend(parts) for parts in attn_weights]
    partial = out_project(mixes, attn_weights, 3)
    own_embeds = lax.dynamic_slice_in_dim(embeds, own_begin + core * (rows // 2), rows // 2, 0)
    first_rows = (own_embeds.astype(F32) + core_rows_sum(partial, core)).astype(BF16)
    normed = both_cores(rms_normed(first_rows), core)

    rest_near, dec_attn_z, normed, w_cross_kv, dec_ff_own = meet(
        rest_near, dec_attn_z, normed, w_cross_kv, dec_ff_own
    )
    gate_far = (swap_x(gate_near[1]),) if size_y == 2 else ()
    rest_far = (swap_y(rest_near[0]),) if size_y == 2 else ()
    cross_z = pieces_z(w_cross_kv, 1)
    dec_ff_z = pieces_z(dec_ff_own, 2)
    dec_attn = join(dec_attn_z, 2).reshape(w_dec_attn.shape[0], features, -1)
    self_partial = self_block(answer_normed, dec_attn, 2)
    exchange = answer_start(self_partial, core, size_y)
    gate_own = ff_piece(gate_block, gate_near, gate_near)[0]
    rest_own = ff_piece(rest_block, rest_near, rest_near)[0]
    hidden = [ff(normed, [((0, gate_own), (0, rest_own))], [], False)]

    gate_far, rest_far, hidden, exchange, cross_z = meet(
        gate_far, rest_far, hidden, exchange, cross_z
    )
    gate_ff = ff_piece(gate_block, gate_near, gate_far)
    exchange = answer_turn(exchange)
    cross_block_z = join(cross_z, 1)
    cross_near = spread_near(cross_block_z)
    rest_ff = ff_piece(rest_block, rest_near, rest_far)
    for gate, rest in zip(gate_ff[1:], rest_ff[1:]):
        hidden.append(ff(normed, [((0, gate), (0, rest))], [], False))

    hidden, exchange, cross_near = meet(hidden, exchange, cross_near)
    cross_far = spread_far(cross_near, 1)
    first_answer = (pick(answers, core, 2, 0).astype(F32) + answer_end(exchange)).astype(BF16)
    cross_q = dot(both_cores(rms_normed(first_answer), core), dec_attn[4]).astype(BF16)
    cross_q = pieces_z(cross_q, 0)
    partial = ff(normed, [], [(h, (1, rest)) for h, rest in zip(hidden, rest_ff)], True)

    cross_q, cross_far, partial = meet(cross_q, cross_far, partial)
    cross_q = join(cross_q, 0)
    shape = (dp_count, length, -1)
    if size_y == 2 and cross_q.shape[1] == LANES:
        side, over = swap_x(cross_q), swap_y(cross_q)
        half = cross_q.shape[0] // 2
        far = (swap_x(over[:half]), swap_y(side[half:]))
        far = jnp.concatenate(far, axis=0)
        cross_q = [[q.reshape(shape) for q in pair] for pair in ((cross_q, side), (over, far))]
    else:
        cross_q = in_order(x == 0, cross_q, swap_x(cross_q), 1)
        cross_q = [[q] for q in gather_y(cross_q.reshape(shape))]
    second_rows = (first_rows.astype(F32) + core_rows_sum(partial, core)).astype(BF16)
    normed = rms_normed(second_rows)
    dec_ff = join(dec_ff_z, 2)
    normed = both_cores(normed, core)
    cross_weights = attn_pieces(cross_block_z, cross_near, cross_far)

    begin = jnp.clip(starts - row_begin, 0, rows)
    end = jnp.clip(ends - row_begin, 0, rows)
    questions = slot_question[0]
    questions = z_place(questions // 2) * 2 + questions % 2
    cross_q, normed, dec_ff = meet(cross_q, normed, dec_ff)

    def answer_part(index):
        sums = cross_block(
            begin, end, questions, x, cross_q[index], normed, cross_weights[index]
        )
        return by_column_x(sums, length)

    def of_x(values, index):
        return lax.dynamic_index_in_dim(values, index, 1, keepdims=False)

    if size_y == 2:
        other = answer_part(1)
        other_far = swap_y(of_x(other, 1 - x))
        other_near = of_x(other, x)
        own = answer_part(0)
        own, other_near = meet(own, other_near)
        other_near = swap_y(other_near)
        far = of_x(own, 1 - x).astype(F32) + other_far.astype(F32)
        far = swap_x(far.astype(BF16))
        summed = of_x(own, x).astype(F32) + other_near.astype(F32) + far.astype(F32)
    else:
        packed = [answer_part(index) for index in range(size_y)]
        summed = packed[0].astype(F32) if size_y == 1 else scatter_y_sum(jnp.stack(packed))
        far = swap_x(of_x(summed, 1 - x).astype(BF16))
        summed = of_x(summed, x) + far.astype(F32)
    if few_z():
        own = summed[0]
        for step in range(1, size_z):
            own = own + swap_z(summed[step].astype(BF16), step).astype(F32)
        summed = own
    else:
        exchanged = lax.all_to_all(
            summed.astype(BF16), "dp", 0, 0, axis_index_groups=z_groups(), tiled=True
        )
        summed = jnp.sum(exchanged.astype(F32), axis=0)
    width = summed.shape[1]
    heads = width // HEAD_DIM
    num = summed[: 2 * length].reshape(2, length, heads, HEAD_DIM)
    tot = summed[2 * length : 2 * length + 2 * heads * length // width]
    tot = tot.reshape(2, heads, length).transpose(0, 2, 1)
    cross_mix = (num / tot[..., None]).astype(BF16).reshape(2 * length, width)
    exchange = answer_start(dot_t(cross_mix, dec_attn[5]).astype(BF16), core, size_y)
    second_sum = answer_end(answer_turn(exchange))
    second_answer = (first_answer.astype(F32) + second_sum).astype(BF16)
    answer_normed = both_cores(rms_normed(second_answer), core)
    halves = [(dec_ff, 0, dec_ff.shape[1], half) for half in range(2)]
    partial = ff(answer_normed, [((0, halves), (2, halves), (4, halves))], [], True)
    per_column = size_z // mp_count
    columns = per_column * shard_width

    def columns_of(values, indices):
        values = values.reshape(values.shape[0], 2, size_z, shard_width)
        blocks = [
            lax.dynamic_index_in_dim(values, z_place(index * per_column + i), 2, keepdims=False)
            for index in indices
            for i in range(per_column)
        ]
        return jnp.stack(blocks, axis=2).reshape(values.shape[0], 2, len(indices), columns)

    other = swap_core(columns_of(partial, [2 * i + 1 - core for i in range(size_y)]))
    mine = columns_of(partial, [2 * i + core for i in range(size_y)])
    mine = mine.astype(F32) + other.astype(F32)
    other = swap_x(pick(mine, 1 - x, 2, 0).astype(BF16)).astype(F32)
    mine = pick(mine, x, 2, 0) + jnp.stack([other[:, 1], other[:, 0]], axis=1)
    summed = scatter_y_sum(mine.astype(BF16).transpose(2, 0, 1, 3))
    residual = pick(both_cores(second_answer, core), x, 2, 0)
    residual = columns_of(residual, [lax.axis_index("mp")])[:, :, 0]
    result = (residual.astype(F32) + summed).astype(BF16)
    result = result.reshape(length, 2, per_column, 1, shard_width)
    return in_order(x == 0, result[:, 0], result[:, 1], 2).reshape(length, 2 * columns)


def solution(mesh):
    in_specs = (
        P("dp", None),
        P("dp", None),
        P("dp", None),
        P("dp", None),
        P(None, "dp", "mp"),
        P(None, "dp", "mp"),
        P(None, "dp", "mp"),
        P(None, "dp", "mp"),
        P(None, "dp", "mp"),
    )
    out_specs = P("dp", "mp")

    return jax.shard_map(local, mesh=mesh, in_specs=in_specs, out_specs=out_specs, check_vma=False)
```
